128 devices in a mesh: ctx: 16 (over z, y), exp: 8 (over x, core).
Axes of the slice: x: 4, y: 4, z: 4, core: 2. Of those that a mesh axis runs over, the one named last changes fastest.
Arguments:
- queries: bfloat16 [16384, 16, 128], P('ctx', 'exp'), may hold values from -6 to 6
- key_vectors: bfloat16 [16384, 16, 128], P('ctx', 'exp'), may hold values from -6 to 6
- values: bfloat16 [16384, 32, 128], P('ctx', 'exp'), may hold values from -6 to 6
- out_gate: bfloat16 [16384, 32, 128], P('ctx', 'exp'), may hold values from -6 to 6
- write_strength: float32 [32, 16384], P('exp', 'ctx'), may hold values from 0.001 to 0.9
- decay_logarithm: float32 [32, 16384], P('exp', 'ctx'), may hold values from -0.75 to 0
- residual: bfloat16 [16384, 2048], P(('ctx', 'exp')), may hold values from -6 to 6
- out_weight: bfloat16 [4096, 2048], P('exp'), may hold values from -0.09375 to 0.09375
- head_gain: float32 [128], replicated, may hold values from 0.1 to 1.9
- post_gain: float32 [2048], replicated, may hold values from 0.1 to 1.9
- gate_proj: bfloat16 [256, 2048, 512], P(('ctx', 'exp')), may hold values from -0.125 to 0.125
- up_proj: bfloat16 [256, 2048, 512], P(('ctx', 'exp')), may hold values from -0.125 to 0.125
- down_proj: bfloat16 [256, 512, 2048], P(('ctx', 'exp')), may hold values from -0.25 to 0.25
- expert_ids: int32 [16384, 10], P(('ctx', 'exp')), may hold values from 0 to 255, all different within a row; in each aligned block of 128 rows (0 to 127, 128 to 255, ...) at most 10 rows name the same one
- route_gates: float32 [16384, 10], P(('ctx', 'exp')), may hold values from 0.02 to 0.3
Outputs:
- attended: bfloat16 [16384, 2048], P(('ctx', 'exp'))
- expert_mix: bfloat16 [16384, 2048], P(('ctx', 'exp'))
The draws below stay inside these ranges and needn't reach their ends.
Inputs may be any that keep to these rules, and one draw needn't show every extreme that they name: `expert_ids`: the 10 ids of a row differ. Among the rows of one device no id appears more than 10 times, and some id appears exactly 10 times.
All inputs are finite; a program needn't handle non-finite values.
Results may differ from the reference program's by a relative error of at most 0.025.
Values may be sent and summed in bfloat16 or wider, within the bound.
No kernel may reach another device: no remote copies, remote signals or barrier semaphores. Data moves between devices by JAX's collectives and lax.ppermute only.
A program may use at most 192 MiB of HBM per device.

```python
import math
import jax
import jax.numpy as jnp
import numpy as np
from jax import lax

D = 2048
HK = 16
VALUE_HEADS = 32
DK = 128
DV = 128
EI = 512
TOPK = 10
SPAN = 64
TOK_DEV = 128
EXPERTS = 256
SEQ_DEV = 1024
SEQUENCE_LENGTH = 16384
CAP = 10
N_CTX = 16
N_EXP = 8


def key_field(key):
    tap_count = 8
    lag_ratio = 0.6
    scale_sum = math.sqrt(sum((lag_ratio ** (2 * offset) for offset in range(tap_count))))
    noise_field = jax.random.truncated_normal(jax.random.fold_in(key, 101), -6.0, 6.0, (SEQUENCE_LENGTH + tap_count - 1, HK, DK), jnp.float32)
    blended = jnp.zeros((SEQUENCE_LENGTH, HK, DK), jnp.float32)
    for offset in range(tap_count):
        start_row = tap_count - 1 - offset
        blended = blended + lag_ratio ** offset / scale_sum * noise_field[start_row:start_row + SEQUENCE_LENGTH]
    return jnp.clip(blended, -6.0, 6.0).astype(jnp.bfloat16)


def decay_fields(key):
    slow_share = 0.5
    slow_head_share = jax.random.uniform(jax.random.fold_in(key, 201), (VALUE_HEADS, 1)) < slow_share
    block_number = SEQUENCE_LENGTH // SEQ_DEV
    quick_decay_rate = jnp.exp(jax.random.uniform(jax.random.fold_in(key, 202), (VALUE_HEADS, 1), minval=math.log(1.0 / 50.0), maxval=math.log(1.0 / 25.0)))
    gradual_decay_rate = jax.random.uniform(jax.random.fold_in(key, 203), (VALUE_HEADS, 1), minval=0.2, maxval=0.5) / SEQUENCE_LENGTH
    multiplier = jnp.exp(jax.random.uniform(jax.random.fold_in(key, 204), (VALUE_HEADS, block_number), minval=0.0, maxval=math.log(2.5)))
    multiplier = jnp.repeat(multiplier, SEQ_DEV, axis=1)
    random_wobble = jax.random.uniform(jax.random.fold_in(key, 205), (VALUE_HEADS, SEQUENCE_LENGTH), minval=0.5, maxval=1.5)
    spike_position = jax.random.randint(jax.random.fold_in(key, 206), (VALUE_HEADS, 2, 1), 0, SEQUENCE_LENGTH)
    token_position = lax.iota(jnp.int32, SEQUENCE_LENGTH)
    sudden_spike = jnp.sum(jnp.where(spike_position == token_position[None, None, :], 1.0, 0.0), axis=1)
    decay_logarithm = -jnp.where(slow_head_share, gradual_decay_rate, quick_decay_rate) * multiplier * random_wobble - 0.35 * jnp.where(slow_head_share, sudden_spike, 0.0)
    fast_beta = jax.random.uniform(jax.random.fold_in(key, 207), (VALUE_HEADS, SEQUENCE_LENGTH), minval=0.6, maxval=0.9)
    slow_beta = jnp.exp(jax.random.uniform(jax.random.fold_in(key, 208), (VALUE_HEADS, SEQUENCE_LENGTH), minval=math.log(0.001), maxval=math.log(0.01)))
    strength = jnp.where(slow_head_share, slow_beta, fast_beta)
    return (strength, decay_logarithm)


def draw_key_vectors(key, part):
    return key_field(key)


def draw_write_strength(key, part):
    return decay_fields(key)[0]


def draw_decay_logarithm(key, part):
    return decay_fields(key)[1]


def block_levels(own_key, dims, pieces, least, high):
    loudness, own = 1.0, jax.random.fold_in(own_key, 6)
    for dim, blocks in pieces:
        heights = jnp.exp(jax.random.uniform(jax.random.fold_in(own, dim), (blocks,), jnp.float32, least / len(pieces), high / len(pieces)))
        loudness = loudness * jnp.repeat(heights, dims[dim] // blocks).reshape([-1 if axis == dim else 1 for axis in range(len(dims))])
    return loudness


def deal_out(own_key, own, number, rows, number_of, top, most, skew):
    order = jax.random.permutation(own_key, number_of)
    crowded, ordinary = portions_of(number_of, rows * top, most, skew, True), portions_of(number_of, rows * top, most, skew, False)
    places = jnp.arange(number_of)

    def named(lengths, offset_by):
        used = int((lengths > 0).sum())
        fixed = max(1, used // 4)
        shifted = fixed + (places - fixed + offset_by * (used - fixed)) % max(1, number_of - fixed)
        return jnp.zeros((number_of,), jnp.int32).at[order[jnp.where(places < fixed, places, shifted)]].set(jnp.asarray(lengths, jnp.int32))

    lengths = jnp.where(number % 4 == 0, named(crowded, number // 4), named(ordinary, number - number // 4 - 1))
    mixed = jax.random.permutation(jax.random.fold_in(own, 3), number_of)
    source_of, taker = mixed[0:number_of // 2 * 2:2], mixed[1:number_of // 2 * 2:2]
    slack = jnp.minimum(lengths[source_of] - 1, most - lengths[taker]) // 2
    slack = jnp.where((source_of == order[0]) | (taker == order[0]) | (lengths[taker] == 0), 0, jnp.maximum(slack, 0))
    shifted = jax.random.randint(jax.random.fold_in(own, 4), (number_of // 2,), 0, 1 << 20) % (slack + 1)
    lengths = lengths.at[source_of].add(-shifted).at[taker].add(shifted)
    labels = jnp.searchsorted(jnp.cumsum(lengths), jnp.arange(rows * top), side="right").astype(jnp.int32)
    grid = labels.reshape(top, rows).T
    grid = grid[jax.random.permutation(jax.random.fold_in(own, 1), rows)]
    offset_by = jax.random.randint(jax.random.fold_in(own, 2), (rows, 1), 0, top)
    return jnp.take_along_axis(grid, (jnp.arange(top)[None, :] + offset_by) % top, axis=1)


def portions_of(amount, total, limit, lean, full):
    weights = [(1 << 20) // math.isqrt(rank ** lean) + 1 for rank in range(1, amount + 1)]
    largest = limit if full else min(limit, max(-(-total // amount), total * weights[0] // sum(weights)))
    least = 1 if total - largest >= amount - 1 else 0
    given, rest = [largest] + [least] * (amount - 1), total - largest - least * (amount - 1)
    while rest > 0:
        movable = [i for i in range(1, amount) if given[i] < largest] or [i for i in range(1, amount) if given[i] < limit]
        pool, remaining = sum([weights[i] for i in movable]), rest
        for i in movable:
            addition = min(limit - given[i], max(1, remaining * weights[i] // pool), rest)
            given[i] = given[i] + addition
            rest = rest - addition
    return np.array(given)


def gaussian(rng, dims, deviation, most, pieces=(), kind=jnp.bfloat16):
    entries = deviation * jax.random.normal(rng, dims, jnp.float32)
    if pieces:
        entries = entries * block_levels(rng, dims, pieces, -0.22, 0.18)
    return jnp.clip(entries, -most, most).astype(kind)


def setup_inputs(seed: int = 0) -> dict:
    keys = jax.random.split(jax.random.key(seed), 16)
    queries = gaussian(keys[0], (SEQUENCE_LENGTH, HK, DK), 1.0, 6.0, ((0, 16), (1, 8)))
    key_vectors = draw_key_vectors(jax.random.fold_in(keys[15], 71), 0)
    values = gaussian(keys[2], (SEQUENCE_LENGTH, VALUE_HEADS, DV), 1.0, 6.0, ((0, 16), (1, 8)))
    out_gate = gaussian(keys[3], (SEQUENCE_LENGTH, VALUE_HEADS, DV), 1.0, 6.0, ((0, 16), (1, 8)))
    write_strength = draw_write_strength(jax.random.fold_in(keys[15], 71), 0)
    decay_logarithm = draw_decay_logarithm(jax.random.fold_in(keys[15], 71), 0)
    residual = gaussian(keys[6], (SEQUENCE_LENGTH, D), 1.0, 6.0, ((0, 128),))
    out_weight = gaussian(keys[7], (VALUE_HEADS * DV, D), (VALUE_HEADS * DV) ** -0.5, 0.09375, ((0, 8),))
    head_gain = jnp.clip(1.0 + 0.18 * jax.random.normal(keys[8], (DV,), jnp.float32), 0.1, 1.9)
    post_gain = jnp.clip(1.0 + 0.18 * jax.random.normal(keys[9], (D,), jnp.float32), 0.1, 1.9)
    gate_proj = gaussian(keys[10], (EXPERTS, D, EI), D ** -0.5, 0.125, ((0, 128),))
    up_proj = gaussian(keys[11], (EXPERTS, D, EI), D ** -0.5, 0.125, ((0, 128),))
    down_proj = gaussian(keys[12], (EXPERTS, EI, D), EI ** -0.5, 0.25, ((0, 128),))
    expert_ids_keys = jax.random.split(jax.random.fold_in(keys[13], 1), SEQUENCE_LENGTH // TOK_DEV)
    expert_ids_turns = jax.random.permutation(jax.random.fold_in(keys[13], 3), SEQUENCE_LENGTH // TOK_DEV)
    expert_ids = jax.vmap(lambda own, number: deal_out(jax.random.fold_in(keys[13], 2), own, number, TOK_DEV, EXPERTS, TOPK, CAP, 1))(expert_ids_keys, expert_ids_turns).reshape((SEQUENCE_LENGTH, TOPK))
    route_gates = jnp.clip(0.02 + 0.28 * jax.random.uniform(keys[14], (SEQUENCE_LENGTH, TOPK), jnp.float32) ** block_levels(keys[14], (SEQUENCE_LENGTH, TOPK), ((0, 128),), -0.2, 0.2), 0.02, 0.3)
    return {"queries": queries, "key_vectors": key_vectors, "values": values, "out_gate": out_gate, "write_strength": write_strength, "decay_logarithm": decay_logarithm, "residual": residual, "out_weight": out_weight, "head_gain": head_gain, "post_gain": post_gain, "gate_proj": gate_proj, "up_proj": up_proj, "down_proj": down_proj, "expert_ids": expert_ids, "route_gates": route_gates}


highest = lax.Precision.HIGHEST

def unit_rows(tensor, multiplier):
    return tensor * multiplier / jnp.sqrt(lax.optimization_barrier(jnp.sum(tensor * tensor, axis=-1, keepdims=True)) + 1e-06)

def solve_span(key_rows, strength, cumulative):
    span_len = key_rows.shape[-2]
    gram = jnp.einsum('...id,...jd->...ij', key_rows, key_rows, precision=highest)
    strict = jnp.tril(jnp.ones((span_len, span_len), jnp.bool_), -1)
    lower = jnp.where(strict, strength[..., :, None] * gram * jnp.exp(jnp.where(strict, cumulative[..., :, None] - cumulative[..., None, :], 0.0)), 0.0)
    eye_span = jnp.eye(span_len, dtype=jnp.float32)
    power = -lower
    inverse = eye_span + power
    reach = 2
    while reach < span_len:
        power = jnp.einsum('...ij,...jk->...ik', power, power, precision=highest)
        inverse = jnp.einsum('...ij,...jk->...ik', inverse, eye_span + power, precision=highest)
        reach = reach * 2
    return inverse

def reference(queries, key_vectors, values, out_gate, write_strength, decay_logarithm, residual, out_weight, head_gain, post_gain, gate_proj, up_proj, down_proj, expert_ids, route_gates):
    block_total = SEQUENCE_LENGTH // SPAN
    head_group = VALUE_HEADS // HK
    causal = jnp.tril(jnp.ones((SPAN, SPAN), jnp.bool_))

    def block_step(state_now, member):
        query_part, key_part, value_part, gate_part, strength, decay_part = member
        query_rows = jnp.repeat(unit_rows(query_part.astype(jnp.float32), DK ** (-0.5)), head_group, axis=1).transpose(1, 0, 2)
        key_rows = jnp.repeat(unit_rows(key_part.astype(jnp.float32), 1.0), head_group, axis=1).transpose(1, 0, 2)
        value_rows = value_part.astype(jnp.float32).transpose(1, 0, 2)
        cumulative = jnp.cumsum(decay_part, axis=-1)
        inverse = solve_span(key_rows, strength, cumulative)
        weighted = jnp.einsum('hij,hjd->hid', inverse, (strength * jnp.exp(cumulative))[..., None] * key_rows, precision=highest)
        written = jnp.einsum('hij,hjd->hid', inverse, strength[..., None] * value_rows, precision=highest)
        fresh_rows = written - jnp.einsum('hid,hde->hie', weighted, state_now, precision=highest)
        spread_mat = jnp.where(causal, jnp.exp(jnp.where(causal, cumulative[:, :, None] - cumulative[:, None, :], 0.0)), 0.0)
        mixing = jnp.einsum('hid,hjd->hij', query_rows, key_rows, precision=highest) * spread_mat
        output = jnp.einsum('hid,hde->hie', query_rows * jnp.exp(cumulative)[..., None], state_now, precision=highest)
        output = output + jnp.einsum('hij,hje->hie', mixing, fresh_rows, precision=highest)
        closing = cumulative[:, -1:]
        tail_keys = key_rows * jnp.exp(closing - cumulative)[..., None]
        state_now = jnp.exp(closing)[..., None] * state_now + jnp.einsum('hjd,hje->hde', tail_keys, fresh_rows, precision=highest)
        output = output.transpose(1, 0, 2)
        root_mean = jnp.sqrt(lax.optimization_barrier(jnp.mean(output * output, axis=-1, keepdims=True)) + 1e-06)
        gated_rows = (output / root_mean * head_gain * jax.nn.silu(gate_part.astype(jnp.float32))).astype(jnp.bfloat16)
        return (state_now, gated_rows.reshape(SPAN, VALUE_HEADS * DV))
    scan_items = (queries.reshape(block_total, SPAN, HK, DK), key_vectors.reshape(block_total, SPAN, HK, DK), values.reshape(block_total, SPAN, VALUE_HEADS, DV), out_gate.reshape(block_total, SPAN, VALUE_HEADS, DV), write_strength.reshape(VALUE_HEADS, block_total, SPAN).transpose(1, 0, 2), decay_logarithm.reshape(VALUE_HEADS, block_total, SPAN).transpose(1, 0, 2))
    zero_state = jnp.zeros((VALUE_HEADS, DK, DV), jnp.float32)
    final_state, gated = lax.scan(block_step, zero_state, scan_items)
    gated = gated.reshape(SEQUENCE_LENGTH, VALUE_HEADS * DV)
    attn_out = jnp.dot(gated, out_weight, preferred_element_type=jnp.float32)
    attended = (residual.astype(jnp.float32) + attn_out).astype(jnp.bfloat16)
    settled = lax.optimization_barrier(attended).astype(jnp.float32)
    normed = (settled / jnp.sqrt(lax.optimization_barrier(jnp.mean(settled * settled, axis=-1, keepdims=True)) + 1e-06) * post_gain).astype(jnp.bfloat16)
    expert_cap = N_CTX * N_EXP * CAP
    expert_hits = jnp.zeros((SEQUENCE_LENGTH, EXPERTS), jnp.int32)
    for which_pick in range(TOPK):
        expert_hits = expert_hits + (expert_ids[:, which_pick, None] == jnp.arange(EXPERTS, dtype=jnp.int32)[None, :]).astype(jnp.int32)
    earlier_hits = jnp.cumsum(expert_hits, axis=0, dtype=jnp.int32) - expert_hits
    slot_rank = jnp.take_along_axis(earlier_hits, expert_ids, axis=1).astype(jnp.int32)
    slot_index = (expert_ids * expert_cap + slot_rank).reshape(-1)
    token_index = jnp.repeat(jnp.arange(SEQUENCE_LENGTH, dtype=jnp.int32), TOPK)
    owner_table = jnp.full((EXPERTS * expert_cap,), SEQUENCE_LENGTH, jnp.int32).at[slot_index].set(token_index).reshape(EXPERTS, expert_cap)
    gate_table = jnp.zeros((EXPERTS * expert_cap,), jnp.float32).at[slot_index].set(route_gates.reshape(-1)).reshape(EXPERTS, expert_cap)
    padded = jnp.concatenate([normed, jnp.zeros((1, D), jnp.bfloat16)], axis=0)

    def expert_step(running_sum, member):
        owner_rows, row_gates, gate_matrix, up_matrix, down_matrix = member
        gathered = padded[owner_rows]
        gate_part = jnp.dot(gathered, gate_matrix, preferred_element_type=jnp.float32)
        up_part = jnp.dot(gathered, up_matrix, preferred_element_type=jnp.float32)
        inner_act = (jax.nn.silu(gate_part) * up_part).astype(jnp.bfloat16)
        expert_rows = jnp.dot(inner_act, down_matrix, preferred_element_type=jnp.float32).astype(jnp.bfloat16)
        running_sum = running_sum.at[owner_rows].add(row_gates[:, None] * expert_rows.astype(jnp.float32))
        return (running_sum, None)
    mixture, unused_tail = lax.scan(expert_step, jnp.zeros((SEQUENCE_LENGTH + 1, D), jnp.float32), (owner_table, gate_table, gate_proj, up_proj, down_proj))
    return (attended, mixture[:SEQUENCE_LENGTH].astype(jnp.bfloat16))
```

```python
import functools

import jax
import jax.numpy as jnp
from jax import lax
from jax.experimental import pallas as pl
from jax.experimental.pallas import tpu as pltpu
from jax.sharding import PartitionSpec as P

CHUNK = 128
CAP = 10
F32 = jnp.float32
BF16 = jnp.bfloat16
VMEM = pltpu.VMEM
MIB = 1024 * 1024


def mxu(a, b, dims=((1,), (0,))):
    return lax.dot_general(a, b, (dims, ((), ())), preferred_element_type=F32)


def halves(a):
    high = a.astype(BF16)
    return high, (a - high.astype(F32)).astype(BF16)


def product(a, b):
    width = b[0].shape[1]
    left = jnp.concatenate([a[0], a[1]], axis=1)
    right = jnp.concatenate(
        [
            jnp.concatenate([b[0], b[1]], axis=1),
            jnp.concatenate([b[0], jnp.zeros_like(b[0])], axis=1),
        ],
        axis=0,
    )
    both = mxu(left, right)
    return both[:, :width] + both[:, width:]


def unit_lower_inverse(lower, row, col):
    eye = (row == col).astype(F32)
    diag = jnp.where(row // 16 == col // 16, lower, 0.0)
    inverse = eye - diag
    power = halves(-diag)
    for step in range(3):
        power = halves(product(power, power))
        inverse = inverse + product(halves(inverse), power)
    size = 16
    while size < lower.shape[0]:
        below = jnp.where((row // (2 * size) == col // (2 * size)) & (row // size != col // size), lower, 0.0)
        inv = halves(inverse)
        inverse = inverse - product(halves(product(inv, halves(below))), inv)
        size = size * 2
    return inverse


def delta_kernel(ds_ref, q_ref, k_ref, v_ref, r_ref, o_ref, msg_ref, state_ref):
    step = pl.program_id(0)
    heads = v_ref.shape[0]
    group = heads // q_ref.shape[0]
    c, d = q_ref.shape[1], q_ref.shape[2]
    row = lax.broadcasted_iota(jnp.int32, (c, c), 0)
    col = lax.broadcasted_iota(jnp.int32, (c, c), 1)
    causal = row >= col
    strict = row > col

    @pl.when(step == 0)
    def _():
        eye = (row == col).astype(F32)
        for h in range(heads):
            state_ref[h] = jnp.concatenate([eye, jnp.zeros_like(eye)], axis=1)

    ds = ds_ref[0]
    upto = (row <= col).astype(BF16)
    d0 = ds.astype(BF16)
    rest = ds - d0.astype(F32)
    d1 = rest.astype(BF16)
    d2 = (rest - d1.astype(F32)).astype(BF16)
    cum = mxu(d0, upto) + mxu(d1, upto) + mxu(d2, upto)
    half = jnp.where(lax.broadcasted_iota(jnp.int32, ds.shape, 0) < heads, cum, ds)
    columns = jnp.transpose(half, (1, 0))

    keyed = []
    for g in range(q_ref.shape[0]):
        q, k = q_ref[g], k_ref[g]
        qf, kf = q.astype(F32), k.astype(F32)
        q_col = (d ** -0.5) / jnp.sqrt(jnp.sum(qf * qf, axis=1, keepdims=True) + 1e-06)
        k_col = 1.0 / jnp.sqrt(jnp.sum(kf * kf, axis=1, keepdims=True) + 1e-06)
        gram = mxu(k, k, ((1,), (1,)))
        k_row = 1.0 / jnp.sqrt(jnp.sum(jnp.where(row == col, gram, 0.0), axis=0, keepdims=True) + 1e-06)
        gram = gram * (k_col * k_row)
        cross = mxu(q, k, ((1,), (1,))) * (q_col * k_row)
        keyed.append((qf, k, kf, q_col, k_col, k_row, gram, cross, jnp.transpose(kf, (1, 0)).astype(BF16)))

    for h in range(heads):
        qf, k, kf, q_col, k_col, k_row, gram, cross, k_t = keyed[h // group]
        cum_col, beta_col = columns[:, h : h + 1], columns[:, heads + h : heads + h + 1]
        cum_row, beta_row = half[h : h + 1, :], half[heads + h : heads + h + 1, :]
        closing = cum_row[:, c - 1 : c]
        spread = jnp.where(causal, jnp.exp(jnp.where(causal, cum_col - cum_row, 0.0)), 0.0)
        lower = jnp.where(strict, beta_col * gram * spread, 0.0)
        mixing = cross * spread
        inverse = unit_lower_inverse(lower, row, col)
        t_k = halves(inverse * (beta_row * jnp.exp(cum_row) * k_row))
        t_v = halves(inverse * beta_row)
        v = v_ref[h]
        weighted = mxu(jnp.concatenate(t_k, axis=1), jnp.concatenate([k, k], axis=0))
        written = mxu(jnp.concatenate(t_v, axis=1), jnp.concatenate([v, v], axis=0))
        state = state_ref[h]
        state_b = state.astype(BF16)
        fresh = jnp.concatenate([jnp.zeros_like(written), written], axis=1) - mxu(weighted.astype(BF16), state_b)
        reads = jnp.concatenate([qf * (q_col * jnp.exp(cum_col)), mixing], axis=1).astype(BF16)
        out = mxu(reads, jnp.concatenate([state_b, fresh.astype(BF16)], axis=0))
        r_ref[h] = out[:, :d].astype(BF16)
        o_ref[h] = out[:, d:]
        tail = (fresh * (k_col * jnp.exp(closing - cum_col))).astype(BF16)
        state_ref[h] = jnp.exp(closing) * state + mxu(k_t, tail)

    @pl.when(step == pl.num_programs(0) - 1)
    def _():
        parts = msg_ref.shape[1]
        wide = d // parts
        for h in range(heads):
            state = state_ref[h]
            moved = state[:, :d].astype(msg_ref.dtype)
            added = jnp.transpose(state[:, d:], (1, 0)).astype(msg_ref.dtype)
            for p in range(parts):
                msg_ref[h, p, :d, :] = moved
                msg_ref[h, p, d:, :] = added[p * wide : (p + 1) * wide]


def local_delta(ds, q, k, v, parts):
    heads, seq, dv = v.shape
    kh, _, dk = q.shape
    wide = dv // parts
    return pl.pallas_call(
        delta_kernel,
        grid=(seq // CHUNK,),
        in_specs=[
            pl.BlockSpec((1, 2 * heads, CHUNK), lambda i: (i, 0, 0)),
            pl.BlockSpec((kh, CHUNK, dk), lambda i: (0, i, 0)),
            pl.BlockSpec((kh, CHUNK, dk), lambda i: (0, i, 0)),
            pl.BlockSpec((heads, CHUNK, dv), lambda i: (0, i, 0)),
        ],
        out_specs=[
            pl.BlockSpec((heads, CHUNK, dk), lambda i: (0, i, 0)),
            pl.BlockSpec((heads, CHUNK, dv), lambda i: (0, i, 0)),
            pl.BlockSpec((heads, parts, dk + wide, dk), lambda i: (0, 0, 0, 0)),
        ],
        out_shape=[
            jax.ShapeDtypeStruct((heads, seq, dk), BF16),
            jax.ShapeDtypeStruct((heads, seq, dv), F32),
            jax.ShapeDtypeStruct((heads, parts, dk + wide, dk), BF16),
        ],
        scratch_shapes=[VMEM((heads, dk, dk + dv), F32)],
        compiler_params=pltpu.CompilerParams(
            dimension_semantics=("arbitrary",), vmem_limit_bytes=40 * MIB
        ),
        name="delta_local",
    )(ds, q, k, v)


def prefix_kernel(msg_ref, out_ref):
    count, tall, dk = msg_ref.shape
    wide = tall - dk
    state = jnp.zeros((wide, dk), F32)
    for i in range(count):
        out_ref[i] = state.astype(out_ref.dtype)
        if i < count - 1:
            both = jnp.concatenate(halves(state), axis=0)
            moved = mxu(both, msg_ref[i, :dk, :], ((1,), (1,)))
            state = moved[:wide] + moved[wide:] + msg_ref[i, dk:, :].astype(F32)


def prefix_states(msg, wide):
    count, tall, dk = msg.shape
    return pl.pallas_call(
        prefix_kernel,
        out_shape=jax.ShapeDtypeStruct((count, wide, dk), BF16),
        compiler_params=pltpu.CompilerParams(vmem_limit_bytes=16 * MIB),
        name="prefix_states",
    )(msg)


def gate_kernel(r_ref, o_ref, s_ref, g_ref, gain_ref, w_ref, out_ref):
    parts = []
    for h in range(r_ref.shape[0]):
        core = o_ref[h] + mxu(r_ref[h], s_ref[h], ((1,), (1,)))
        root = jnp.sqrt(jnp.mean(core * core, axis=1, keepdims=True) + 1e-06)
        gate = g_ref[h].astype(F32)
        silu = gate / (1.0 + jnp.exp(-gate))
        parts.append((core / root * gain_ref[...] * silu).astype(BF16))
    out_ref[...] = mxu(jnp.concatenate(parts, axis=1), w_ref[...]).astype(BF16)


def gate_project(r, o, states, gate, gain, weight):
    heads, seq, d = r.shape
    rows = 256
    width = weight.shape[1]
    by_rows = pl.BlockSpec((heads, rows, d), lambda i: (0, i, 0))
    return pl.pallas_call(
        gate_kernel,
        grid=(seq // rows,),
        in_specs=[
            by_rows,
            by_rows,
            pl.BlockSpec((heads, d, d), lambda i: (0, 0, 0)),
            by_rows,
            pl.BlockSpec((1, d), lambda i: (0, 0)),
            pl.BlockSpec(weight.shape, lambda i: (0, 0)),
        ],
        out_specs=pl.BlockSpec((rows, width), lambda i: (i, 0)),
        out_shape=jax.ShapeDtypeStruct((seq, width), BF16),
        compiler_params=pltpu.CompilerParams(
            dimension_semantics=("arbitrary",), vmem_limit_bytes=40 * MIB
        ),
        name="gate_project",
    )(r, o, states, gate, gain, weight)


def slot_kernel(experts, ids_ref, out_ref):
    top, toks = ids_ref.shape
    expert = lax.broadcasted_iota(jnp.int32, (experts, toks), 0)
    hits = jnp.zeros((experts, toks), F32)
    for k in range(top):
        hits = hits + (expert == ids_ref[k : k + 1, :]).astype(F32)
    before = (
        lax.broadcasted_iota(jnp.int32, (toks, toks), 0) < lax.broadcasted_iota(jnp.int32, (toks, toks), 1)
    ).astype(BF16)
    earlier = mxu(hits.astype(BF16), before)
    for k in range(top):
        ids = ids_ref[k : k + 1, :]
        rank = jnp.sum(jnp.where(expert == ids, earlier, 0.0), axis=0, keepdims=True)
        out_ref[k : k + 1, :] = ids * CAP + rank.astype(jnp.int32)


def slots_of(ids, experts):
    return pl.pallas_call(
        functools.partial(slot_kernel, experts),
        out_shape=jax.ShapeDtypeStruct(ids.shape, jnp.int32),
        compiler_params=pltpu.CompilerParams(vmem_limit_bytes=16 * MIB),
        name="slots",
    )(ids)


def dispatch_kernel(part_ref, res_ref, gain_ref, slot_ref, att_ref, send_ref, flat_ref):
    toks, width = part_ref.shape
    pieces = width // 128
    attended = (res_ref[...].astype(F32) + part_ref[...].astype(F32)).astype(BF16)
    att_ref[...] = attended
    settled = attended.astype(F32)
    root = jnp.sqrt(jnp.mean(settled * settled, axis=1, keepdims=True) + 1e-06)
    normed = settled / root * gain_ref[...]
    for j in range(pieces):
        flat_ref[pl.ds(j, toks, stride=pieces), :] = normed[:, j * 128 : (j + 1) * 128]

    @pl.loop(0, toks)
    def _(t):
        tile = flat_ref[pl.ds(pl.multiple_of(t * pieces, pieces), pieces), :].astype(BF16)
        for k in range(slot_ref.shape[0]):
            send_ref[slot_ref[k, t]] = tile


def dispatch(part, residual, gain, slots, count):
    toks, width = part.shape
    pieces = width // 128
    whole = pl.BlockSpec(memory_space=VMEM)
    return pl.pallas_call(
        dispatch_kernel,
        in_specs=[whole, whole, whole, pl.BlockSpec(memory_space=pltpu.SMEM)],
        out_specs=[whole, whole],
        out_shape=[
            jax.ShapeDtypeStruct((toks, width), BF16),
            jax.ShapeDtypeStruct((count, pieces, 128), BF16),
        ],
        scratch_shapes=[VMEM((toks * pieces, 128), F32)],
        compiler_params=pltpu.CompilerParams(vmem_limit_bytes=40 * MIB),
        name="dispatch",
    )(part, residual, gain, slots)


def expert_kernel(x_ref, wg_ref, wu_ref, wd_ref, out_ref, flat_ref):
    sources, _, tall, lanes = x_ref.shape
    rows = flat_ref.shape[0] // 16
    pieces = 16
    flat_ref[...] = x_ref[...].reshape(sources * tall, lanes).astype(F32)
    x = jnp.concatenate(
        [flat_ref[pl.ds(j, rows, stride=pieces), :].astype(BF16) for j in range(pieces)], axis=1
    )
    gate = mxu(x, wg_ref[0])
    up = mxu(x, wu_ref[0])
    inner = (gate / (1.0 + jnp.exp(-gate)) * up).astype(BF16)
    y = mxu(inner, wd_ref[0])
    for j in range(pieces):
        flat_ref[pl.ds(j, rows, stride=pieces), :] = y[:, j * 128 : (j + 1) * 128]
    out_ref[...] = flat_ref[...].astype(BF16).reshape(sources, 1, tall, lanes)


def run_experts(x, gate_proj, up_proj, down_proj):
    count, local, tall, lanes = x.shape
    sources = 32
    rows = sources * tall // 16
    tokens = pl.BlockSpec((sources, 1, tall, lanes), lambda e, i: (i, e, 0, 0))
    return pl.pallas_call(
        expert_kernel,
        grid=(local, count // sources),
        in_specs=[
            tokens,
            pl.BlockSpec((1,) + gate_proj.shape[1:], lambda e, i: (e, 0, 0)),
            pl.BlockSpec((1,) + up_proj.shape[1:], lambda e, i: (e, 0, 0)),
            pl.BlockSpec((1,) + down_proj.shape[1:], lambda e, i: (e, 0, 0)),
        ],
        out_specs=tokens,
        out_shape=jax.ShapeDtypeStruct(x.shape, BF16),
        scratch_shapes=[VMEM((sources * tall, lanes), F32)],
        compiler_params=pltpu.CompilerParams(
            dimension_semantics=("arbitrary", "arbitrary"), vmem_limit_bytes=48 * MIB
        ),
        name="experts",
    )(x, gate_proj, up_proj, down_proj)


def combine_kernel(back_ref, slot_ref, gate_ref, out_ref, flat_ref):
    toks, width = out_ref.shape
    pieces = width // 128

    @pl.loop(0, toks)
    def _(t):
        total = jnp.zeros((pieces, 128), F32)
        for k in range(slot_ref.shape[0]):
            total = total + gate_ref[k, t] * back_ref[slot_ref[k, t]].astype(F32)
        flat_ref[pl.ds(pl.multiple_of(t * pieces, pieces), pieces), :] = total

    for j in range(pieces):
        out_ref[:, j * 128 : (j + 1) * 128] = flat_ref[pl.ds(j, toks, stride=pieces), :].astype(BF16)


def combine(back, slots, gates):
    count, pieces, lanes = back.shape
    toks = slots.shape[1]
    smem = pl.BlockSpec(memory_space=pltpu.SMEM)
    return pl.pallas_call(
        combine_kernel,
        in_specs=[pl.BlockSpec(memory_space=VMEM), smem, smem],
        out_specs=pl.BlockSpec(memory_space=VMEM),
        out_shape=jax.ShapeDtypeStruct((toks, pieces * lanes), BF16),
        scratch_shapes=[VMEM((toks * pieces, lanes), F32)],
        compiler_params=pltpu.CompilerParams(vmem_limit_bytes=40 * MIB),
        name="combine",
    )(back, slots, gates)


def shards(
    queries,
    key_vectors,
    values,
    out_gate,
    write_strength,
    decay_logarithm,
    residual,
    out_weight,
    head_gain,
    post_gain,
    gate_proj,
    up_proj,
    down_proj,
    expert_ids,
    route_gates,
):
    seq, heads, dv = values.shape
    dk = queries.shape[2]
    n_ctx = lax.axis_size("ctx")
    n_dev = n_ctx * lax.axis_size("exp")
    parts = n_ctx // heads
    wide = dv // parts
    local_experts = gate_proj.shape[0]
    toks, width = residual.shape

    slots = slots_of(expert_ids.T, local_experts * n_dev)
    gates = route_gates.T

    by_head = lambda a: jnp.transpose(a, (1, 0, 2))
    ds = jnp.transpose(
        jnp.concatenate([decay_logarithm, write_strength], axis=0).reshape(2 * heads, seq // CHUNK, CHUNK),
        (1, 0, 2),
    )
    reads, local_out, msg = local_delta(ds, by_head(queries), by_head(key_vectors), by_head(values), parts)
    msg = lax.all_to_all(msg.reshape(n_ctx, dk + wide, dk), "ctx", 0, 0, tiled=True)
    states = lax.all_to_all(prefix_states(msg, wide), "ctx", 0, 0, tiled=True).reshape(heads, dv, dk)
    share = gate_project(reads, local_out, states, by_head(out_gate), head_gain.reshape(1, dv), out_weight)
    summed = lax.psum_scatter(share, "exp", scatter_dimension=0, tiled=True)
    attended, send = dispatch(
        summed, residual, post_gain.reshape(1, width), slots, n_dev * local_experts * CAP
    )
    tall = CAP * width // 128
    held = lax.all_to_all(
        send.reshape(n_dev, local_experts, tall, 128), ("ctx", "exp"), 0, 0, tiled=True
    )
    done = run_experts(held, gate_proj, up_proj, down_proj)
    back = lax.all_to_all(done, ("ctx", "exp"), 0, 0, tiled=True)
    mixture = combine(back.reshape(n_dev * local_experts * CAP, width // 128, 128), slots, gates)
    return (attended, mixture)


def solution(mesh):
    in_specs = (
        P("ctx", "exp", None),
        P("ctx", "exp", None),
        P("ctx", "exp", None),
        P("ctx", "exp", None),
        P("exp", "ctx"),
        P("exp", "ctx"),
        P(("ctx", "exp"), None),
        P("exp", None),
        P(),
        P(),
        P(("ctx", "exp"), None, None),
        P(("ctx", "exp"), None, None),
        P(("ctx", "exp"), None, None),
        P(("ctx", "exp"), None),
        P(("ctx", "exp"), None),
    )
    out_specs = (P(("ctx", "exp"), None), P(("ctx", "exp"), None))
    return jax.shard_map(shards, mesh=mesh, in_specs=in_specs, out_specs=out_specs, check_vma=False)
```

```python
import functools

import jax
import jax.numpy as jnp
from jax import lax
from jax.experimental import pallas as pl
from jax.experimental.pallas import tpu as pltpu
from jax.sharding import PartitionSpec as P

CHUNK = 128
PER_STEP = 4
CAP = 10
F32 = jnp.float32
BF16 = jnp.bfloat16
VMEM = pltpu.VMEM
MIB = 1024 * 1024


def mxu(a, b, dims=((1,), (0,))):
    return lax.dot_general(a, b, (dims, ((), ())), preferred_element_type=F32)


def halves(a):
    high = a.astype(BF16)
    return high, (a - high.astype(F32)).astype(BF16)


def product(a, b):
    width = b[0].shape[1]
    left = jnp.concatenate([a[0], a[1]], axis=1)
    right = jnp.concatenate(
        [
            jnp.concatenate([b[0], b[1]], axis=1),
            jnp.concatenate([b[0], jnp.zeros_like(b[0])], axis=1),
        ],
        axis=0,
    )
    both = mxu(left, right)
    return both[:, :width] + both[:, width:]


def unit_lower_inverses(lowers, row, col):
    eye = (row == col).astype(F32)
    near = row // 16 == col // 16
    diags = [jnp.where(near, low, 0.0) for low in lowers]
    inverses = [eye - diag for diag in diags]
    powers = [halves(-diag) for diag in diags]
    for step in range(3):
        powers = [halves(product(power, power)) for power in powers]
        inverses = [inv + product(halves(inv), power) for inv, power in zip(inverses, powers)]
    size = 16
    while size < row.shape[0]:
        pick = (row // (2 * size) == col // (2 * size)) & (row // size != col // size)
        invs = [halves(inv) for inv in inverses]
        crossed = [halves(product(inv, halves(jnp.where(pick, low, 0.0)))) for inv, low in zip(invs, lowers)]
        inverses = [full - product(cro, inv) for full, cro, inv in zip(inverses, crossed, invs)]
        size = size * 2
    return inverses


def delta_kernel(ds_ref, q_ref, k_ref, v_ref, r_ref, o_ref, msg_ref, state_ref):
    step = pl.program_id(0)
    heads = v_ref.shape[0]
    group = heads // q_ref.shape[0]
    d = q_ref.shape[2]
    c = CHUNK
    per_step = q_ref.shape[1] // c
    row = lax.broadcasted_iota(jnp.int32, (c, c), 0)
    col = lax.broadcasted_iota(jnp.int32, (c, c), 1)
    causal = row >= col
    strict = row > col

    @pl.when(step == 0)
    def _():
        eye = (row == col).astype(F32)
        for h in range(heads):
            state_ref[h] = jnp.concatenate([eye, jnp.zeros_like(eye)], axis=1)

    upto = (row <= col).astype(BF16)
    rows_of, columns_of = [], []
    for n in range(per_step):
        ds = ds_ref[n]
        d0 = ds.astype(BF16)
        rest = ds - d0.astype(F32)
        d1 = rest.astype(BF16)
        d2 = (rest - d1.astype(F32)).astype(BF16)
        cum = mxu(d0, upto) + mxu(d1, upto) + mxu(d2, upto)
        half = jnp.where(lax.broadcasted_iota(jnp.int32, ds.shape, 0) < heads, cum, ds)
        rows_of.append(half)
        columns_of.append(jnp.transpose(half, (1, 0)))

    keyed = []
    for n in range(per_step):
        span = pl.ds(n * c, c)
        for g in range(q_ref.shape[0]):
            q, k = q_ref[g, span], k_ref[g, span]
            qf, kf = q.astype(F32), k.astype(F32)
            q_col = (d ** -0.5) / jnp.sqrt(jnp.sum(qf * qf, axis=1, keepdims=True) + 1e-06)
            k_col = 1.0 / jnp.sqrt(jnp.sum(kf * kf, axis=1, keepdims=True) + 1e-06)
            gram = mxu(k, k, ((1,), (1,)))
            k_row = 1.0 / jnp.sqrt(jnp.sum(jnp.where(row == col, gram, 0.0), axis=0, keepdims=True) + 1e-06)
            gram = gram * (k_col * k_row)
            cross = mxu(q, k, ((1,), (1,))) * (q_col * k_row)
            keyed.append((qf, k, q_col, k_col, k_row, gram, cross, jnp.transpose(kf, (1, 0)).astype(BF16)))

    lowers, mixings = [], []
    for n in range(per_step):
        for h in range(heads):
            gram, cross = keyed[n * q_ref.shape[0] + h // group][5:7]
            cum_col, beta_col = columns_of[n][:, h : h + 1], columns_of[n][:, heads + h : heads + h + 1]
            cum_row = rows_of[n][h : h + 1, :]
            spread = jnp.where(causal, jnp.exp(jnp.where(causal, cum_col - cum_row, 0.0)), 0.0)
            lowers.append(jnp.where(strict, beta_col * gram * spread, 0.0))
            mixings.append((cross * spread).astype(BF16))
    inverses = unit_lower_inverses(lowers, row, col)
    weights, writes = [], []
    for n in range(per_step):
        for h in range(heads):
            k, k_row = keyed[n * q_ref.shape[0] + h // group][1], keyed[n * q_ref.shape[0] + h // group][4]
            cum_row, beta_row = rows_of[n][h : h + 1, :], rows_of[n][heads + h : heads + h + 1, :]
            inverse = inverses[n * heads + h]
            t_k = halves(inverse * (beta_row * jnp.exp(cum_row) * k_row))
            t_v = halves(inverse * beta_row)
            v = v_ref[h, pl.ds(n * c, c)]
            weights.append(
                mxu(jnp.concatenate(t_k, axis=1), jnp.concatenate([k, k], axis=0)).astype(BF16)
            )
            writes.append(mxu(jnp.concatenate(t_v, axis=1), jnp.concatenate([v, v], axis=0)))

    states = [state_ref[h] for h in range(heads)]
    for n in range(per_step):
        span = pl.ds(n * c, c)
        bases = [state.astype(BF16) for state in states]
        reads = [mxu(weights[n * heads + h], bases[h]) for h in range(heads)]
        freshes, tails = [], []
        for h in range(heads):
            k_col = keyed[n * q_ref.shape[0] + h // group][3]
            cum_col = columns_of[n][:, h : h + 1]
            closing = rows_of[n][h : h + 1, c - 1 : c]
            written = writes[n * heads + h]
            fresh = jnp.concatenate([-reads[h][:, :d], written - reads[h][:, d:]], axis=1)
            freshes.append(fresh.astype(BF16))
            tails.append((fresh * (k_col * jnp.exp(closing - cum_col))).astype(BF16))
        for h in range(heads):
            closing = rows_of[n][h : h + 1, c - 1 : c]
            k_t = keyed[n * q_ref.shape[0] + h // group][7]
            states[h] = jnp.exp(closing) * states[h] + mxu(k_t, tails[h])
        for h in range(heads):
            qf, q_col = keyed[n * q_ref.shape[0] + h // group][0], keyed[n * q_ref.shape[0] + h // group][2]
            cum_col = columns_of[n][:, h : h + 1]
            query = (qf * (q_col * jnp.exp(cum_col))).astype(BF16)
            out = mxu(
                jnp.concatenate([query, mixings[n * heads + h]], axis=1),
                jnp.concatenate([bases[h], freshes[h]], axis=0),
            )
            r_ref[h, span] = out[:, :d].astype(BF16)
            o_ref[h, span] = out[:, d:]
    for h in range(heads):
        state_ref[h] = states[h]

    @pl.when(step == pl.num_programs(0) - 1)
    def _():
        parts = msg_ref.shape[1]
        wide = d // parts
        for h in range(heads):
            state = state_ref[h]
            moved = state[:, :d].astype(msg_ref.dtype)
            added = jnp.transpose(state[:, d:], (1, 0)).astype(msg_ref.dtype)
            for p in range(parts):
                msg_ref[h, p, :d, :] = moved
                msg_ref[h, p, d:, :] = added[p * wide : (p + 1) * wide]


def local_delta(ds, q, k, v, parts):
    heads, seq, dv = v.shape
    kh, _, dk = q.shape
    wide = dv // parts
    rows = PER_STEP * CHUNK
    return pl.pallas_call(
        delta_kernel,
        grid=(seq // rows,),
        in_specs=[
            pl.BlockSpec((PER_STEP, 2 * heads, CHUNK), lambda i: (i, 0, 0)),
            pl.BlockSpec((kh, rows, dk), lambda i: (0, i, 0)),
            pl.BlockSpec((kh, rows, dk), lambda i: (0, i, 0)),
            pl.BlockSpec((heads, rows, dv), lambda i: (0, i, 0)),
        ],
        out_specs=[
            pl.BlockSpec((heads, rows, dk), lambda i: (0, i, 0)),
            pl.BlockSpec((heads, rows, dv), lambda i: (0, i, 0)),
            pl.BlockSpec((heads, parts, dk + wide, dk), lambda i: (0, 0, 0, 0)),
        ],
        out_shape=[
            jax.ShapeDtypeStruct((heads, seq, dk), BF16),
            jax.ShapeDtypeStruct((heads, seq, dv), F32),
            jax.ShapeDtypeStruct((heads, parts, dk + wide, dk), BF16),
        ],
        scratch_shapes=[VMEM((heads, dk, dk + dv), F32)],
        compiler_params=pltpu.CompilerParams(
            dimension_semantics=("arbitrary",), vmem_limit_bytes=56 * MIB
        ),
        name="delta_local",
    )(ds, q, k, v)


def prefix_kernel(msg_ref, out_ref):
    count, tall, dk = msg_ref.shape
    wide = tall - dk
    state = jnp.zeros((wide, dk), F32)
    for i in range(count):
        out_ref[i] = state.astype(out_ref.dtype)
        if i < count - 1:
            both = jnp.concatenate(halves(state), axis=0)
            moved = mxu(both, msg_ref[i, :dk, :], ((1,), (1,)))
            state = moved[:wide] + moved[wide:] + msg_ref[i, dk:, :].astype(F32)


def prefix_states(msg, wide):
    count, tall, dk = msg.shape
    return pl.pallas_call(
        prefix_kernel,
        out_shape=jax.ShapeDtypeStruct((count, wide, dk), BF16),
        compiler_params=pltpu.CompilerParams(vmem_limit_bytes=16 * MIB),
        name="prefix_states",
    )(msg)


def gate_kernel(r_ref, o_ref, s_ref, g_ref, gain_ref, out_ref):
    d = r_ref.shape[2]
    for h in range(r_ref.shape[0]):
        core = o_ref[h] + mxu(r_ref[h], s_ref[h], ((1,), (1,)))
        root = jnp.sqrt(jnp.mean(core * core, axis=1, keepdims=True) + 1e-06)
        gate = g_ref[h].astype(F32)
        silu = gate / (1.0 + jnp.exp(-gate))
        out_ref[:, h * d : (h + 1) * d] = (core / root * gain_ref[...] * silu).astype(BF16)


def gated_rows(r, o, states, gate, gain):
    heads, seq, d = r.shape
    rows = 256
    by_rows = pl.BlockSpec((heads, rows, d), lambda i: (0, i, 0))
    return pl.pallas_call(
        gate_kernel,
        grid=(seq // rows,),
        in_specs=[
            by_rows,
            by_rows,
            pl.BlockSpec((heads, d, d), lambda i: (0, 0, 0)),
            by_rows,
            pl.BlockSpec((1, d), lambda i: (0, 0)),
        ],
        out_specs=pl.BlockSpec((rows, heads * d), lambda i: (i, 0)),
        out_shape=jax.ShapeDtypeStruct((seq, heads * d), BF16),
        compiler_params=pltpu.CompilerParams(dimension_semantics=("arbitrary",), vmem_limit_bytes=56 * MIB),
        name="gated_rows",
    )(r, o, states, gate, gain)


def project_kernel(g_ref, w_ref, out_ref):
    part = mxu(g_ref[0], w_ref[...])

    @pl.when(pl.program_id(0) == 0)
    def _():
        out_ref[...] = part

    @pl.when(pl.program_id(0) > 0)
    def _():
        out_ref[...] += part


def project(gated, weight):
    count, toks, deep = gated.shape
    width = weight.shape[1]
    return pl.pallas_call(
        project_kernel,
        grid=(count,),
        in_specs=[
            pl.BlockSpec((1, toks, deep), lambda i: (i, 0, 0)),
            pl.BlockSpec((deep, width), lambda i: (i, 0)),
        ],
        out_specs=pl.BlockSpec((toks, width), lambda i: (0, 0)),
        out_shape=jax.ShapeDtypeStruct((toks, width), F32),
        compiler_params=pltpu.CompilerParams(dimension_semantics=("arbitrary",), vmem_limit_bytes=46 * MIB),
        name="project",
    )(gated, weight)


def slot_kernel(experts, ids_ref, out_ref):
    top, toks = ids_ref.shape
    expert = lax.broadcasted_iota(jnp.int32, (experts, toks), 0)
    hits = jnp.zeros((experts, toks), F32)
    for k in range(top):
        hits = hits + (expert == ids_ref[k : k + 1, :]).astype(F32)
    before = (
        lax.broadcasted_iota(jnp.int32, (toks, toks), 0) < lax.broadcasted_iota(jnp.int32, (toks, toks), 1)
    ).astype(BF16)
    earlier = mxu(hits.astype(BF16), before)
    for k in range(top):
        ids = ids_ref[k : k + 1, :]
        rank = jnp.sum(jnp.where(expert == ids, earlier, 0.0), axis=0, keepdims=True)
        out_ref[k : k + 1, :] = ids * CAP + rank.astype(jnp.int32)


def slots_of(ids, experts):
    return pl.pallas_call(
        functools.partial(slot_kernel, experts),
        out_shape=jax.ShapeDtypeStruct(ids.shape, jnp.int32),
        compiler_params=pltpu.CompilerParams(vmem_limit_bytes=16 * MIB),
        name="slots",
    )(ids)


def dispatch_kernel(part_ref, res_ref, gain_ref, slot_ref, att_ref, send_ref, flat_ref):
    toks, width = part_ref.shape
    pieces = width // 128
    attended = (res_ref[...].astype(F32) + part_ref[...]).astype(BF16)
    att_ref[...] = attended
    settled = attended.astype(F32)
    root = jnp.sqrt(jnp.mean(settled * settled, axis=1, keepdims=True) + 1e-06)
    normed = settled / root * gain_ref[...]
    for j in range(pieces):
        flat_ref[pl.ds(j, toks, stride=pieces), :] = normed[:, j * 128 : (j + 1) * 128]

    @pl.loop(0, toks)
    def _(t):
        tile = flat_ref[pl.ds(pl.multiple_of(t * pieces, pieces), pieces), :].astype(BF16)
        for k in range(slot_ref.shape[0]):
            send_ref[slot_ref[k, t]] = tile


def dispatch(part, residual, gain, slots, count):
    toks, width = part.shape
    pieces = width // 128
    whole = pl.BlockSpec(memory_space=VMEM)
    return pl.pallas_call(
        dispatch_kernel,
        in_specs=[whole, whole, whole, pl.BlockSpec(memory_space=pltpu.SMEM)],
        out_specs=[whole, whole],
        out_shape=[
            jax.ShapeDtypeStruct((toks, width), BF16),
            jax.ShapeDtypeStruct((count, pieces, 128), BF16),
        ],
        scratch_shapes=[VMEM((toks * pieces, 128), F32)],
        compiler_params=pltpu.CompilerParams(vmem_limit_bytes=24 * MIB),
        name="dispatch",
    )(part, residual, gain, slots)


def expert_kernel(x_ref, wg_ref, wu_ref, wd_ref, out_ref, flat_ref):
    sources, _, tall, lanes = x_ref.shape
    rows = flat_ref.shape[0] // 16
    pieces = 16
    flat_ref[...] = x_ref[...].reshape(sources * tall, lanes).astype(F32)
    x = jnp.concatenate(
        [flat_ref[pl.ds(j, rows, stride=pieces), :].astype(BF16) for j in range(pieces)], axis=1
    )
    gate = mxu(x, wg_ref[0])
    up = mxu(x, wu_ref[0])
    inner = (gate / (1.0 + jnp.exp(-gate)) * up).astype(BF16)
    y = mxu(inner, wd_ref[0])
    for j in range(pieces):
        flat_ref[pl.ds(j, rows, stride=pieces), :] = y[:, j * 128 : (j + 1) * 128]
    out_ref[...] = flat_ref[...].astype(BF16).reshape(sources, 1, tall, lanes)


def run_experts(x, gate_proj, up_proj, down_proj):
    count, local, tall, lanes = x.shape
    sources = 64
    rows = sources * tall // 16
    tokens = pl.BlockSpec((sources, 1, tall, lanes), lambda e, i: (i, e, 0, 0))
    return pl.pallas_call(
        expert_kernel,
        grid=(local, count // sources),
        in_specs=[
            tokens,
            pl.BlockSpec((1,) + gate_proj.shape[1:], lambda e, i: (e, 0, 0)),
            pl.BlockSpec((1,) + up_proj.shape[1:], lambda e, i: (e, 0, 0)),
            pl.BlockSpec((1,) + down_proj.shape[1:], lambda e, i: (e, 0, 0)),
        ],
        out_specs=tokens,
        out_shape=jax.ShapeDtypeStruct(x.shape, BF16),
        scratch_shapes=[VMEM((sources * tall, lanes), F32)],
        compiler_params=pltpu.CompilerParams(
            dimension_semantics=("arbitrary", "arbitrary"), vmem_limit_bytes=56 * MIB
        ),
        name="experts",
    )(x, gate_proj, up_proj, down_proj)


def combine_kernel(back_ref, slot_ref, gate_ref, out_ref, flat_ref):
    toks, width = out_ref.shape
    pieces = width // 128

    @pl.loop(0, toks)
    def _(t):
        total = jnp.zeros((pieces, 128), F32)
        for k in range(slot_ref.shape[0]):
            total = total + gate_ref[k, t] * back_ref[slot_ref[k, t]].astype(F32)
        flat_ref[pl.ds(pl.multiple_of(t * pieces, pieces), pieces), :] = total

    for j in range(pieces):
        out_ref[:, j * 128 : (j + 1) * 128] = flat_ref[pl.ds(j, toks, stride=pieces), :].astype(BF16)


def combine(back, slots, gates):
    count, pieces, lanes = back.shape
    toks = slots.shape[1]
    smem = pl.BlockSpec(memory_space=pltpu.SMEM)
    return pl.pallas_call(
        combine_kernel,
        in_specs=[pl.BlockSpec(memory_space=VMEM), smem, smem],
        out_specs=pl.BlockSpec(memory_space=VMEM),
        out_shape=jax.ShapeDtypeStruct((toks, pieces * lanes), BF16),
        scratch_shapes=[VMEM((toks * pieces, lanes), F32)],
        compiler_params=pltpu.CompilerParams(vmem_limit_bytes=24 * MIB),
        name="combine",
    )(back, slots, gates)


def shards(
    queries,
    key_vectors,
    values,
    out_gate,
    write_strength,
    decay_logarithm,
    residual,
    out_weight,
    head_gain,
    post_gain,
    gate_proj,
    up_proj,
    down_proj,
    expert_ids,
    route_gates,
):
    seq, heads, dv = values.shape
    dk = queries.shape[2]
    n_ctx = lax.axis_size("ctx")
    n_exp = lax.axis_size("exp")
    n_dev = n_ctx * n_exp
    parts = n_ctx // heads
    wide = dv // parts
    local_experts = gate_proj.shape[0]
    toks, width = residual.shape

    whole_weight = lax.all_gather(out_weight, "exp", axis=0, tiled=True)
    slots = slots_of(expert_ids.T, local_experts * n_dev)
    gates = route_gates.T

    by_head = lambda a: jnp.transpose(a, (1, 0, 2))
    ds = jnp.transpose(
        jnp.concatenate([decay_logarithm, write_strength], axis=0).reshape(2 * heads, seq // CHUNK, CHUNK),
        (1, 0, 2),
    )
    reads, local_out, msg = local_delta(ds, by_head(queries), by_head(key_vectors), by_head(values), parts)
    msg = lax.all_to_all(msg.reshape(n_ctx, dk + wide, dk), "ctx", 0, 0, tiled=True)
    states = lax.all_to_all(prefix_states(msg, wide), "ctx", 0, 0, tiled=True).reshape(heads, dv, dk)
    gated = gated_rows(reads, local_out, states, by_head(out_gate), head_gain.reshape(1, dv))
    gated = lax.all_to_all(gated.reshape(n_exp, toks, heads * dv), "exp", 0, 0, tiled=True)
    summed = project(gated, whole_weight)
    attended, send = dispatch(
        summed, residual, post_gain.reshape(1, width), slots, n_dev * local_experts * CAP
    )
    tall = CAP * width // 128
    held = lax.all_to_all(
        send.reshape(n_dev, local_experts, tall, 128), ("ctx", "exp"), 0, 0, tiled=True
    )
    done = run_experts(held, gate_proj, up_proj, down_proj)
    back = lax.all_to_all(done, ("ctx", "exp"), 0, 0, tiled=True)
    mixture = combine(back.reshape(n_dev * local_experts * CAP, width // 128, 128), slots, gates)
    return (attended, mixture)


def solution(mesh):
    in_specs = (
        P("ctx", "exp", None),
        P("ctx", "exp", None),
        P("ctx", "exp", None),
        P("ctx", "exp", None),
        P("exp", "ctx"),
        P("exp", "ctx"),
        P(("ctx", "exp"), None),
        P("exp", None),
        P(),
        P(),
        P(("ctx", "exp"), None, None),
        P(("ctx", "exp"), None, None),
        P(("ctx", "exp"), None, None),
        P(("ctx", "exp"), None),
        P(("ctx", "exp"), None),
    )
    out_specs = (P(("ctx", "exp"), None), P(("ctx", "exp"), None))
    return jax.shard_map(shards, mesh=mesh, in_specs=in_specs, out_specs=out_specs, check_vma=False)
```

```python
import functools

import jax
import jax.numpy as jnp
from jax import lax
from jax.experimental import pallas as pl
from jax.experimental.pallas import tpu as pltpu
from jax.sharding import PartitionSpec as P

CHUNK = 128
PER_STEP = 4
CAP = 10
PITCH = 24
F32 = jnp.float32
BF16 = jnp.bfloat16
VMEM = pltpu.VMEM
MIB = 1024 * 1024


def mxu(a, b, dims=((1,), (0,))):
    return lax.dot_general(a, b, (dims, ((), ())), preferred_element_type=F32)


def halves(a):
    high = a.astype(BF16)
    return high, (a - high.astype(F32)).astype(BF16)


def product(a, b):
    width = b[0].shape[1]
    left = jnp.concatenate([a[0], a[1]], axis=1)
    right = jnp.concatenate(
        [
            jnp.concatenate([b[0], b[1]], axis=1),
            jnp.concatenate([b[0], jnp.zeros_like(b[0])], axis=1),
        ],
        axis=0,
    )
    both = mxu(left, right)
    return both[:, :width] + both[:, width:]


def unit_lower_inverses(lowers, row, col):
    eye = (row == col).astype(F32)
    near = row // 16 == col // 16
    diags = [jnp.where(near, low, 0.0) for low in lowers]
    inverses = [eye - diag for diag in diags]
    powers = [halves(-diag) for diag in diags]
    for step in range(3):
        powers = [halves(product(power, power)) for power in powers]
        inverses = [inv + product(halves(inv), power) for inv, power in zip(inverses, powers)]
    size = 16
    while size < row.shape[0]:
        pick = (row // (2 * size) == col // (2 * size)) & (row // size != col // size)
        invs = [halves(inv) for inv in inverses]
        crossed = [halves(product(inv, halves(jnp.where(pick, low, 0.0)))) for inv, low in zip(invs, lowers)]
        inverses = [full - product(cro, inv) for full, cro, inv in zip(inverses, crossed, invs)]
        size = size * 2
    return inverses


def delta_kernel(ds_ref, q_ref, k_ref, v_ref, r_ref, o_ref, msg_ref, state_ref):
    step = pl.program_id(0)
    heads = v_ref.shape[0]
    group = heads // q_ref.shape[0]
    d = q_ref.shape[2]
    c = CHUNK
    per_step = q_ref.shape[1] // c
    row = lax.broadcasted_iota(jnp.int32, (c, c), 0)
    col = lax.broadcasted_iota(jnp.int32, (c, c), 1)
    causal = row >= col
    strict = row > col

    @pl.when(step == 0)
    def _():
        eye = (row == col).astype(F32)
        for h in range(heads):
            state_ref[h] = jnp.concatenate([eye, jnp.zeros_like(eye)], axis=1)

    upto = (row <= col).astype(BF16)
    rows_of, columns_of = [], []
    for n in range(per_step):
        ds = ds_ref[n]
        d0 = ds.astype(BF16)
        rest = ds - d0.astype(F32)
        d1 = rest.astype(BF16)
        d2 = (rest - d1.astype(F32)).astype(BF16)
        cum = mxu(d0, upto) + mxu(d1, upto) + mxu(d2, upto)
        half = jnp.where(lax.broadcasted_iota(jnp.int32, ds.shape, 0) < heads, cum, ds)
        rows_of.append(half)
        columns_of.append(jnp.transpose(half, (1, 0)))

    keyed = []
    for n in range(per_step):
        span = pl.ds(n * c, c)
        for g in range(q_ref.shape[0]):
            q, k = q_ref[g, span], k_ref[g, span]
            qf, kf = q.astype(F32), k.astype(F32)
            q_col = (d ** -0.5) / jnp.sqrt(jnp.sum(qf * qf, axis=1, keepdims=True) + 1e-06)
            k_col = 1.0 / jnp.sqrt(jnp.sum(kf * kf, axis=1, keepdims=True) + 1e-06)
            gram = mxu(k, k, ((1,), (1,)))
            k_row = 1.0 / jnp.sqrt(jnp.sum(jnp.where(row == col, gram, 0.0), axis=0, keepdims=True) + 1e-06)
            gram = gram * (k_col * k_row)
            cross = mxu(q, k, ((1,), (1,))) * (q_col * k_row)
            keyed.append((qf, k, q_col, k_col, k_row, gram, cross, jnp.transpose(kf, (1, 0)).astype(BF16)))

    lowers, mixings = [], []
    for n in range(per_step):
        for h in range(heads):
            gram, cross = keyed[n * q_ref.shape[0] + h // group][5:7]
            cum_col, beta_col = columns_of[n][:, h : h + 1], columns_of[n][:, heads + h : heads + h + 1]
            cum_row = rows_of[n][h : h + 1, :]
            spread = jnp.where(causal, jnp.exp(jnp.where(causal, cum_col - cum_row, 0.0)), 0.0)
            lowers.append(jnp.where(strict, beta_col * gram * spread, 0.0))
            mixings.append((cross * spread).astype(BF16))
    inverses = unit_lower_inverses(lowers, row, col)
    weights, writes = [], []
    for n in range(per_step):
        for h in range(heads):
            k, k_row = keyed[n * q_ref.shape[0] + h // group][1], keyed[n * q_ref.shape[0] + h // group][4]
            cum_row, beta_row = rows_of[n][h : h + 1, :], rows_of[n][heads + h : heads + h + 1, :]
            inverse = inverses[n * heads + h]
            t_k = halves(inverse * (beta_row * jnp.exp(cum_row) * k_row))
            t_v = halves(inverse * beta_row)
            v = v_ref[h, pl.ds(n * c, c)]
            weights.append(
                mxu(jnp.concatenate(t_k, axis=1), jnp.concatenate([k, k], axis=0)).astype(BF16)
            )
            writes.append(mxu(jnp.concatenate(t_v, axis=1), jnp.concatenate([v, v], axis=0)))

    states = [state_ref[h] for h in range(heads)]
    for n in range(per_step):
        span = pl.ds(n * c, c)
        bases = [state.astype(BF16) for state in states]
        reads = [mxu(weights[n * heads + h], bases[h]) for h in range(heads)]
        freshes, tails = [], []
        for h in range(heads):
            k_col = keyed[n * q_ref.shape[0] + h // group][3]
            cum_col = columns_of[n][:, h : h + 1]
            closing = rows_of[n][h : h + 1, c - 1 : c]
            written = writes[n * heads + h]
            fresh = jnp.concatenate([-reads[h][:, :d], written - reads[h][:, d:]], axis=1)
            freshes.append(fresh.astype(BF16))
            tails.append((fresh * (k_col * jnp.exp(closing - cum_col))).astype(BF16))
        for h in range(heads):
            closing = rows_of[n][h : h + 1, c - 1 : c]
            k_t = keyed[n * q_ref.shape[0] + h // group][7]
            states[h] = jnp.exp(closing) * states[h] + mxu(k_t, tails[h])
        for h in range(heads):
            qf, q_col = keyed[n * q_ref.shape[0] + h // group][0], keyed[n * q_ref.shape[0] + h // group][2]
            cum_col = columns_of[n][:, h : h + 1]
            query = (qf * (q_col * jnp.exp(cum_col))).astype(BF16)
            out = mxu(
                jnp.concatenate([query, mixings[n * heads + h]], axis=1),
                jnp.concatenate([bases[h], freshes[h]], axis=0),
            )
            r_ref[h, span] = out[:, :d].astype(BF16)
            o_ref[h, span] = out[:, d:]
    for h in range(heads):
        state_ref[h] = states[h]

    @pl.when(step == pl.num_programs(0) - 1)
    def _():
        parts = msg_ref.shape[1]
        wide = d // parts
        for h in range(heads):
            state = state_ref[h]
            moved = state[:, :d].astype(msg_ref.dtype)
            added = jnp.transpose(state[:, d:], (1, 0)).astype(msg_ref.dtype)
            for p in range(parts):
                msg_ref[h, p, :d, :] = moved
                msg_ref[h, p, d:, :] = added[p * wide : (p + 1) * wide]


def local_delta(ds, q, k, v, parts):
    heads, seq, dv = v.shape
    kh, _, dk = q.shape
    wide = dv // parts
    rows = PER_STEP * CHUNK
    return pl.pallas_call(
        delta_kernel,
        grid=(seq // rows,),
        in_specs=[
            pl.BlockSpec((PER_STEP, 2 * heads, CHUNK), lambda i: (i, 0, 0)),
            pl.BlockSpec((kh, rows, dk), lambda i: (0, i, 0)),
            pl.BlockSpec((kh, rows, dk), lambda i: (0, i, 0)),
            pl.BlockSpec((heads, rows, dv), lambda i: (0, i, 0)),
        ],
        out_specs=[
            pl.BlockSpec((heads, rows, dk), lambda i: (0, i, 0)),
            pl.BlockSpec((heads, rows, dv), lambda i: (0, i, 0)),
            pl.BlockSpec((heads, parts, dk + wide, dk), lambda i: (0, 0, 0, 0)),
        ],
        out_shape=[
            jax.ShapeDtypeStruct((heads, seq, dk), BF16),
            jax.ShapeDtypeStruct((heads, seq, dv), F32),
            jax.ShapeDtypeStruct((heads, parts, dk + wide, dk), BF16),
        ],
        scratch_shapes=[VMEM((heads, dk, dk + dv), F32)],
        compiler_params=pltpu.CompilerParams(
            dimension_semantics=("arbitrary",), vmem_limit_bytes=56 * MIB
        ),
        name="delta_local",
    )(ds, q, k, v)


def prefix_kernel(msg_ref, out_ref):
    count, tall, dk = msg_ref.shape
    wide = tall - dk
    state = jnp.zeros((wide, dk), F32)
    for i in range(count):
        out_ref[i] = state.astype(out_ref.dtype)
        if i < count - 1:
            both = jnp.concatenate(halves(state), axis=0)
            moved = mxu(both, msg_ref[i, :dk, :], ((1,), (1,)))
            state = moved[:wide] + moved[wide:] + msg_ref[i, dk:, :].astype(F32)


def prefix_states(msg, wide):
    count, tall, dk = msg.shape
    return pl.pallas_call(
        prefix_kernel,
        out_shape=jax.ShapeDtypeStruct((count, wide, dk), BF16),
        compiler_params=pltpu.CompilerParams(vmem_limit_bytes=16 * MIB),
        name="prefix_states",
    )(msg)


def gate_kernel(place_ref, r_ref, o_ref, s_ref, g_ref, gain_ref, keep_ref, give_ref):
    d = r_ref.shape[2]
    rows = keep_ref.shape[1]
    core = place_ref[0]
    for part, out_ref in ((core, keep_ref), (1 - core, give_ref)):
        span = pl.ds(pl.multiple_of(part * rows, rows), rows)
        for h in range(r_ref.shape[0]):
            value = o_ref[h, span, :] + mxu(r_ref[h, span, :], s_ref[h], ((1,), (1,)))
            root = jnp.sqrt(jnp.mean(value * value, axis=1, keepdims=True) + 1e-06)
            gate = g_ref[h, span, :].astype(F32)
            silu = gate / (1.0 + jnp.exp(-gate))
            out_ref[0, :, h * d : (h + 1) * d] = (value / root * gain_ref[...] * silu).astype(BF16)


def gated_rows(place, r, o, states, gate, gain, toks):
    heads, seq, d = r.shape
    rows = 2 * toks
    by_rows = pl.BlockSpec((heads, rows, d), lambda i, p: (0, i, 0))
    out = pl.BlockSpec((1, toks, heads * d), lambda i, p: (i, 0, 0))
    shape = jax.ShapeDtypeStruct((seq // rows, toks, heads * d), BF16)
    return pl.pallas_call(
        gate_kernel,
        grid_spec=pltpu.PrefetchScalarGridSpec(
            num_scalar_prefetch=1,
            grid=(seq // rows,),
            in_specs=[
                by_rows,
                by_rows,
                pl.BlockSpec((heads, d, d), lambda i, p: (0, 0, 0)),
                by_rows,
                pl.BlockSpec((1, d), lambda i, p: (0, 0)),
            ],
            out_specs=[out, out],
        ),
        out_shape=[shape, shape],
        compiler_params=pltpu.CompilerParams(dimension_semantics=("arbitrary",), vmem_limit_bytes=56 * MIB),
        name="gated_rows",
    )(place, r, o, states, gate, gain)


def far_kernel(place_ref, mine_ref, got_ref, w_ref, v_ref, a_ref, b_ref):
    part = mxu(mine_ref[0], w_ref[...]) + mxu(got_ref[0], v_ref[...])
    half = a_ref.shape[0]
    a_ref[...] = part[:half].astype(BF16)
    b_ref[...] = part[half:].astype(BF16)


def near_kernel(place_ref, mine_ref, got_ref, w_ref, v_ref, out_ref):
    out_ref[0] = mxu(mine_ref[0], w_ref[...]) + mxu(got_ref[0], v_ref[...])


def project(place, mine, got, weight, other, near):
    count, toks, deep = mine.shape
    width = weight.shape[1]
    step = (lambda i: lax.rem(1 + 2 * i, 4) * (1 - i // 2)) if near else (lambda i: i + 2)
    chunk = pl.BlockSpec((1, toks, deep), lambda i, p: (lax.rem(p[1] + step(i), count), 0, 0))
    whole = pl.BlockSpec(weight.shape, lambda i, p: (0, 0))
    half = jax.ShapeDtypeStruct((toks // 2, width), BF16)
    steps = 3 if near else 1
    return pl.pallas_call(
        near_kernel if near else far_kernel,
        grid_spec=pltpu.PrefetchScalarGridSpec(
            num_scalar_prefetch=1,
            grid=(steps,),
            in_specs=[chunk, chunk, whole, whole],
            out_specs=pl.BlockSpec((1, toks, width), lambda i, p: (i, 0, 0))
            if near
            else [pl.BlockSpec((toks // 2, width), lambda i, p: (0, 0))] * 2,
        ),
        out_shape=jax.ShapeDtypeStruct((3, toks, width), F32) if near else [half, half],
        cost_estimate=pl.CostEstimate(
            flops=4 * steps * toks * deep * width,
            bytes_accessed=4 * weight.size + 4 * steps * toks * width,
            transcendentals=0,
        ),
        compiler_params=pltpu.CompilerParams(dimension_semantics=("arbitrary",), vmem_limit_bytes=24 * MIB),
        name="project_near" if near else "project_far",
    )(place, mine, got, weight, other)


def relay_kernel(near_ref, a_ref, b_ref, right_ref, left_ref):
    half = a_ref.shape[0]
    right_ref[:half] = (near_ref[0, :half] + a_ref[...].astype(F32)).astype(BF16)
    right_ref[half:] = near_ref[0, half:].astype(BF16)
    left_ref[:half] = near_ref[1, :half].astype(BF16)
    left_ref[half:] = (near_ref[1, half:] + b_ref[...].astype(F32)).astype(BF16)


def relay(near, first, second):
    shape = jax.ShapeDtypeStruct(near.shape[1:], BF16)
    return pl.pallas_call(
        relay_kernel,
        out_shape=[shape, shape],
        compiler_params=pltpu.CompilerParams(vmem_limit_bytes=16 * MIB),
        name="relay",
    )(near, first, second)


def slot_kernel(experts, ids_ref, out_ref):
    top, toks = ids_ref.shape
    expert = lax.broadcasted_iota(jnp.int32, (experts, toks), 0)
    hits = jnp.zeros((experts, toks), F32)
    for k in range(top):
        hits = hits + (expert == ids_ref[k : k + 1, :]).astype(F32)
    before = (
        lax.broadcasted_iota(jnp.int32, (toks, toks), 0) < lax.broadcasted_iota(jnp.int32, (toks, toks), 1)
    ).astype(BF16)
    earlier = mxu(hits.astype(BF16), before)
    for k in range(top):
        ids = ids_ref[k : k + 1, :]
        rank = jnp.sum(jnp.where(expert == ids, earlier, 0.0), axis=0, keepdims=True)
        out_ref[k : k + 1, :] = ids * CAP + rank.astype(jnp.int32)


def slots_of(ids, experts):
    return pl.pallas_call(
        functools.partial(slot_kernel, experts),
        out_shape=jax.ShapeDtypeStruct(ids.shape, jnp.int32),
        compiler_params=pltpu.CompilerParams(vmem_limit_bytes=16 * MIB),
        name="slots",
    )(ids)


def dispatch_kernel(near_ref, back_ref, ahead_ref, res_ref, gain_ref, slot_ref, att_ref, send_ref, flat_ref):
    toks, width = res_ref.shape
    pieces = width // 128
    total = near_ref[2] + back_ref[...].astype(F32) + ahead_ref[...].astype(F32)
    attended = (res_ref[...].astype(F32) + total).astype(BF16)
    att_ref[...] = attended
    settled = attended.astype(F32)
    root = jnp.sqrt(jnp.mean(settled * settled, axis=1, keepdims=True) + 1e-06)
    normed = settled / root * gain_ref[...]
    for j in range(pieces):
        flat_ref[pl.ds(j, toks, stride=pieces), :] = normed[:, j * 128 : (j + 1) * 128]

    @pl.loop(0, toks)
    def _(t):
        tile = flat_ref[pl.ds(pl.multiple_of(t * pieces, pieces), pieces), :].astype(BF16)
        for k in range(slot_ref.shape[0]):
            send_ref[slot_ref[k, t]] = tile


def dispatch(near, back, ahead, residual, gain, slots, count):
    toks, width = residual.shape
    pieces = width // 128
    whole = pl.BlockSpec(memory_space=VMEM)
    return pl.pallas_call(
        dispatch_kernel,
        in_specs=[whole] * 5 + [pl.BlockSpec(memory_space=pltpu.SMEM)],
        out_specs=[whole, whole],
        out_shape=[
            jax.ShapeDtypeStruct((toks, width), BF16),
            jax.ShapeDtypeStruct((count, pieces, 128), BF16),
        ],
        scratch_shapes=[VMEM((toks * pieces, 128), F32)],
        compiler_params=pltpu.CompilerParams(vmem_limit_bytes=24 * MIB),
        name="dispatch",
    )(near, back, ahead, residual, gain, slots)


def expert_kernel(x_ref, wg_ref, wu_ref, wd_ref, out_ref, flat_ref):
    sources, _, tall, lanes = x_ref.shape
    pieces = wg_ref.shape[1] // lanes
    rows = flat_ref.shape[0] // PITCH
    tiles_ref = flat_ref.reshape(rows, PITCH, lanes)
    tiles_ref[:, :pieces, :] = x_ref[...].reshape(rows, pieces, lanes).astype(F32)
    x = jnp.concatenate(
        [flat_ref[pl.ds(j, rows, stride=PITCH), :].astype(BF16) for j in range(pieces)], axis=1
    )
    gate = mxu(x, wg_ref[0])
    up = mxu(x, wu_ref[0])
    inner = (gate / (1.0 + jnp.exp(-gate)) * up).astype(BF16)
    y = mxu(inner, wd_ref[0])
    for j in range(pieces):
        flat_ref[pl.ds(j, rows, stride=PITCH), :] = y[:, j * lanes : (j + 1) * lanes]
    out_ref[...] = tiles_ref[:, :pieces, :].astype(BF16).reshape(sources, 1, tall, lanes)


def run_experts(x, gate_proj, up_proj, down_proj):
    count, local, tall, lanes = x.shape
    sources = 64
    rows = sources * tall * lanes // gate_proj.shape[1]
    tokens = pl.BlockSpec((sources, 1, tall, lanes), lambda e, i: (i, e, 0, 0))
    return pl.pallas_call(
        expert_kernel,
        grid=(local, count // sources),
        in_specs=[
            tokens,
            pl.BlockSpec((1,) + gate_proj.shape[1:], lambda e, i: (e, 0, 0)),
            pl.BlockSpec((1,) + up_proj.shape[1:], lambda e, i: (e, 0, 0)),
            pl.BlockSpec((1,) + down_proj.shape[1:], lambda e, i: (e, 0, 0)),
        ],
        out_specs=tokens,
        out_shape=jax.ShapeDtypeStruct(x.shape, BF16),
        scratch_shapes=[VMEM((rows * PITCH, lanes), F32)],
        compiler_params=pltpu.CompilerParams(
            dimension_semantics=("arbitrary", "arbitrary"), vmem_limit_bytes=56 * MIB
        ),
        name="experts",
    )(x, gate_proj, up_proj, down_proj)


def combine_kernel(back_ref, slot_ref, gate_ref, out_ref, flat_ref):
    toks, width = out_ref.shape
    pieces = width // 128

    @pl.loop(0, toks)
    def _(t):
        total = jnp.zeros((pieces, 128), F32)
        for k in range(slot_ref.shape[0]):
            total = total + gate_ref[k, t] * back_ref[slot_ref[k, t]].astype(F32)
        flat_ref[pl.ds(pl.multiple_of(t * pieces, pieces), pieces), :] = total

    for j in range(pieces):
        out_ref[:, j * 128 : (j + 1) * 128] = flat_ref[pl.ds(j, toks, stride=pieces), :].astype(BF16)


def combine(back, slots, gates):
    count, pieces, lanes = back.shape
    toks = slots.shape[1]
    smem = pl.BlockSpec(memory_space=pltpu.SMEM)
    return pl.pallas_call(
        combine_kernel,
        in_specs=[pl.BlockSpec(memory_space=VMEM), smem, smem],
        out_specs=pl.BlockSpec(memory_space=VMEM),
        out_shape=jax.ShapeDtypeStruct((toks, pieces * lanes), BF16),
        scratch_shapes=[VMEM((toks * pieces, lanes), F32)],
        compiler_params=pltpu.CompilerParams(vmem_limit_bytes=24 * MIB),
        name="combine",
    )(back, slots, gates)


def shards(
    queries,
    key_vectors,
    values,
    out_gate,
    write_strength,
    decay_logarithm,
    residual,
    out_weight,
    head_gain,
    post_gain,
    gate_proj,
    up_proj,
    down_proj,
    expert_ids,
    route_gates,
):
    seq, heads, dv = values.shape
    dk = queries.shape[2]
    n_ctx = lax.axis_size("ctx")
    n_exp = lax.axis_size("exp")
    n_dev = n_ctx * n_exp
    parts = n_ctx // heads
    wide = dv // parts
    local_experts = gate_proj.shape[0]
    toks, width = residual.shape

    place = lax.axis_index("exp")
    place = jnp.stack([place & 1, place >> 1])
    shift = lambda a, by: lax.ppermute(a, "exp", [(i, (i + 2 * by) % n_exp) for i in range(n_exp)])
    swap = lambda a: lax.ppermute(a, "exp", [(i, i ^ 1) for i in range(n_exp)])
    other_weight = swap(out_weight)
    slots = slots_of(expert_ids.T, local_experts * n_dev)
    gates = route_gates.T

    by_head = lambda a: jnp.transpose(a, (1, 0, 2))
    ds = jnp.transpose(
        jnp.concatenate([decay_logarithm, write_strength], axis=0).reshape(2 * heads, seq // CHUNK, CHUNK),
        (1, 0, 2),
    )
    reads, local_out, msg = local_delta(ds, by_head(queries), by_head(key_vectors), by_head(values), parts)
    msg = lax.all_to_all(msg.reshape(n_ctx, dk + wide, dk), "ctx", 0, 0, tiled=True)
    states = lax.all_to_all(prefix_states(msg, wide), "ctx", 0, 0, tiled=True).reshape(heads, dv, dk)
    mine, give = gated_rows(
        place, reads, local_out, states, by_head(out_gate), head_gain.reshape(1, dv), toks
    )
    got = swap(give)
    first, second = project(place, mine, got, out_weight, other_weight, False)
    first, second = shift(first, 1), shift(second, -1)
    near = project(place, mine, got, out_weight, other_weight, True)
    right, left = relay(near, first, second)
    attended, send = dispatch(
        near, shift(right, 1), shift(left, -1), residual, post_gain.reshape(1, width), slots, n_dev * local_experts * CAP
    )
    tall = CAP * width // 128
    held = lax.all_to_all(
        send.reshape(n_dev, local_experts, tall, 128), ("ctx", "exp"), 0, 0, tiled=True
    )
    done = run_experts(held, gate_proj, up_proj, down_proj)
    back = lax.all_to_all(done, ("ctx", "exp"), 0, 0, tiled=True)
    mixture = combine(back.reshape(n_dev * local_experts * CAP, width // 128, 128), slots, gates)
    return (attended, mixture)


def solution(mesh):
    in_specs = (
        P("ctx", "exp", None),
        P("ctx", "exp", None),
        P("ctx", "exp", None),
        P("ctx", "exp", None),
        P("exp", "ctx"),
        P("exp", "ctx"),
        P(("ctx", "exp"), None),
        P("exp", None),
        P(),
        P(),
        P(("ctx", "exp"), None, None),
        P(("ctx", "exp"), None, None),
        P(("ctx", "exp"), None, None),
        P(("ctx", "exp"), None),
        P(("ctx", "exp"), None),
    )
    out_specs = (P(("ctx", "exp"), None), P(("ctx", "exp"), None))
    return jax.shard_map(shards, mesh=mesh, in_specs=in_specs, out_specs=out_specs, check_vma=False)
```

```python
import functools

import jax
import jax.numpy as jnp
from jax import lax
from jax.experimental import pallas as pl
from jax.experimental.pallas import tpu as pltpu
from jax.sharding import PartitionSpec as P

CHUNK = 128
PER_STEP = 4
CAP = 10
PITCH = 24
F32 = jnp.float32
BF16 = jnp.bfloat16
VMEM = pltpu.VMEM
MIB = 1024 * 1024


def mxu(a, b, dims=((1,), (0,))):
    return lax.dot_general(a, b, (dims, ((), ())), preferred_element_type=F32)


def halves(a):
    high = a.astype(BF16)
    return high, (a - high.astype(F32)).astype(BF16)


def product(a, b):
    width = b[0].shape[1]
    left = jnp.concatenate([a[0], a[1]], axis=1)
    right = jnp.concatenate(
        [
            jnp.concatenate([b[0], b[1]], axis=1),
            jnp.concatenate([b[0], jnp.zeros_like(b[0])], axis=1),
        ],
        axis=0,
    )
    both = mxu(left, right)
    return both[:, :width] + both[:, width:]


def unit_lower_inverses(lowers, row, col):
    eye = (row == col).astype(F32)
    near = row // 16 == col // 16
    diags = [jnp.where(near, low, 0.0) for low in lowers]
    inverses = [eye - diag for diag in diags]
    powers = [halves(-diag) for diag in diags]
    for step in range(3):
        powers = [halves(product(power, power)) for power in powers]
        inverses = [inv + product(halves(inv), power) for inv, power in zip(inverses, powers)]
    size = 16
    while size < row.shape[0]:
        pick = (row // (2 * size) == col // (2 * size)) & (row // size != col // size)
        belows = [jnp.where(pick, low, 0.0).astype(BF16) for low in lowers]
        invs = [inv.astype(BF16) for inv in inverses]
        crossed = [mxu(inv, below).astype(BF16) for inv, below in zip(invs, belows)]
        inverses = [full - mxu(cro, inv) for full, cro, inv in zip(inverses, crossed, invs)]
        size = size * 2
    return inverses


def delta_kernel(ds_ref, q_ref, k_ref, v_ref, r_ref, o_ref, msg_ref, state_ref):
    step = pl.program_id(0)
    heads = v_ref.shape[0]
    group = heads // q_ref.shape[0]
    d = q_ref.shape[2]
    c = CHUNK
    per_step = q_ref.shape[1] // c
    row = lax.broadcasted_iota(jnp.int32, (c, c), 0)
    col = lax.broadcasted_iota(jnp.int32, (c, c), 1)
    causal = row >= col
    strict = row > col

    @pl.when(step == 0)
    def _():
        eye = (row == col).astype(F32)
        for h in range(heads):
            state_ref[h] = jnp.concatenate([eye, jnp.zeros_like(eye)], axis=1)

    upto = (row <= col).astype(BF16)
    rows_of, columns_of = [], []
    for n in range(per_step):
        ds = ds_ref[n]
        d0 = ds.astype(BF16)
        rest = ds - d0.astype(F32)
        d1 = rest.astype(BF16)
        d2 = (rest - d1.astype(F32)).astype(BF16)
        cum = mxu(d0, upto) + mxu(d1, upto) + mxu(d2, upto)
        half = jnp.where(lax.broadcasted_iota(jnp.int32, ds.shape, 0) < heads, cum, ds)
        rows_of.append(half)
        columns_of.append(jnp.transpose(half, (1, 0)))

    keyed = []
    for n in range(per_step):
        span = pl.ds(n * c, c)
        for g in range(q_ref.shape[0]):
            q, k = q_ref[g, span], k_ref[g, span]
            qf, kf = q.astype(F32), k.astype(F32)
            q_col = (d ** -0.5) / jnp.sqrt(jnp.sum(qf * qf, axis=1, keepdims=True) + 1e-06)
            k_col = 1.0 / jnp.sqrt(jnp.sum(kf * kf, axis=1, keepdims=True) + 1e-06)
            gram = mxu(k, k, ((1,), (1,)))
            k_row = 1.0 / jnp.sqrt(jnp.sum(jnp.where(row == col, gram, 0.0), axis=0, keepdims=True) + 1e-06)
            gram = gram * (k_col * k_row)
            cross = mxu(q, k, ((1,), (1,))) * (q_col * k_row)
            keyed.append((qf, k, q_col, k_col, k_row, gram, cross, jnp.transpose(kf, (1, 0)).astype(BF16)))

    lowers, mixings = [], []
    for n in range(per_step):
        for h in range(heads):
            gram, cross = keyed[n * q_ref.shape[0] + h // group][5:7]
            cum_col, beta_col = columns_of[n][:, h : h + 1], columns_of[n][:, heads + h : heads + h + 1]
            cum_row = rows_of[n][h : h + 1, :]
            spread = jnp.where(causal, jnp.exp(jnp.where(causal, cum_col - cum_row, 0.0)), 0.0)
            lowers.append(jnp.where(strict, beta_col * gram * spread, 0.0))
            mixings.append((cross * spread).astype(BF16))
    inverses = unit_lower_inverses(lowers, row, col)
    weights, writes = [], []
    for n in range(per_step):
        for h in range(heads):
            k, k_row = keyed[n * q_ref.shape[0] + h // group][1], keyed[n * q_ref.shape[0] + h // group][4]
            cum_row, beta_row = rows_of[n][h : h + 1, :], rows_of[n][heads + h : heads + h + 1, :]
            inverse = inverses[n * heads + h]
            t_k = halves(inverse * (beta_row * jnp.exp(cum_row) * k_row))
            t_v = halves(inverse * beta_row)
            v = v_ref[h, pl.ds(n * c, c)]
            weights.append(
                mxu(jnp.concatenate(t_k, axis=1), jnp.concatenate([k, k], axis=0)).astype(BF16)
            )
            writes.append(mxu(jnp.concatenate(t_v, axis=1), jnp.concatenate([v, v], axis=0)))

    states = [state_ref[h] for h in range(heads)]
    for n in range(per_step):
        span = pl.ds(n * c, c)
        bases = [state.astype(BF16) for state in states]
        reads = [mxu(weights[n * heads + h], bases[h]) for h in range(heads)]
        freshes, tails = [], []
        for h in range(heads):
            k_col = keyed[n * q_ref.shape[0] + h // group][3]
            cum_col = columns_of[n][:, h : h + 1]
            closing = rows_of[n][h : h + 1, c - 1 : c]
            written = writes[n * heads + h]
            fresh = jnp.concatenate([-reads[h][:, :d], written - reads[h][:, d:]], axis=1)
            freshes.append(fresh.astype(BF16))
            tails.append((fresh * (k_col * jnp.exp(closing - cum_col))).astype(BF16))
        for h in range(heads):
            closing = rows_of[n][h : h + 1, c - 1 : c]
            k_t = keyed[n * q_ref.shape[0] + h // group][7]
            states[h] = jnp.exp(closing) * states[h] + mxu(k_t, tails[h])
        for h in range(heads):
            qf, q_col = keyed[n * q_ref.shape[0] + h // group][0], keyed[n * q_ref.shape[0] + h // group][2]
            cum_col = columns_of[n][:, h : h + 1]
            query = (qf * (q_col * jnp.exp(cum_col))).astype(BF16)
            out = mxu(
                jnp.concatenate([query, mixings[n * heads + h]], axis=1),
                jnp.concatenate([bases[h], freshes[h]], axis=0),
            )
            r_ref[h, span] = out[:, :d].astype(BF16)
            o_ref[h, span] = out[:, d:].astype(BF16)
    for h in range(heads):
        state_ref[h] = states[h]

    @pl.when(step == pl.num_programs(0) - 1)
    def _():
        parts = msg_ref.shape[1]
        wide = d // parts
        for h in range(heads):
            state = state_ref[h]
            moved = state[:, :d].astype(msg_ref.dtype)
            added = jnp.transpose(state[:, d:], (1, 0)).astype(msg_ref.dtype)
            for p in range(parts):
                msg_ref[h, p, :d, :] = moved
                msg_ref[h, p, d:, :] = added[p * wide : (p + 1) * wide]


def local_delta(ds, q, k, v, parts):
    heads, seq, dv = v.shape
    kh, _, dk = q.shape
    wide = dv // parts
    rows = PER_STEP * CHUNK
    return pl.pallas_call(
        delta_kernel,
        grid=(seq // rows,),
        in_specs=[
            pl.BlockSpec((PER_STEP, 2 * heads, CHUNK), lambda i: (i, 0, 0)),
            pl.BlockSpec((kh, rows, dk), lambda i: (0, i, 0)),
            pl.BlockSpec((kh, rows, dk), lambda i: (0, i, 0)),
            pl.BlockSpec((heads, rows, dv), lambda i: (0, i, 0)),
        ],
        out_specs=[
            pl.BlockSpec((heads, rows, dk), lambda i: (0, i, 0)),
            pl.BlockSpec((heads, rows, dv), lambda i: (0, i, 0)),
            pl.BlockSpec((heads, parts, dk + wide, dk), lambda i: (0, 0, 0, 0)),
        ],
        out_shape=[
            pltpu.HBM((heads, seq, dk), BF16),
            pltpu.HBM((heads, seq, dv), BF16),
            jax.ShapeDtypeStruct((heads, parts, dk + wide, dk), BF16),
        ],
        scratch_shapes=[VMEM((heads, dk, dk + dv), F32)],
        compiler_params=pltpu.CompilerParams(
            dimension_semantics=("arbitrary",), vmem_limit_bytes=30 * MIB
        ),
        name="delta_local",
    )(ds, q, k, v)


def prefix_kernel(msg_ref, out_ref):
    count, tall, dk = msg_ref.shape
    wide = tall - dk
    state = jnp.zeros((wide, dk), F32)
    for i in range(count):
        out_ref[i] = state.astype(out_ref.dtype)
        if i < count - 1:
            both = jnp.concatenate(halves(state), axis=0)
            moved = mxu(both, msg_ref[i, :dk, :], ((1,), (1,)))
            state = moved[:wide] + moved[wide:] + msg_ref[i, dk:, :].astype(F32)


def prefix_states(msg, wide):
    count, tall, dk = msg.shape
    return pl.pallas_call(
        prefix_kernel,
        out_shape=jax.ShapeDtypeStruct((count, wide, dk), BF16),
        compiler_params=pltpu.CompilerParams(vmem_limit_bytes=16 * MIB),
        name="prefix_states",
    )(msg)


def gate_kernel(place_ref, r_ref, o_ref, s_ref, g_ref, gain_ref, keep_ref, give_ref):
    d = r_ref.shape[2]
    rows = keep_ref.shape[1]
    core = place_ref[0]
    for part, out_ref in ((core, keep_ref), (1 - core, give_ref)):
        span = pl.ds(pl.multiple_of(part * rows, rows), rows)
        for h in range(r_ref.shape[0]):
            value = o_ref[h, span, :].astype(F32) + mxu(r_ref[h, span, :], s_ref[h], ((1,), (1,)))
            scale = 1.0 / jnp.sqrt(jnp.mean(value * value, axis=1, keepdims=True) + 1e-06)
            gate = g_ref[h, span, :].astype(F32)
            silu = gate * lax.logistic(gate)
            out_ref[0, :, h * d : (h + 1) * d] = (value * scale * gain_ref[...] * silu).astype(BF16)


def gated_rows(place, r, o, states, gate, gain, toks):
    heads, seq, d = r.shape
    rows = 2 * toks
    by_rows = pl.BlockSpec((heads, rows, d), lambda i, p: (0, i, 0))
    out = pl.BlockSpec((1, toks, heads * d), lambda i, p: (i, 0, 0))
    shape = jax.ShapeDtypeStruct((seq // rows, toks, heads * d), BF16)
    return pl.pallas_call(
        gate_kernel,
        grid_spec=pltpu.PrefetchScalarGridSpec(
            num_scalar_prefetch=1,
            grid=(seq // rows,),
            in_specs=[
                by_rows,
                by_rows,
                pl.BlockSpec((heads, d, d), lambda i, p: (0, 0, 0)),
                by_rows,
                pl.BlockSpec((1, d), lambda i, p: (0, 0)),
            ],
            out_specs=[out, out],
        ),
        out_shape=[shape, shape],
        compiler_params=pltpu.CompilerParams(dimension_semantics=("arbitrary",), vmem_limit_bytes=56 * MIB),
        name="gated_rows",
    )(place, r, o, states, gate, gain)


def far_kernel(place_ref, mine_ref, got_ref, w_ref, v_ref, a_ref, b_ref):
    part = mxu(mine_ref[0], w_ref[...]) + mxu(got_ref[0], v_ref[...])
    half = a_ref.shape[0]
    a_ref[...] = part[:half].astype(BF16)
    b_ref[...] = part[half:].astype(BF16)


def near_kernel(place_ref, ahead_ref, ahead_got_ref, behind_ref, behind_got_ref, w_ref, v_ref, right_ref, left_ref):
    half = right_ref.shape[0]
    for row_ref, got_ref, first, out_ref in (
        (ahead_ref, ahead_got_ref, half, right_ref),
        (behind_ref, behind_got_ref, 0, left_ref),
    ):
        rows = pl.ds(first, half)
        out_ref[...] = (mxu(row_ref[0, rows, :], w_ref[...]) + mxu(got_ref[0, rows, :], v_ref[...])).astype(BF16)


def rest_kernel(
    place_ref, ahead_ref, ahead_got_ref, behind_ref, behind_got_ref, own_ref, own_got_ref, w_ref, v_ref, out_ref
):
    half = own_ref.shape[1] // 2
    rows = jnp.concatenate([ahead_ref[0, :half, :], behind_ref[0, half:, :], own_ref[0]], axis=0)
    got = jnp.concatenate([ahead_got_ref[0, :half, :], behind_got_ref[0, half:, :], own_got_ref[0]], axis=0)
    out_ref[...] = mxu(rows, w_ref[...]) + mxu(got, v_ref[...])


def project(kernel, steps, out_shape, name, place, mine, got, weight, other):
    count, toks, deep = mine.shape
    width = weight.shape[1]
    chunk = lambda step: pl.BlockSpec((1, toks, deep), lambda i, p: (lax.rem(p[1] + step, count), 0, 0))
    whole = lambda shape: pl.BlockSpec(shape, lambda i, p: (0, 0))
    return pl.pallas_call(
        kernel,
        grid_spec=pltpu.PrefetchScalarGridSpec(
            num_scalar_prefetch=1,
            grid=(1,),
            in_specs=[chunk(step) for step in steps for _ in range(2)] + [whole(weight.shape)] * 2,
            out_specs=[whole(shape.shape) for shape in out_shape],
        ),
        out_shape=out_shape,
        cost_estimate=pl.CostEstimate(
            flops=4 * len(steps) * toks * deep * width,
            bytes_accessed=4 * weight.size + 4 * len(steps) * toks * width,
            transcendentals=0,
        ),
        compiler_params=pltpu.CompilerParams(dimension_semantics=("arbitrary",), vmem_limit_bytes=24 * MIB),
        name=name,
    )(place, *([mine, got] * len(steps)), weight, other)


def relay_kernel(rest_ref, a_ref, b_ref, right_ref, left_ref):
    half = a_ref.shape[0]
    right_ref[...] = (rest_ref[:half] + a_ref[...].astype(F32)).astype(BF16)
    left_ref[...] = (rest_ref[half : 2 * half] + b_ref[...].astype(F32)).astype(BF16)


def relay(rest, first, second):
    shape = jax.ShapeDtypeStruct(first.shape, BF16)
    return pl.pallas_call(
        relay_kernel,
        out_shape=[shape, shape],
        compiler_params=pltpu.CompilerParams(vmem_limit_bytes=16 * MIB),
        name="relay",
    )(rest, first, second)


def slot_kernel(experts, ids_ref, out_ref):
    top, toks = ids_ref.shape
    expert = lax.broadcasted_iota(jnp.int32, (experts, toks), 0)
    hits = jnp.zeros((experts, toks), F32)
    for k in range(top):
        hits = hits + (expert == ids_ref[k : k + 1, :]).astype(F32)
    before = (
        lax.broadcasted_iota(jnp.int32, (toks, toks), 0) < lax.broadcasted_iota(jnp.int32, (toks, toks), 1)
    ).astype(BF16)
    earlier = mxu(hits.astype(BF16), before)
    for k in range(top):
        ids = ids_ref[k : k + 1, :]
        rank = jnp.sum(jnp.where(expert == ids, earlier, 0.0), axis=0, keepdims=True)
        out_ref[k : k + 1, :] = ids * CAP + rank.astype(jnp.int32)


def slots_of(ids, experts):
    return pl.pallas_call(
        functools.partial(slot_kernel, experts),
        out_shape=jax.ShapeDtypeStruct(ids.shape, jnp.int32),
        compiler_params=pltpu.CompilerParams(vmem_limit_bytes=16 * MIB),
        name="slots",
    )(ids)


def dispatch_kernel(rest_ref, a0_ref, a1_ref, b0_ref, b1_ref, res_ref, gain_ref, slot_ref, att_ref, send_ref, flat_ref):
    toks, width = res_ref.shape
    pieces = width // 128
    own = rest_ref[toks:]
    early = own[: toks // 2] + a0_ref[...].astype(F32) + a1_ref[...].astype(F32)
    late = own[toks // 2 :] + b0_ref[...].astype(F32) + b1_ref[...].astype(F32)
    total = jnp.concatenate([early, late], axis=0)
    attended = (res_ref[...].astype(F32) + total).astype(BF16)
    att_ref[...] = attended
    settled = attended.astype(F32)
    root = jnp.sqrt(jnp.mean(settled * settled, axis=1, keepdims=True) + 1e-06)
    normed = settled / root * gain_ref[...]
    for j in range(pieces):
        flat_ref[pl.ds(j, toks, stride=pieces), :] = normed[:, j * 128 : (j + 1) * 128]

    @pl.loop(0, toks)
    def _(t):
        tile = flat_ref[pl.ds(pl.multiple_of(t * pieces, pieces), pieces), :].astype(BF16)
        for k in range(slot_ref.shape[0]):
            send_ref[slot_ref[k, t]] = tile


def dispatch(rest, early, late, residual, gain, slots, count):
    toks, width = residual.shape
    pieces = width // 128
    whole = pl.BlockSpec(memory_space=VMEM)
    return pl.pallas_call(
        dispatch_kernel,
        in_specs=[whole] * 7 + [pl.BlockSpec(memory_space=pltpu.SMEM)],
        out_specs=[whole, whole],
        out_shape=[
            jax.ShapeDtypeStruct((toks, width), BF16),
            jax.ShapeDtypeStruct((count, pieces, 128), BF16),
        ],
        scratch_shapes=[VMEM((toks * pieces, 128), F32)],
        compiler_params=pltpu.CompilerParams(vmem_limit_bytes=24 * MIB),
        name="dispatch",
    )(rest, *early, *late, residual, gain, slots)


def expert_kernel(x_ref, wg_ref, wu_ref, wd_ref, out_ref, flat_ref):
    sources, _, tall, lanes = x_ref.shape
    pieces = wg_ref.shape[1] // lanes
    rows = flat_ref.shape[0] // PITCH
    tiles_ref = flat_ref.reshape(rows, PITCH, lanes)
    tiles_ref[:, :pieces, :] = x_ref[...].reshape(rows, pieces, lanes).astype(F32)
    x = jnp.concatenate(
        [flat_ref[pl.ds(j, rows, stride=PITCH), :].astype(BF16) for j in range(pieces)], axis=1
    )
    gate = mxu(x, wg_ref[0])
    up = mxu(x, wu_ref[0])
    inner = (gate * lax.logistic(gate) * up).astype(BF16)
    y = mxu(inner, wd_ref[0])
    for j in range(pieces):
        flat_ref[pl.ds(j, rows, stride=PITCH), :] = y[:, j * lanes : (j + 1) * lanes]
    out_ref[...] = tiles_ref[:, :pieces, :].astype(BF16).reshape(sources, 1, tall, lanes)


def run_experts(x, gate_proj, up_proj, down_proj):
    count, local, tall, lanes = x.shape
    sources = 64
    rows = sources * tall * lanes // gate_proj.shape[1]
    tokens = pl.BlockSpec((sources, 1, tall, lanes), lambda e, i: (i, e, 0, 0))
    return pl.pallas_call(
        expert_kernel,
        grid=(local, count // sources),
        in_specs=[
            tokens,
            pl.BlockSpec((1,) + gate_proj.shape[1:], lambda e, i: (e, 0, 0)),
            pl.BlockSpec((1,) + up_proj.shape[1:], lambda e, i: (e, 0, 0)),
            pl.BlockSpec((1,) + down_proj.shape[1:], lambda e, i: (e, 0, 0)),
        ],
        out_specs=tokens,
        out_shape=jax.ShapeDtypeStruct(x.shape, BF16),
        scratch_shapes=[VMEM((rows * PITCH, lanes), F32)],
        compiler_params=pltpu.CompilerParams(
            dimension_semantics=("arbitrary", "arbitrary"), vmem_limit_bytes=56 * MIB
        ),
        name="experts",
    )(x, gate_proj, up_proj, down_proj)


def combine_kernel(back_ref, slot_ref, gate_ref, out_ref, flat_ref):
    toks, width = out_ref.shape
    pieces = width // 128

    @pl.loop(0, toks)
    def _(t):
        total = jnp.zeros((pieces, 128), F32)
        for k in range(slot_ref.shape[0]):
            total = total + gate_ref[k, t] * back_ref[slot_ref[k, t]].astype(F32)
        flat_ref[pl.ds(pl.multiple_of(t * pieces, pieces), pieces), :] = total

    for j in range(pieces):
        out_ref[:, j * 128 : (j + 1) * 128] = flat_ref[pl.ds(j, toks, stride=pieces), :].astype(BF16)


def combine(back, slots, gates):
    count, pieces, lanes = back.shape
    toks = slots.shape[1]
    smem = pl.BlockSpec(memory_space=pltpu.SMEM)
    return pl.pallas_call(
        combine_kernel,
        in_specs=[pl.BlockSpec(memory_space=VMEM), smem, smem],
        out_specs=pl.BlockSpec(memory_space=VMEM),
        out_shape=jax.ShapeDtypeStruct((toks, pieces * lanes), BF16),
        scratch_shapes=[VMEM((toks * pieces, lanes), F32)],
        compiler_params=pltpu.CompilerParams(vmem_limit_bytes=24 * MIB),
        name="combine",
    )(back, slots, gates)


def shards(
    queries,
    key_vectors,
    values,
    out_gate,
    write_strength,
    decay_logarithm,
    residual,
    out_weight,
    head_gain,
    post_gain,
    gate_proj,
    up_proj,
    down_proj,
    expert_ids,
    route_gates,
):
    seq, heads, dv = values.shape
    dk = queries.shape[2]
    n_ctx = lax.axis_size("ctx")
    n_exp = lax.axis_size("exp")
    n_dev = n_ctx * n_exp
    parts = n_ctx // heads
    wide = dv // parts
    local_experts = gate_proj.shape[0]
    toks, width = residual.shape

    place = lax.axis_index("exp")
    place = jnp.stack([place & 1, place >> 1])
    shift = lambda a, by: lax.ppermute(a, "exp", [(i, (i + 2 * by) % n_exp) for i in range(n_exp)])
    swap = lambda a: lax.ppermute(a, "exp", [(i, i ^ 1) for i in range(n_exp)])
    other_weight = swap(out_weight)
    slots = slots_of(expert_ids.T, local_experts * n_dev)
    gates = route_gates.T

    by_head = lambda a: jnp.transpose(a, (1, 0, 2))
    ds = jnp.transpose(
        jnp.concatenate([decay_logarithm, write_strength], axis=0).reshape(2 * heads, seq // CHUNK, CHUNK),
        (1, 0, 2),
    )
    reads, local_out, msg = local_delta(ds, by_head(queries), by_head(key_vectors), by_head(values), parts)
    msg = lax.all_to_all(msg.reshape(n_ctx, dk + wide, dk), "ctx", 0, 0, tiled=True)
    states = lax.all_to_all(prefix_states(msg, wide), "ctx", 0, 0, tiled=True).reshape(heads, dv, dk)
    mine, give = gated_rows(
        place, reads, local_out, states, by_head(out_gate), head_gain.reshape(1, dv), toks
    )
    got = swap(give)
    half = jax.ShapeDtypeStruct((toks // 2, width), BF16)
    operands = (place, mine, got, out_weight, other_weight)
    first, second = project(far_kernel, (2,), [half, half], "project_far", *operands)
    first, second = shift(first, 1), shift(second, -1)
    ahead, behind = project(near_kernel, (1, n_exp // 2 - 1), [half, half], "project_near", *operands)
    ahead, behind = shift(ahead, 1), shift(behind, -1)
    [rest] = project(
        rest_kernel,
        (1, n_exp // 2 - 1, 0),
        [jax.ShapeDtypeStruct((2 * toks, width), F32)],
        "project_rest",
        *operands,
    )
    right, left = relay(rest, first, second)
    attended, send = dispatch(
        rest,
        (shift(right, 1), behind),
        (ahead, shift(left, -1)),
        residual,
        post_gain.reshape(1, width),
        slots,
        n_dev * local_experts * CAP,
    )
    tall = CAP * width // 128
    held = lax.all_to_all(
        send.reshape(n_dev, local_experts, tall, 128), ("ctx", "exp"), 0, 0, tiled=True
    )
    done = run_experts(held, gate_proj, up_proj, down_proj)
    back = lax.all_to_all(done, ("ctx", "exp"), 0, 0, tiled=True)
    mixture = combine(back.reshape(n_dev * local_experts * CAP, width // 128, 128), slots, gates)
    return (attended, mixture)


def solution(mesh):
    in_specs = (
        P("ctx", "exp", None),
        P("ctx", "exp", None),
        P("ctx", "exp", None),
        P("ctx", "exp", None),
        P("exp", "ctx"),
        P("exp", "ctx"),
        P(("ctx", "exp"), None),
        P("exp", None),
        P(),
        P(),
        P(("ctx", "exp"), None, None),
        P(("ctx", "exp"), None, None),
        P(("ctx", "exp"), None, None),
        P(("ctx", "exp"), None),
        P(("ctx", "exp"), None),
    )
    out_specs = (P(("ctx", "exp"), None), P(("ctx", "exp"), None))
    return jax.shard_map(shards, mesh=mesh, in_specs=in_specs, out_specs=out_specs, check_vma=False)
```

```python
import functools

import jax
import jax.numpy as jnp
from jax import lax
from jax.experimental import pallas as pl
from jax.experimental.pallas import tpu as pltpu
from jax.sharding import PartitionSpec as P

CHUNK = 128
PER_STEP = 4
CAP = 10
PITCH = 24
F32 = jnp.float32
BF16 = jnp.bfloat16
VMEM = pltpu.VMEM
MIB = 1024 * 1024


def mxu(a, b, dims=((1,), (0,))):
    return lax.dot_general(a, b, (dims, ((), ())), preferred_element_type=F32)


def halves(a):
    high = a.astype(BF16)
    return high, (a - high.astype(F32)).astype(BF16)


def product(a, b):
    width = b[0].shape[1]
    left = jnp.concatenate([a[0], a[1]], axis=1)
    right = jnp.concatenate(
        [
            jnp.concatenate([b[0], b[1]], axis=1),
            jnp.concatenate([b[0], jnp.zeros_like(b[0])], axis=1),
        ],
        axis=0,
    )
    both = mxu(left, right)
    return both[:, :width] + both[:, width:]


def unit_lower_inverses(lowers, row, col):
    eye = (row == col).astype(F32)
    near = row // 16 == col // 16
    diags = [jnp.where(near, low, 0.0) for low in lowers]
    inverses = [eye - diag for diag in diags]
    powers = [halves(-diag) for diag in diags]
    for step in range(3):
        powers = [halves(product(power, power)) for power in powers]
        inverses = [inv + product(halves(inv), power) for inv, power in zip(inverses, powers)]
    size = 16
    while size < row.shape[0]:
        pick = (row // (2 * size) == col // (2 * size)) & (row // size != col // size)
        belows = [jnp.where(pick, low, 0.0).astype(BF16) for low in lowers]
        invs = [inv.astype(BF16) for inv in inverses]
        crossed = [mxu(inv, below).astype(BF16) for inv, below in zip(invs, belows)]
        inverses = [full - mxu(cro, inv) for full, cro, inv in zip(inverses, crossed, invs)]
        size = size * 2
    return inverses


def delta_kernel(ds_ref, q_ref, k_ref, v_ref, r_ref, o_ref, msg_ref, state_ref):
    step = pl.program_id(0)
    heads = v_ref.shape[0]
    group = heads // q_ref.shape[0]
    d = q_ref.shape[2]
    c = CHUNK
    per_step = q_ref.shape[1] // c
    row = lax.broadcasted_iota(jnp.int32, (c, c), 0)
    col = lax.broadcasted_iota(jnp.int32, (c, c), 1)
    causal = row >= col
    strict = row > col

    @pl.when(step == 0)
    def _():
        eye = (row == col).astype(F32)
        for h in range(heads):
            state_ref[h] = jnp.concatenate([eye, jnp.zeros_like(eye)], axis=1)

    upto = (row <= col).astype(BF16)
    rows_of, columns_of = [], []
    for n in range(per_step):
        ds = ds_ref[n]
        d0 = ds.astype(BF16)
        rest = ds - d0.astype(F32)
        d1 = rest.astype(BF16)
        d2 = (rest - d1.astype(F32)).astype(BF16)
        cum = mxu(d0, upto) + mxu(d1, upto) + mxu(d2, upto)
        half = jnp.where(lax.broadcasted_iota(jnp.int32, ds.shape, 0) < heads, cum, ds)
        rows_of.append(half)
        columns_of.append(jnp.transpose(half, (1, 0)))

    keyed = []
    for n in range(per_step):
        span = pl.ds(n * c, c)
        for g in range(q_ref.shape[0]):
            q, k = q_ref[g, span], k_ref[g, span]
            qf, kf = q.astype(F32), k.astype(F32)
            q_col = (d ** -0.5) / jnp.sqrt(jnp.sum(qf * qf, axis=1, keepdims=True) + 1e-06)
            k_col = 1.0 / jnp.sqrt(jnp.sum(kf * kf, axis=1, keepdims=True) + 1e-06)
            gram = mxu(k, k, ((1,), (1,)))
            k_row = 1.0 / jnp.sqrt(jnp.sum(jnp.where(row == col, gram, 0.0), axis=0, keepdims=True) + 1e-06)
            gram = gram * (k_col * k_row)
            cross = mxu(q, k, ((1,), (1,))) * (q_col * k_row)
            keyed.append((qf, k, q_col, k_col, k_row, gram, cross, jnp.transpose(kf, (1, 0)).astype(BF16)))

    lowers, mixings = [], []
    for n in range(per_step):
        for h in range(heads):
            gram, cross = keyed[n * q_ref.shape[0] + h // group][5:7]
            cum_col, beta_col = columns_of[n][:, h : h + 1], columns_of[n][:, heads + h : heads + h + 1]
            cum_row = rows_of[n][h : h + 1, :]
            spread = jnp.where(causal, jnp.exp(jnp.where(causal, cum_col - cum_row, 0.0)), 0.0)
            lowers.append(jnp.where(strict, beta_col * gram * spread, 0.0))
            mixings.append((cross * spread).astype(BF16))
    inverses = unit_lower_inverses(lowers, row, col)
    weights, writes = [], []
    for n in range(per_step):
        for h in range(heads):
            k, k_row = keyed[n * q_ref.shape[0] + h // group][1], keyed[n * q_ref.shape[0] + h // group][4]
            cum_row, beta_row = rows_of[n][h : h + 1, :], rows_of[n][heads + h : heads + h + 1, :]
            inverse = inverses[n * heads + h]
            t_k = halves(inverse * (beta_row * jnp.exp(cum_row) * k_row))
            t_v = halves(inverse * beta_row)
            v = v_ref[h, pl.ds(n * c, c)]
            weights.append(
                mxu(jnp.concatenate(t_k, axis=1), jnp.concatenate([k, k], axis=0)).astype(BF16)
            )
            writes.append(mxu(jnp.concatenate(t_v, axis=1), jnp.concatenate([v, v], axis=0)))

    states = [state_ref[h] for h in range(heads)]
    for n in range(per_step):
        span = pl.ds(n * c, c)
        bases = [state.astype(BF16) for state in states]
        reads = [mxu(weights[n * heads + h], bases[h]) for h in range(heads)]
        freshes, tails = [], []
        for h in range(heads):
            k_col = keyed[n * q_ref.shape[0] + h // group][3]
            cum_col = columns_of[n][:, h : h + 1]
            closing = rows_of[n][h : h + 1, c - 1 : c]
            written = writes[n * heads + h]
            fresh = jnp.concatenate([-reads[h][:, :d], written - reads[h][:, d:]], axis=1)
            freshes.append(fresh.astype(BF16))
            tails.append((fresh * (k_col * jnp.exp(closing - cum_col))).astype(BF16))
        for h in range(heads):
            closing = rows_of[n][h : h + 1, c - 1 : c]
            k_t = keyed[n * q_ref.shape[0] + h // group][7]
            states[h] = jnp.exp(closing) * states[h] + mxu(k_t, tails[h])
        for h in range(heads):
            qf, q_col = keyed[n * q_ref.shape[0] + h // group][0], keyed[n * q_ref.shape[0] + h // group][2]
            cum_col = columns_of[n][:, h : h + 1]
            query = (qf * (q_col * jnp.exp(cum_col))).astype(BF16)
            out = mxu(
                jnp.concatenate([query, mixings[n * heads + h]], axis=1),
                jnp.concatenate([bases[h], freshes[h]], axis=0),
            )
            r_ref[h, span] = out[:, :d].astype(BF16)
            o_ref[h, span] = out[:, d:].astype(BF16)
    for h in range(heads):
        state_ref[h] = states[h]

    @pl.when(step == pl.num_programs(0) - 1)
    def _():
        parts = msg_ref.shape[1]
        wide = d // parts
        for h in range(heads):
            state = state_ref[h]
            moved = state[:, :d].astype(msg_ref.dtype)
            added = jnp.transpose(state[:, d:], (1, 0)).astype(msg_ref.dtype)
            for p in range(parts):
                msg_ref[h, p, :d, :] = moved
                msg_ref[h, p, d:, :] = added[p * wide : (p + 1) * wide]


def local_delta(ds, q, k, v, parts):
    heads, seq, dv = v.shape
    kh, _, dk = q.shape
    wide = dv // parts
    rows = PER_STEP * CHUNK
    return pl.pallas_call(
        delta_kernel,
        grid=(seq // rows,),
        in_specs=[
            pl.BlockSpec((PER_STEP, 2 * heads, CHUNK), lambda i: (i, 0, 0)),
            pl.BlockSpec((kh, rows, dk), lambda i: (0, i, 0)),
            pl.BlockSpec((kh, rows, dk), lambda i: (0, i, 0)),
            pl.BlockSpec((heads, rows, dv), lambda i: (0, i, 0)),
        ],
        out_specs=[
            pl.BlockSpec((heads, rows, dk), lambda i: (0, i, 0)),
            pl.BlockSpec((heads, rows, dv), lambda i: (0, i, 0)),
            pl.BlockSpec((heads, parts, dk + wide, dk), lambda i: (0, 0, 0, 0)),
        ],
        out_shape=[
            pltpu.HBM((heads, seq, dk), BF16),
            pltpu.HBM((heads, seq, dv), BF16),
            jax.ShapeDtypeStruct((heads, parts, dk + wide, dk), BF16),
        ],
        scratch_shapes=[VMEM((heads, dk, dk + dv), F32)],
        compiler_params=pltpu.CompilerParams(
            dimension_semantics=("arbitrary",), vmem_limit_bytes=30 * MIB
        ),
        name="delta_local",
    )(ds, q, k, v)


def prefix_kernel(msg_ref, out_ref):
    count, tall, dk = msg_ref.shape
    wide = tall - dk
    state = jnp.zeros((wide, dk), F32)
    for i in range(count):
        out_ref[i] = state.astype(out_ref.dtype)
        if i < count - 1:
            both = jnp.concatenate(halves(state), axis=0)
            moved = mxu(both, msg_ref[i, :dk, :], ((1,), (1,)))
            state = moved[:wide] + moved[wide:] + msg_ref[i, dk:, :].astype(F32)


def prefix_states(msg, wide):
    count, tall, dk = msg.shape
    return pl.pallas_call(
        prefix_kernel,
        out_shape=jax.ShapeDtypeStruct((count, wide, dk), BF16),
        compiler_params=pltpu.CompilerParams(vmem_limit_bytes=16 * MIB),
        name="prefix_states",
    )(msg)


def gate_kernel(r_ref, o_ref, s_ref, g_ref, gain_ref, keep_ref, give_ref):
    heads, _, d = r_ref.shape
    rows = keep_ref.shape[1]
    core = lax.axis_index("exp") & 1
    spans = [pl.ds(pl.multiple_of(part * rows, rows), rows) for part in (core, 1 - core)]
    each = [(span, h) for span in spans for h in range(heads)]
    reads = [mxu(r_ref[h, span, :], s_ref[h], ((1,), (1,))) for span, h in each]
    silus = []
    for span, h in each:
        gate = g_ref[h, span, :].astype(F32)
        silus.append(gate * lax.logistic(gate) * gain_ref[...])
    values = [o_ref[h, span, :].astype(F32) + read for (span, h), read in zip(each, reads)]
    scales = [1.0 / jnp.sqrt(jnp.mean(value * value, axis=1, keepdims=True) + 1e-06) for value in values]
    for n, (value, scale, silu) in enumerate(zip(values, scales, silus)):
        out_ref, h = (keep_ref, give_ref)[n // heads], n % heads
        out_ref[0, :, h * d : (h + 1) * d] = (value * scale * silu).astype(BF16)


def gated_rows(r, o, states, gate, gain, toks):
    heads, seq, d = r.shape
    rows = 2 * toks
    by_rows = pl.BlockSpec((heads, rows, d), lambda i: (0, i, 0))
    out = pl.BlockSpec((1, toks, heads * d), lambda i: (i, 0, 0))
    shape = jax.ShapeDtypeStruct((seq // rows, toks, heads * d), BF16)
    return pl.pallas_call(
        gate_kernel,
        grid=(seq // rows,),
        in_specs=[
            by_rows,
            by_rows,
            pl.BlockSpec((heads, d, d), lambda i: (0, 0, 0)),
            by_rows,
            pl.BlockSpec((1, d), lambda i: (0, 0)),
        ],
        out_specs=[out, out],
        out_shape=[shape, shape],
        compiler_params=pltpu.CompilerParams(dimension_semantics=("arbitrary",), vmem_limit_bytes=56 * MIB),
        name="gated_rows",
    )(r, o, states, gate, gain)


def chunk_at(step, mine_ref, got_ref):
    place = lax.rem((lax.axis_index("exp") >> 1) + step, mine_ref.shape[0])
    return jnp.concatenate([mine_ref[place], got_ref[place]], axis=1)


def far_kernel(mine_ref, got_ref, w_ref, v_ref, a_ref, b_ref):
    rows = chunk_at(2, mine_ref, got_ref)
    deep, half = w_ref.shape[0], a_ref.shape[0]
    part = mxu(rows[:, :deep], w_ref[...]) + mxu(rows[:, deep:], v_ref[...])
    a_ref[...] = part[:half].astype(BF16)
    b_ref[...] = part[half:].astype(BF16)


def near_kernel(mine_ref, got_ref, w_ref, v_ref, right_ref, left_ref, held_ref):
    half = right_ref.shape[0]
    deep = w_ref.shape[0]
    rows = jnp.concatenate(
        [chunk_at(1, mine_ref, got_ref), chunk_at(mine_ref.shape[0] - 1, mine_ref, got_ref)], axis=0
    )
    part = mxu(rows[:, :deep], w_ref[...]) + mxu(rows[:, deep:], v_ref[...])
    held_ref[:half] = part[:half]
    right_ref[...] = part[half : 2 * half].astype(BF16)
    left_ref[...] = part[2 * half : 3 * half].astype(BF16)
    held_ref[half:] = part[3 * half :]


def own_kernel(mine_ref, got_ref, w_ref, v_ref, out_ref):
    rows = chunk_at(0, mine_ref, got_ref)
    deep = w_ref.shape[0]
    out_ref[...] = mxu(rows[:, :deep], w_ref[...]) + mxu(rows[:, deep:], v_ref[...])


def project(kernel, chunks, out_shape, name, mine, got, weight, other):
    count, toks, deep = mine.shape
    width = weight.shape[1]
    whole = pl.BlockSpec(memory_space=VMEM)
    return pl.pallas_call(
        kernel,
        in_specs=[whole] * 4,
        out_specs=[whole] * len(out_shape),
        out_shape=out_shape,
        cost_estimate=pl.CostEstimate(
            flops=4 * chunks * toks * deep * width,
            bytes_accessed=4 * weight.size + 4 * chunks * toks * width,
            transcendentals=0,
        ),
        compiler_params=pltpu.CompilerParams(vmem_limit_bytes=24 * MIB),
        name=name,
    )(mine, got, weight, other)


def relay_kernel(held_ref, a_ref, b_ref, right_ref, left_ref):
    half = a_ref.shape[0]
    right_ref[...] = (held_ref[:half] + a_ref[...].astype(F32)).astype(BF16)
    left_ref[...] = (held_ref[half:] + b_ref[...].astype(F32)).astype(BF16)


def relay(held, first, second):
    shape = jax.ShapeDtypeStruct(first.shape, BF16)
    return pl.pallas_call(
        relay_kernel,
        out_shape=[shape, shape],
        compiler_params=pltpu.CompilerParams(vmem_limit_bytes=16 * MIB),
        name="relay",
    )(held, first, second)


def slot_kernel(experts, ids_ref, out_ref):
    top, toks = ids_ref.shape
    expert = lax.broadcasted_iota(jnp.int32, (experts, toks), 0)
    hits = jnp.zeros((experts, toks), F32)
    for k in range(top):
        hits = hits + (expert == ids_ref[k : k + 1, :]).astype(F32)
    before = (
        lax.broadcasted_iota(jnp.int32, (toks, toks), 0) < lax.broadcasted_iota(jnp.int32, (toks, toks), 1)
    ).astype(BF16)
    earlier = mxu(hits.astype(BF16), before)
    for k in range(top):
        ids = ids_ref[k : k + 1, :]
        rank = jnp.sum(jnp.where(expert == ids, earlier, 0.0), axis=0, keepdims=True)
        out_ref[k : k + 1, :] = ids * CAP + rank.astype(jnp.int32)


def slots_of(ids, experts):
    return pl.pallas_call(
        functools.partial(slot_kernel, experts),
        out_shape=jax.ShapeDtypeStruct(ids.shape, jnp.int32),
        compiler_params=pltpu.CompilerParams(vmem_limit_bytes=16 * MIB),
        name="slots",
    )(ids)


def dispatch_kernel(own_ref, a0_ref, a1_ref, b0_ref, b1_ref, res_ref, gain_ref, slot_ref, att_ref, send_ref, flat_ref):
    toks, width = res_ref.shape
    pieces = width // 128
    own = own_ref[...]
    early = own[: toks // 2] + a0_ref[...].astype(F32) + a1_ref[...].astype(F32)
    late = own[toks // 2 :] + b0_ref[...].astype(F32) + b1_ref[...].astype(F32)
    total = jnp.concatenate([early, late], axis=0)
    attended = (res_ref[...].astype(F32) + total).astype(BF16)
    att_ref[...] = attended
    settled = attended.astype(F32)
    root = jnp.sqrt(jnp.mean(settled * settled, axis=1, keepdims=True) + 1e-06)
    normed = settled / root * gain_ref[...]
    for j in range(pieces):
        flat_ref[pl.ds(j, toks, stride=PITCH), :] = normed[:, j * 128 : (j + 1) * 128]

    @pl.loop(0, toks, unroll=4)
    def _(t):
        tile = flat_ref[pl.ds(pl.multiple_of(t * PITCH, 8), pieces), :].astype(BF16)
        for k in range(slot_ref.shape[0]):
            send_ref[slot_ref[k, t]] = tile


def dispatch(own, early, late, residual, gain, slots, count):
    toks, width = residual.shape
    pieces = width // 128
    whole = pl.BlockSpec(memory_space=VMEM)
    return pl.pallas_call(
        dispatch_kernel,
        in_specs=[whole] * 7 + [pl.BlockSpec(memory_space=pltpu.SMEM)],
        out_specs=[whole, whole],
        out_shape=[
            jax.ShapeDtypeStruct((toks, width), BF16),
            jax.ShapeDtypeStruct((count, pieces, 128), BF16),
        ],
        scratch_shapes=[VMEM((toks * PITCH, 128), F32)],
        compiler_params=pltpu.CompilerParams(vmem_limit_bytes=24 * MIB),
        name="dispatch",
    )(own, *early, *late, residual, gain, slots)


def expert_kernel(x_ref, wg_ref, wu_ref, wd_ref, out_ref, flat_ref):
    sources, _, tall, lanes = x_ref.shape
    pieces = wg_ref.shape[1] // lanes
    rows = flat_ref.shape[0] // PITCH
    tiles_ref = flat_ref.reshape(rows, PITCH, lanes)
    tiles_ref[:, :pieces, :] = x_ref[...].reshape(rows, pieces, lanes).astype(F32)
    x = jnp.concatenate(
        [flat_ref[pl.ds(j, rows, stride=PITCH), :].astype(BF16) for j in range(pieces)], axis=1
    )
    gate = mxu(x, wg_ref[0])
    up = mxu(x, wu_ref[0])
    inner = (gate * lax.logistic(gate) * up).astype(BF16)
    y = mxu(inner, wd_ref[0])
    for j in range(pieces):
        flat_ref[pl.ds(j, rows, stride=PITCH), :] = y[:, j * lanes : (j + 1) * lanes]
    out_ref[...] = tiles_ref[:, :pieces, :].astype(BF16).reshape(sources, 1, tall, lanes)


def run_experts(x, gate_proj, up_proj, down_proj):
    count, local, tall, lanes = x.shape
    sources = 64
    rows = sources * tall * lanes // gate_proj.shape[1]
    tokens = pl.BlockSpec((sources, 1, tall, lanes), lambda e, i: (i, e, 0, 0))
    return pl.pallas_call(
        expert_kernel,
        grid=(local, count // sources),
        in_specs=[
            tokens,
            pl.BlockSpec((1,) + gate_proj.shape[1:], lambda e, i: (e, 0, 0)),
            pl.BlockSpec((1,) + up_proj.shape[1:], lambda e, i: (e, 0, 0)),
            pl.BlockSpec((1,) + down_proj.shape[1:], lambda e, i: (e, 0, 0)),
        ],
        out_specs=tokens,
        out_shape=jax.ShapeDtypeStruct(x.shape, BF16),
        scratch_shapes=[VMEM((rows * PITCH, lanes), F32)],
        compiler_params=pltpu.CompilerParams(
            dimension_semantics=("arbitrary", "arbitrary"), vmem_limit_bytes=56 * MIB
        ),
        name="experts",
    )(x, gate_proj, up_proj, down_proj)


def combine_kernel(back_ref, slot_ref, gate_ref, out_ref, flat_ref):
    toks, width = out_ref.shape
    pieces = width // 128

    @pl.loop(0, toks, unroll=4)
    def _(t):
        total = jnp.zeros((pieces, 128), F32)
        for k in range(slot_ref.shape[0]):
            total = total + gate_ref[k, t] * back_ref[slot_ref[k, t]].astype(F32)
        flat_ref[pl.ds(pl.multiple_of(t * PITCH, 8), pieces), :] = total

    for j in range(pieces):
        out_ref[:, j * 128 : (j + 1) * 128] = flat_ref[pl.ds(j, toks, stride=PITCH), :].astype(BF16)


def combine(back, slots, gates):
    count, pieces, lanes = back.shape
    toks = slots.shape[1]
    smem = pl.BlockSpec(memory_space=pltpu.SMEM)
    return pl.pallas_call(
        combine_kernel,
        in_specs=[pl.BlockSpec(memory_space=VMEM), smem, smem],
        out_specs=pl.BlockSpec(memory_space=VMEM),
        out_shape=jax.ShapeDtypeStruct((toks, pieces * lanes), BF16),
        scratch_shapes=[VMEM((toks * PITCH, lanes), F32)],
        compiler_params=pltpu.CompilerParams(vmem_limit_bytes=24 * MIB),
        name="combine",
    )(back, slots, gates)


def shards(
    queries,
    key_vectors,
    values,
    out_gate,
    write_strength,
    decay_logarithm,
    residual,
    out_weight,
    head_gain,
    post_gain,
    gate_proj,
    up_proj,
    down_proj,
    expert_ids,
    route_gates,
):
    seq, heads, dv = values.shape
    dk = queries.shape[2]
    n_ctx = lax.axis_size("ctx")
    n_exp = lax.axis_size("exp")
    n_dev = n_ctx * n_exp
    parts = n_ctx // heads
    wide = dv // parts
    local_experts = gate_proj.shape[0]
    toks, width = residual.shape

    shift = lambda a, by: lax.ppermute(a, "exp", [(i, (i + 2 * by) % n_exp) for i in range(n_exp)])
    swap = lambda a: lax.ppermute(a, "exp", [(i, i ^ 1) for i in range(n_exp)])
    other_weight = swap(out_weight)
    slots = slots_of(expert_ids.T, local_experts * n_dev)
    gates = route_gates.T

    by_head = lambda a: jnp.transpose(a, (1, 0, 2))
    ds = jnp.transpose(
        jnp.concatenate([decay_logarithm, write_strength], axis=0).reshape(2 * heads, seq // CHUNK, CHUNK),
        (1, 0, 2),
    )
    reads, local_out, msg = local_delta(ds, by_head(queries), by_head(key_vectors), by_head(values), parts)
    msg = lax.all_to_all(msg.reshape(n_ctx, dk + wide, dk), "ctx", 0, 0, tiled=True)
    states = lax.all_to_all(prefix_states(msg, wide), "ctx", 0, 0, tiled=True).reshape(heads, dv, dk)
    mine, give = gated_rows(
        reads, local_out, states, by_head(out_gate), head_gain.reshape(1, dv), toks
    )
    got = swap(give)
    half = jax.ShapeDtypeStruct((toks // 2, width), BF16)
    operands = (mine, got, out_weight, other_weight)
    first, second = project(far_kernel, 1, [half, half], "project_far", *operands)
    first, second = shift(first, 1), shift(second, -1)
    total = jax.ShapeDtypeStruct((toks, width), F32)
    ahead, behind, held = project(near_kernel, 2, [half, half, total], "project_near", *operands)
    ahead, behind = shift(ahead, 1), shift(behind, -1)
    right, left = relay(held, first, second)
    [own] = project(own_kernel, 1, [total], "project_own", *operands)
    attended, send = dispatch(
        own,
        (shift(right, 1), behind),
        (ahead, shift(left, -1)),
        residual,
        post_gain.reshape(1, width),
        slots,
        n_dev * local_experts * CAP,
    )
    tall = CAP * width // 128
    held = lax.all_to_all(
        send.reshape(n_dev, local_experts, tall, 128), ("ctx", "exp"), 0, 0, tiled=True
    )
    done = run_experts(held, gate_proj, up_proj, down_proj)
    back = lax.all_to_all(done, ("ctx", "exp"), 0, 0, tiled=True)
    mixture = combine(back.reshape(n_dev * local_experts * CAP, width // 128, 128), slots, gates)
    return (attended, mixture)


def solution(mesh):
    in_specs = (
        P("ctx", "exp", None),
        P("ctx", "exp", None),
        P("ctx", "exp", None),
        P("ctx", "exp", None),
        P("exp", "ctx"),
        P("exp", "ctx"),
        P(("ctx", "exp"), None),
        P("exp", None),
        P(),
        P(),
        P(("ctx", "exp"), None, None),
        P(("ctx", "exp"), None, None),
        P(("ctx", "exp"), None, None),
        P(("ctx", "exp"), None),
        P(("ctx", "exp"), None),
    )
    out_specs = (P(("ctx", "exp"), None), P(("ctx", "exp"), None))
    return jax.shard_map(shards, mesh=mesh, in_specs=in_specs, out_specs=out_specs, check_vma=False)
```

```python
import functools

import jax
import jax.numpy as jnp
from jax import lax
from jax.experimental import pallas as pl
from jax.experimental.pallas import tpu as pltpu
from jax.sharding import PartitionSpec as P

CHUNK = 128
PER_STEP = 4
CAP = 10
PITCH = 24
F32 = jnp.float32
BF16 = jnp.bfloat16
VMEM = pltpu.VMEM
MIB = 1024 * 1024


def mxu(a, b, dims=((1,), (0,))):
    return lax.dot_general(a, b, (dims, ((), ())), preferred_element_type=F32)


def halves(a):
    high = a.astype(BF16)
    return high, (a - high.astype(F32)).astype(BF16)


def product(a, b):
    width = b[0].shape[1]
    left = jnp.concatenate([a[0], a[1]], axis=1)
    right = jnp.concatenate(
        [
            jnp.concatenate([b[0], b[1]], axis=1),
            jnp.concatenate([b[0], jnp.zeros_like(b[0])], axis=1),
        ],
        axis=0,
    )
    both = mxu(left, right)
    return both[:, :width] + both[:, width:]


def unit_lower_inverses(lowers, row, col):
    eye = (row == col).astype(F32)
    near = row // 16 == col // 16
    diags = [jnp.where(near, low, 0.0) for low in lowers]
    inverses = [eye - diag for diag in diags]
    powers = [halves(-diag) for diag in diags]
    for step in range(3):
        powers = [halves(product(power, power)) for power in powers]
        inverses = [inv + product(halves(inv), power) for inv, power in zip(inverses, powers)]
    size = 16
    while size < row.shape[0]:
        pick = (row // (2 * size) == col // (2 * size)) & (row // size != col // size)
        belows = [jnp.where(pick, low, 0.0).astype(BF16) for low in lowers]
        invs = [inv.astype(BF16) for inv in inverses]
        crossed = [mxu(inv, below).astype(BF16) for inv, below in zip(invs, belows)]
        inverses = [full - mxu(cro, inv) for full, cro, inv in zip(inverses, crossed, invs)]
        size = size * 2
    return inverses


def delta_kernel(decay_ref, beta_ref, q_ref, k_ref, v_ref, r_ref, o_ref, msg_ref, state_ref):
    step = pl.program_id(0)
    heads = v_ref.shape[0]
    group = heads // q_ref.shape[0]
    d = q_ref.shape[2]
    c = CHUNK
    per_step = q_ref.shape[1] // c
    row = lax.broadcasted_iota(jnp.int32, (c, c), 0)
    col = lax.broadcasted_iota(jnp.int32, (c, c), 1)
    causal = row >= col
    strict = row > col

    @pl.when(step == 0)
    def _():
        eye = (row == col).astype(F32)
        for h in range(heads):
            state_ref[h] = jnp.concatenate([eye, jnp.zeros_like(eye)], axis=1)

    upto = (row <= col).astype(BF16)
    rows_of, columns_of = [], []
    for n in range(per_step):
        ds = jnp.concatenate([a[:, n * c : (n + 1) * c] for a in (decay_ref, beta_ref)], axis=0)
        d0 = ds.astype(BF16)
        rest = ds - d0.astype(F32)
        d1 = rest.astype(BF16)
        d2 = (rest - d1.astype(F32)).astype(BF16)
        cum = mxu(d0, upto) + mxu(d1, upto) + mxu(d2, upto)
        half = jnp.where(lax.broadcasted_iota(jnp.int32, ds.shape, 0) < heads, cum, ds)
        rows_of.append(half)
        columns_of.append(jnp.transpose(half, (1, 0)))

    keyed = []
    for n in range(per_step):
        span = pl.ds(n * c, c)
        for g in range(q_ref.shape[0]):
            q, k = q_ref[g, span], k_ref[g, span]
            qf, kf = q.astype(F32), k.astype(F32)
            q_col = (d ** -0.5) / jnp.sqrt(jnp.sum(qf * qf, axis=1, keepdims=True) + 1e-06)
            k_col = 1.0 / jnp.sqrt(jnp.sum(kf * kf, axis=1, keepdims=True) + 1e-06)
            gram = mxu(k, k, ((1,), (1,)))
            k_row = 1.0 / jnp.sqrt(jnp.sum(jnp.where(row == col, gram, 0.0), axis=0, keepdims=True) + 1e-06)
            gram = gram * (k_col * k_row)
            cross = mxu(q, k, ((1,), (1,))) * (q_col * k_row)
            keyed.append((qf, k, q_col, k_col, k_row, gram, cross, jnp.transpose(kf, (1, 0)).astype(BF16)))

    lowers, mixings = [], []
    for n in range(per_step):
        for h in range(heads):
            gram, cross = keyed[n * q_ref.shape[0] + h // group][5:7]
            cum_col, beta_col = columns_of[n][:, h : h + 1], columns_of[n][:, heads + h : heads + h + 1]
            cum_row = rows_of[n][h : h + 1, :]
            spread = jnp.where(causal, jnp.exp(jnp.where(causal, cum_col - cum_row, 0.0)), 0.0)
            lowers.append(jnp.where(strict, beta_col * gram * spread, 0.0))
            mixings.append((cross * spread).astype(BF16))
    inverses = unit_lower_inverses(lowers, row, col)
    weights, writes = [], []
    for n in range(per_step):
        for h in range(heads):
            k, k_row = keyed[n * q_ref.shape[0] + h // group][1], keyed[n * q_ref.shape[0] + h // group][4]
            cum_row, beta_row = rows_of[n][h : h + 1, :], rows_of[n][heads + h : heads + h + 1, :]
            inverse = inverses[n * heads + h]
            t_k = halves(inverse * (beta_row * jnp.exp(cum_row) * k_row))
            t_v = halves(inverse * beta_row)
            v = v_ref[h, pl.ds(n * c, c)]
            weights.append(
                mxu(jnp.concatenate(t_k, axis=1), jnp.concatenate([k, k], axis=0)).astype(BF16)
            )
            writes.append(mxu(jnp.concatenate(t_v, axis=1), jnp.concatenate([v, v], axis=0)))

    states = [state_ref[h] for h in range(heads)]
    for n in range(per_step):
        span = pl.ds(n * c, c)
        bases = [state.astype(BF16) for state in states]
        reads = [mxu(weights[n * heads + h], bases[h]) for h in range(heads)]
        freshes, tails = [], []
        for h in range(heads):
            k_col = keyed[n * q_ref.shape[0] + h // group][3]
            cum_col = columns_of[n][:, h : h + 1]
            closing = rows_of[n][h : h + 1, c - 1 : c]
            written = writes[n * heads + h]
            fresh = jnp.concatenate([-reads[h][:, :d], written - reads[h][:, d:]], axis=1)
            freshes.append(fresh.astype(BF16))
            tails.append((fresh * (k_col * jnp.exp(closing - cum_col))).astype(BF16))
        for h in range(heads):
            closing = rows_of[n][h : h + 1, c - 1 : c]
            k_t = keyed[n * q_ref.shape[0] + h // group][7]
            states[h] = jnp.exp(closing) * states[h] + mxu(k_t, tails[h])
        for h in range(heads):
            qf, q_col = keyed[n * q_ref.shape[0] + h // group][0], keyed[n * q_ref.shape[0] + h // group][2]
            cum_col = columns_of[n][:, h : h + 1]
            query = (qf * (q_col * jnp.exp(cum_col))).astype(BF16)
            out = mxu(
                jnp.concatenate([query, mixings[n * heads + h]], axis=1),
                jnp.concatenate([bases[h], freshes[h]], axis=0),
            )
            r_ref[h, span] = out[:, :d].astype(BF16)
            o_ref[h, span] = out[:, d:].astype(BF16)
    for h in range(heads):
        state_ref[h] = states[h]

    @pl.when(step == pl.num_programs(0) - 1)
    def _():
        parts = msg_ref.shape[1]
        wide = d // parts
        for h in range(heads):
            state = state_ref[h]
            moved = state[:, :d].astype(msg_ref.dtype)
            added = jnp.transpose(state[:, d:], (1, 0)).astype(msg_ref.dtype)
            for p in range(parts):
                msg_ref[h, p, :d, :] = moved
                msg_ref[h, p, d:, :] = added[p * wide : (p + 1) * wide]


def local_delta(decay, beta, q, k, v, parts):
    heads, seq, dv = v.shape
    kh, _, dk = q.shape
    wide = dv // parts
    rows = PER_STEP * CHUNK
    return pl.pallas_call(
        delta_kernel,
        grid=(seq // rows,),
        in_specs=[
            pl.BlockSpec((heads, rows), lambda i: (0, i)),
            pl.BlockSpec((heads, rows), lambda i: (0, i)),
            pl.BlockSpec((kh, rows, dk), lambda i: (0, i, 0)),
            pl.BlockSpec((kh, rows, dk), lambda i: (0, i, 0)),
            pl.BlockSpec((heads, rows, dv), lambda i: (0, i, 0)),
        ],
        out_specs=[
            pl.BlockSpec((heads, rows, dk), lambda i: (0, i, 0)),
            pl.BlockSpec((heads, rows, dv), lambda i: (0, i, 0)),
            pl.BlockSpec((heads, parts, dk + wide, dk), lambda i: (0, 0, 0, 0)),
        ],
        out_shape=[
            pltpu.HBM((heads, seq, dk), BF16),
            pltpu.HBM((heads, seq, dv), BF16),
            jax.ShapeDtypeStruct((heads, parts, dk + wide, dk), BF16),
        ],
        scratch_shapes=[VMEM((heads, dk, dk + dv), F32)],
        compiler_params=pltpu.CompilerParams(
            dimension_semantics=("arbitrary",), vmem_limit_bytes=30 * MIB
        ),
        name="delta_local",
    )(decay, beta, q, k, v)


def prefix_kernel(msg_ref, out_ref):
    count, tall, dk = msg_ref.shape
    wide = tall - dk
    state = jnp.zeros((wide, dk), F32)
    for i in range(count):
        out_ref[i] = state.astype(out_ref.dtype)
        if i < count - 1:
            both = jnp.concatenate(halves(state), axis=0)
            moved = mxu(both, msg_ref[i, :dk, :], ((1,), (1,)))
            state = moved[:wide] + moved[wide:] + msg_ref[i, dk:, :].astype(F32)


def prefix_states(msg, wide):
    count, tall, dk = msg.shape
    return pl.pallas_call(
        prefix_kernel,
        out_shape=jax.ShapeDtypeStruct((count, wide, dk), BF16),
        compiler_params=pltpu.CompilerParams(vmem_limit_bytes=16 * MIB),
        name="prefix_states",
    )(msg)


def gate_kernel(r_ref, o_ref, s_ref, g_ref, gain_ref, keep_ref, give_ref):
    heads, _, d = r_ref.shape
    rows = keep_ref.shape[1]
    core = lax.axis_index("exp") & 1
    spans = [pl.ds(pl.multiple_of(part * rows, rows), rows) for part in (core, 1 - core)]
    each = [(span, h) for span in spans for h in range(heads)]
    reads = [mxu(r_ref[h, span, :], s_ref[h], ((1,), (1,))) for span, h in each]
    silus = []
    for span, h in each:
        gate = g_ref[h, span, :].astype(F32)
        silus.append(gate * lax.logistic(gate) * gain_ref[...])
    values = [o_ref[h, span, :].astype(F32) + read for (span, h), read in zip(each, reads)]
    scales = [1.0 / jnp.sqrt(jnp.mean(value * value, axis=1, keepdims=True) + 1e-06) for value in values]
    for n, (value, scale, silu) in enumerate(zip(values, scales, silus)):
        out_ref, h = (keep_ref, give_ref)[n // heads], n % heads
        out_ref[0, :, h * d : (h + 1) * d] = (value * scale * silu).astype(BF16)


def gated_rows(r, o, states, gate, gain, toks):
    heads, seq, d = r.shape
    rows = 2 * toks
    by_rows = pl.BlockSpec((heads, rows, d), lambda i: (0, i, 0))
    out = pl.BlockSpec((1, toks, heads * d), lambda i: (i, 0, 0))
    shape = jax.ShapeDtypeStruct((seq // rows, toks, heads * d), BF16)
    return pl.pallas_call(
        gate_kernel,
        grid=(seq // rows,),
        in_specs=[
            by_rows,
            by_rows,
            pl.BlockSpec((heads, d, d), lambda i: (0, 0, 0)),
            by_rows,
            pl.BlockSpec((1, d), lambda i: (0, 0)),
        ],
        out_specs=[out, out],
        out_shape=[shape, shape],
        compiler_params=pltpu.CompilerParams(dimension_semantics=("arbitrary",), vmem_limit_bytes=44 * MIB),
        name="gated_rows",
    )(r, o, states, gate, gain)


def chunk_at(step, mine_ref, got_ref):
    place = lax.rem((lax.axis_index("exp") >> 1) + step, mine_ref.shape[0])
    return jnp.concatenate([mine_ref[place], got_ref[place]], axis=1)


def far_kernel(mine_ref, got_ref, w_ref, v_ref, a_ref, b_ref):
    rows = chunk_at(2, mine_ref, got_ref)
    deep, half = w_ref.shape[0], a_ref.shape[0]
    part = mxu(rows[:, :deep], w_ref[...]) + mxu(rows[:, deep:], v_ref[...])
    a_ref[...] = part[:half].astype(BF16)
    b_ref[...] = part[half:].astype(BF16)


def near_kernel(mine_ref, got_ref, w_ref, v_ref, right_ref, left_ref, held_ref):
    half = right_ref.shape[0]
    deep = w_ref.shape[0]
    rows = jnp.concatenate(
        [chunk_at(1, mine_ref, got_ref), chunk_at(mine_ref.shape[0] - 1, mine_ref, got_ref)], axis=0
    )
    part = mxu(rows[:, :deep], w_ref[...]) + mxu(rows[:, deep:], v_ref[...])
    held_ref[:half] = part[:half]
    right_ref[...] = part[half : 2 * half].astype(BF16)
    left_ref[...] = part[2 * half : 3 * half].astype(BF16)
    held_ref[half:] = part[3 * half :]


def own_kernel(mine_ref, got_ref, w_ref, v_ref, out_ref):
    rows = chunk_at(0, mine_ref, got_ref)
    deep = w_ref.shape[0]
    out_ref[...] = mxu(rows[:, :deep], w_ref[...]) + mxu(rows[:, deep:], v_ref[...])


def project(kernel, chunks, out_shape, name, mine, got, weight, other):
    count, toks, deep = mine.shape
    width = weight.shape[1]
    whole = pl.BlockSpec(memory_space=VMEM)
    return pl.pallas_call(
        kernel,
        in_specs=[whole] * 4,
        out_specs=[whole] * len(out_shape),
        out_shape=out_shape,
        cost_estimate=pl.CostEstimate(
            flops=4 * chunks * toks * deep * width,
            bytes_accessed=4 * weight.size + 4 * chunks * toks * width,
            transcendentals=0,
        ),
        compiler_params=pltpu.CompilerParams(vmem_limit_bytes=24 * MIB),
        name=name,
    )(mine, got, weight, other)


def relay_kernel(held_ref, a_ref, b_ref, right_ref, left_ref):
    half = a_ref.shape[0]
    right_ref[...] = (held_ref[:half] + a_ref[...].astype(F32)).astype(BF16)
    left_ref[...] = (held_ref[half:] + b_ref[...].astype(F32)).astype(BF16)


def relay(held, first, second):
    shape = jax.ShapeDtypeStruct(first.shape, BF16)
    return pl.pallas_call(
        relay_kernel,
        out_shape=[shape, shape],
        compiler_params=pltpu.CompilerParams(vmem_limit_bytes=16 * MIB),
        name="relay",
    )(held, first, second)


def slot_kernel(experts, ids_ref, out_ref):
    top, toks = ids_ref.shape
    expert = lax.broadcasted_iota(jnp.int32, (experts, toks), 0)
    hits = jnp.zeros((experts, toks), F32)
    for k in range(top):
        hits = hits + (expert == ids_ref[k : k + 1, :]).astype(F32)
    before = (
        lax.broadcasted_iota(jnp.int32, (toks, toks), 0) < lax.broadcasted_iota(jnp.int32, (toks, toks), 1)
    ).astype(BF16)
    earlier = mxu(hits.astype(BF16), before)
    for k in range(top):
        ids = ids_ref[k : k + 1, :]
        rank = jnp.sum(jnp.where(expert == ids, earlier, 0.0), axis=0, keepdims=True)
        out_ref[k : k + 1, :] = ids * CAP + rank.astype(jnp.int32)


def slots_of(ids, experts):
    return pl.pallas_call(
        functools.partial(slot_kernel, experts),
        out_shape=jax.ShapeDtypeStruct(ids.shape, jnp.int32),
        compiler_params=pltpu.CompilerParams(vmem_limit_bytes=16 * MIB),
        name="slots",
    )(ids)


def dispatch_kernel(own_ref, a0_ref, a1_ref, b0_ref, b1_ref, res_ref, gain_ref, slot_ref, att_ref, send_ref, flat_ref):
    toks, width = res_ref.shape
    pieces = width // 128
    own = own_ref[...]
    early = own[: toks // 2] + a0_ref[...].astype(F32) + a1_ref[...].astype(F32)
    late = own[toks // 2 :] + b0_ref[...].astype(F32) + b1_ref[...].astype(F32)
    total = jnp.concatenate([early, late], axis=0)
    attended = (res_ref[...].astype(F32) + total).astype(BF16)
    att_ref[...] = attended
    settled = attended.astype(F32)
    root = jnp.sqrt(jnp.mean(settled * settled, axis=1, keepdims=True) + 1e-06)
    normed = settled / root * gain_ref[...]
    for j in range(pieces):
        flat_ref[pl.ds(j, toks, stride=PITCH), :] = normed[:, j * 128 : (j + 1) * 128]

    @pl.loop(0, toks, unroll=4)
    def _(t):
        tile = flat_ref[pl.ds(pl.multiple_of(t * PITCH, 8), pieces), :].astype(BF16)
        for k in range(slot_ref.shape[0]):
            send_ref[slot_ref[k, t]] = tile


def dispatch(own, early, late, residual, gain, slots, count):
    toks, width = residual.shape
    pieces = width // 128
    whole = pl.BlockSpec(memory_space=VMEM)
    return pl.pallas_call(
        dispatch_kernel,
        in_specs=[whole] * 7 + [pl.BlockSpec(memory_space=pltpu.SMEM)],
        out_specs=[whole, whole],
        out_shape=[
            jax.ShapeDtypeStruct((toks, width), BF16),
            jax.ShapeDtypeStruct((count, pieces, 128), BF16),
        ],
        scratch_shapes=[VMEM((toks * PITCH, 128), F32)],
        compiler_params=pltpu.CompilerParams(vmem_limit_bytes=24 * MIB),
        name="dispatch",
    )(own, *early, *late, residual, gain, slots)


def expert_kernel(x_ref, wg_ref, wu_ref, wd_ref, out_ref, flat_ref):
    sources, _, tall, lanes = x_ref.shape
    pieces = wg_ref.shape[1] // lanes
    rows = flat_ref.shape[0] // PITCH
    tiles_ref = flat_ref.reshape(rows, PITCH, lanes)
    tiles_ref[:, :pieces, :] = x_ref[...].reshape(rows, pieces, lanes).astype(F32)
    x = jnp.concatenate(
        [flat_ref[pl.ds(j, rows, stride=PITCH), :].astype(BF16) for j in range(pieces)], axis=1
    )
    e = pl.program_id(0)
    gate = mxu(x, wg_ref[e])
    up = mxu(x, wu_ref[e])
    inner = (gate * lax.logistic(gate) * up).astype(BF16)
    y = mxu(inner, wd_ref[e])
    for j in range(pieces):
        flat_ref[pl.ds(j, rows, stride=PITCH), :] = y[:, j * lanes : (j + 1) * lanes]
    out_ref[...] = tiles_ref[:, :pieces, :].astype(BF16).reshape(sources, 1, tall, lanes)


def run_experts(x, gate_proj, up_proj, down_proj):
    count, local, tall, lanes = x.shape
    sources = 64
    rows = sources * tall * lanes // gate_proj.shape[1]
    tokens = pl.BlockSpec((sources, 1, tall, lanes), lambda e, i: (i, e, 0, 0))
    return pl.pallas_call(
        expert_kernel,
        grid=(local, count // sources),
        in_specs=[
            tokens,
            pl.BlockSpec(memory_space=VMEM),
            pl.BlockSpec(memory_space=VMEM),
            pl.BlockSpec(memory_space=VMEM),
        ],
        out_specs=tokens,
        out_shape=jax.ShapeDtypeStruct(x.shape, BF16),
        scratch_shapes=[VMEM((rows * PITCH, lanes), F32)],
        compiler_params=pltpu.CompilerParams(
            dimension_semantics=("arbitrary", "arbitrary"), vmem_limit_bytes=36 * MIB
        ),
        name="experts",
    )(x, gate_proj, up_proj, down_proj)


def combine_kernel(back_ref, slot_ref, gate_ref, out_ref, flat_ref):
    toks, width = out_ref.shape
    pieces = width // 128

    @pl.loop(0, toks, unroll=4)
    def _(t):
        total = jnp.zeros((pieces, 128), F32)
        for k in range(slot_ref.shape[0]):
            total = total + gate_ref[k, t] * back_ref[slot_ref[k, t]].astype(F32)
        flat_ref[pl.ds(pl.multiple_of(t * PITCH, 8), pieces), :] = total

    for j in range(pieces):
        out_ref[:, j * 128 : (j + 1) * 128] = flat_ref[pl.ds(j, toks, stride=PITCH), :].astype(BF16)


def combine(back, slots, gates):
    count, pieces, lanes = back.shape
    toks = slots.shape[1]
    smem = pl.BlockSpec(memory_space=pltpu.SMEM)
    return pl.pallas_call(
        combine_kernel,
        in_specs=[pl.BlockSpec(memory_space=VMEM), smem, smem],
        out_specs=pl.BlockSpec(memory_space=VMEM),
        out_shape=jax.ShapeDtypeStruct((toks, pieces * lanes), BF16),
        scratch_shapes=[VMEM((toks * PITCH, lanes), F32)],
        compiler_params=pltpu.CompilerParams(vmem_limit_bytes=24 * MIB),
        name="combine",
    )(back, slots, gates)


def shards(
    queries,
    key_vectors,
    values,
    out_gate,
    write_strength,
    decay_logarithm,
    residual,
    out_weight,
    head_gain,
    post_gain,
    gate_proj,
    up_proj,
    down_proj,
    expert_ids,
    route_gates,
):
    seq, heads, dv = values.shape
    dk = queries.shape[2]
    n_ctx = lax.axis_size("ctx")
    n_exp = lax.axis_size("exp")
    n_dev = n_ctx * n_exp
    parts = n_ctx // heads
    wide = dv // parts
    local_experts = gate_proj.shape[0]
    toks, width = residual.shape

    shift = lambda a, by: lax.ppermute(a, "exp", [(i, (i + 2 * by) % n_exp) for i in range(n_exp)])
    swap = lambda a: lax.ppermute(a, "exp", [(i, i ^ 1) for i in range(n_exp)])
    other_weight = swap(out_weight)
    slots = slots_of(expert_ids.T, local_experts * n_dev)
    gates = route_gates.T

    by_head = lambda a: jnp.transpose(a, (1, 0, 2))
    reads, local_out, msg = local_delta(
        decay_logarithm, write_strength, by_head(queries), by_head(key_vectors), by_head(values), parts)
    msg = lax.all_to_all(msg.reshape(n_ctx, dk + wide, dk), "ctx", 0, 0, tiled=True)
    states = lax.all_to_all(prefix_states(msg, wide), "ctx", 0, 0, tiled=True).reshape(heads, dv, dk)
    mine, give = gated_rows(
        reads, local_out, states, by_head(out_gate), head_gain.reshape(1, dv), toks
    )
    got = swap(give)
    half = jax.ShapeDtypeStruct((toks // 2, width), BF16)
    operands = (mine, got, out_weight, other_weight)
    first, second = project(far_kernel, 1, [half, half], "project_far", *operands)
    first, second = shift(first, 1), shift(second, -1)
    total = jax.ShapeDtypeStruct((toks, width), F32)
    ahead, behind, held = project(near_kernel, 2, [half, half, total], "project_near", *operands)
    ahead, behind = shift(ahead, 1), shift(behind, -1)
    right, left = relay(held, first, second)
    [own] = project(own_kernel, 1, [total], "project_own", *operands)
    attended, send = dispatch(
        own,
        (shift(right, 1), behind),
        (ahead, shift(left, -1)),
        residual,
        post_gain.reshape(1, width),
        slots,
        n_dev * local_experts * CAP,
    )
    tall = CAP * width // 128
    held = lax.all_to_all(
        send.reshape(n_dev, local_experts, tall, 128), ("ctx", "exp"), 0, 0, tiled=True
    )
    done = run_experts(held, gate_proj, up_proj, down_proj)
    back = lax.all_to_all(done, ("ctx", "exp"), 0, 0, tiled=True)
    mixture = combine(back.reshape(n_dev * local_experts * CAP, width // 128, 128), slots, gates)
    return (attended, mixture)


def solution(mesh):
    in_specs = (
        P("ctx", "exp", None),
        P("ctx", "exp", None),
        P("ctx", "exp", None),
        P("ctx", "exp", None),
        P("exp", "ctx"),
        P("exp", "ctx"),
        P(("ctx", "exp"), None),
        P("exp", None),
        P(),
        P(),
        P(("ctx", "exp"), None, None),
        P(("ctx", "exp"), None, None),
        P(("ctx", "exp"), None, None),
        P(("ctx", "exp"), None),
        P(("ctx", "exp"), None),
    )
    out_specs = (P(("ctx", "exp"), None), P(("ctx", "exp"), None))
    return jax.shard_map(shards, mesh=mesh, in_specs=in_specs, out_specs=out_specs, check_vma=False)
```

```python
import functools

import jax
import jax.numpy as jnp
from jax import lax
from jax.experimental import pallas as pl
from jax.experimental.pallas import tpu as pltpu
from jax.sharding import PartitionSpec as P

CHUNK = 128
PER_STEP = 4
CAP = 10
PITCH = 24
F32 = jnp.float32
BF16 = jnp.bfloat16
VMEM = pltpu.VMEM
MIB = 1024 * 1024


def mxu(a, b, dims=((1,), (0,))):
    return lax.dot_general(a, b, (dims, ((), ())), preferred_element_type=F32)


def halves(a):
    high = a.astype(BF16)
    return high, (a - high.astype(F32)).astype(BF16)


def product(a, b):
    width = b[0].shape[1]
    left = jnp.concatenate([a[0], a[1]], axis=1)
    right = jnp.concatenate(
        [
            jnp.concatenate([b[0], b[1]], axis=1),
            jnp.concatenate([b[0], jnp.zeros_like(b[0])], axis=1),
        ],
        axis=0,
    )
    both = mxu(left, right)
    return both[:, :width] + both[:, width:]


def unit_lower_inverses(lowers, row, col):
    eye = (row == col).astype(F32)
    near = row // 16 == col // 16
    diags = [jnp.where(near, low, 0.0) for low in lowers]
    inverses = [eye - diag for diag in diags]
    powers = [halves(-diag) for diag in diags]
    for step in range(3):
        powers = [halves(product(power, power)) for power in powers]
        inverses = [inv + product(halves(inv), power) for inv, power in zip(inverses, powers)]
    size = 16
    while size < row.shape[0]:
        pick = (row // (2 * size) == col // (2 * size)) & (row // size != col // size)
        belows = [jnp.where(pick, low, 0.0).astype(BF16) for low in lowers]
        invs = [inv.astype(BF16) for inv in inverses]
        crossed = [mxu(inv, below).astype(BF16) for inv, below in zip(invs, belows)]
        inverses = [full - mxu(cro, inv) for full, cro, inv in zip(inverses, crossed, invs)]
        size = size * 2
    return inverses


def delta_kernel(decay_ref, beta_ref, q_ref, k_ref, v_ref, out_ref, msg_ref, state_ref):
    step = pl.program_id(0)
    heads = v_ref.shape[0]
    group = heads // q_ref.shape[0]
    d = q_ref.shape[2]
    c = CHUNK
    per_step = q_ref.shape[1] // c
    row = lax.broadcasted_iota(jnp.int32, (c, c), 0)
    col = lax.broadcasted_iota(jnp.int32, (c, c), 1)
    causal = row >= col
    strict = row > col

    @pl.when(step == 0)
    def _():
        eye = (row == col).astype(F32)
        for h in range(heads):
            state_ref[h] = jnp.concatenate([eye, jnp.zeros_like(eye)], axis=1)

    upto = (row <= col).astype(BF16)
    rows_of, columns_of = [], []
    for n in range(per_step):
        ds = jnp.concatenate([a[:, n * c : (n + 1) * c] for a in (decay_ref, beta_ref)], axis=0)
        d0 = ds.astype(BF16)
        rest = ds - d0.astype(F32)
        d1 = rest.astype(BF16)
        d2 = (rest - d1.astype(F32)).astype(BF16)
        cum = mxu(d0, upto) + mxu(d1, upto) + mxu(d2, upto)
        half = jnp.where(lax.broadcasted_iota(jnp.int32, ds.shape, 0) < heads, cum, ds)
        rows_of.append(half)
        columns_of.append(jnp.transpose(half, (1, 0)))

    keyed = []
    for n in range(per_step):
        span = pl.ds(n * c, c)
        for g in range(q_ref.shape[0]):
            q, k = q_ref[g, span], k_ref[g, span]
            qf, kf = q.astype(F32), k.astype(F32)
            q_col = (d ** -0.5) / jnp.sqrt(jnp.sum(qf * qf, axis=1, keepdims=True) + 1e-06)
            k_col = 1.0 / jnp.sqrt(jnp.sum(kf * kf, axis=1, keepdims=True) + 1e-06)
            gram = mxu(k, k, ((1,), (1,)))
            k_row = 1.0 / jnp.sqrt(jnp.sum(jnp.where(row == col, gram, 0.0), axis=0, keepdims=True) + 1e-06)
            gram = gram * (k_col * k_row)
            cross = mxu(q, k, ((1,), (1,))) * (q_col * k_row)
            keyed.append((qf, k, q_col, k_col, k_row, gram, cross, jnp.transpose(kf, (1, 0)).astype(BF16)))

    lowers, mixings = [], []
    for n in range(per_step):
        for h in range(heads):
            gram, cross = keyed[n * q_ref.shape[0] + h // group][5:7]
            cum_col, beta_col = columns_of[n][:, h : h + 1], columns_of[n][:, heads + h : heads + h + 1]
            cum_row = rows_of[n][h : h + 1, :]
            spread = jnp.where(causal, jnp.exp(jnp.where(causal, cum_col - cum_row, 0.0)), 0.0)
            lowers.append(jnp.where(strict, beta_col * gram * spread, 0.0))
            mixings.append((cross * spread).astype(BF16))
    inverses = unit_lower_inverses(lowers, row, col)
    weights, writes = [], []
    for n in range(per_step):
        for h in range(heads):
            k, k_row = keyed[n * q_ref.shape[0] + h // group][1], keyed[n * q_ref.shape[0] + h // group][4]
            cum_row, beta_row = rows_of[n][h : h + 1, :], rows_of[n][heads + h : heads + h + 1, :]
            inverse = inverses[n * heads + h]
            t_k = halves(inverse * (beta_row * jnp.exp(cum_row) * k_row))
            t_v = halves(inverse * beta_row)
            v = v_ref[h, pl.ds(n * c, c)]
            weights.append(
                mxu(jnp.concatenate(t_k, axis=1), jnp.concatenate([k, k], axis=0)).astype(BF16)
            )
            writes.append(mxu(jnp.concatenate(t_v, axis=1), jnp.concatenate([v, v], axis=0)))

    states = [state_ref[h] for h in range(heads)]
    for n in range(per_step):
        span = pl.ds(n * c, c)
        bases = [state.astype(BF16) for state in states]
        reads = [mxu(weights[n * heads + h], bases[h]) for h in range(heads)]
        freshes, tails = [], []
        for h in range(heads):
            k_col = keyed[n * q_ref.shape[0] + h // group][3]
            cum_col = columns_of[n][:, h : h + 1]
            closing = rows_of[n][h : h + 1, c - 1 : c]
            written = writes[n * heads + h]
            fresh = jnp.concatenate([-reads[h][:, :d], written - reads[h][:, d:]], axis=1)
            freshes.append(fresh.astype(BF16))
            tails.append((fresh * (k_col * jnp.exp(closing - cum_col))).astype(BF16))
        for h in range(heads):
            closing = rows_of[n][h : h + 1, c - 1 : c]
            k_t = keyed[n * q_ref.shape[0] + h // group][7]
            states[h] = jnp.exp(closing) * states[h] + mxu(k_t, tails[h])
        for h in range(heads):
            qf, q_col = keyed[n * q_ref.shape[0] + h // group][0], keyed[n * q_ref.shape[0] + h // group][2]
            cum_col = columns_of[n][:, h : h + 1]
            query = (qf * (q_col * jnp.exp(cum_col))).astype(BF16)
            out = mxu(
                jnp.concatenate([query, mixings[n * heads + h]], axis=1),
                jnp.concatenate([bases[h], freshes[h]], axis=0),
            )
            out_ref[h, span] = out.astype(BF16)
    for h in range(heads):
        state_ref[h] = states[h]

    @pl.when(step == pl.num_programs(0) - 1)
    def _():
        parts = msg_ref.shape[1]
        wide = d // parts
        for h in range(heads):
            state = state_ref[h]
            moved = state[:, :d].astype(msg_ref.dtype)
            added = jnp.transpose(state[:, d:], (1, 0)).astype(msg_ref.dtype)
            for p in range(parts):
                msg_ref[h, p, :d, :] = moved
                msg_ref[h, p, d:, :] = added[p * wide : (p + 1) * wide]


def local_delta(decay, beta, q, k, v, parts):
    heads, seq, dv = v.shape
    kh, _, dk = q.shape
    wide = dv // parts
    rows = PER_STEP * CHUNK
    return pl.pallas_call(
        delta_kernel,
        grid=(seq // rows,),
        in_specs=[
            pl.BlockSpec((heads, rows), lambda i: (0, i)),
            pl.BlockSpec((heads, rows), lambda i: (0, i)),
            pl.BlockSpec((kh, rows, dk), lambda i: (0, i, 0)),
            pl.BlockSpec((kh, rows, dk), lambda i: (0, i, 0)),
            pl.BlockSpec((heads, rows, dv), lambda i: (0, i, 0)),
        ],
        out_specs=[
            pl.BlockSpec((heads, rows, dk + dv), lambda i: (0, i, 0)),
            pl.BlockSpec((heads, parts, dk + wide, dk), lambda i: (0, 0, 0, 0)),
        ],
        out_shape=[
            pltpu.HBM((heads, seq, dk + dv), BF16),
            jax.ShapeDtypeStruct((heads, parts, dk + wide, dk), BF16),
        ],
        scratch_shapes=[VMEM((heads, dk, dk + dv), F32)],
        compiler_params=pltpu.CompilerParams(
            dimension_semantics=("arbitrary",), vmem_limit_bytes=30 * MIB
        ),
        name="delta_local",
    )(decay, beta, q, k, v)


def prefix_kernel(msg_ref, out_ref):
    count, tall, dk = msg_ref.shape
    wide = tall - dk
    state = jnp.zeros((wide, dk), F32)
    for i in range(count):
        out_ref[i] = state.astype(out_ref.dtype)
        if i < count - 1:
            both = jnp.concatenate(halves(state), axis=0)
            moved = mxu(both, msg_ref[i, :dk, :], ((1,), (1,)))
            state = moved[:wide] + moved[wide:] + msg_ref[i, dk:, :].astype(F32)


def prefix_states(msg, wide):
    count, tall, dk = msg.shape
    return pl.pallas_call(
        prefix_kernel,
        out_shape=jax.ShapeDtypeStruct((count, wide, dk), BF16),
        compiler_params=pltpu.CompilerParams(vmem_limit_bytes=16 * MIB),
        name="prefix_states",
    )(msg)


def gate_kernel(other, ro_ref, s_ref, g_ref, gain_ref, out_ref):
    heads, d, _ = s_ref.shape
    chunks, rows, _ = out_ref.shape
    part = (lax.axis_index("exp") & 1) ^ other
    for i in range(chunks):
        span = pl.ds(pl.multiple_of((2 * i + part) * rows, rows), rows)
        both = [ro_ref[h, span, :] for h in range(heads)]
        reads = [mxu(both[h][:, :d], s_ref[h], ((1,), (1,))) for h in range(heads)]
        gates = [g_ref[h, span, :].astype(F32) for h in range(heads)]
        silus = [gate * lax.logistic(gate) * gain_ref[...] for gate in gates]
        values = [both[h][:, d:].astype(F32) + reads[h] for h in range(heads)]
        scales = [1.0 / jnp.sqrt(jnp.mean(value * value, axis=1, keepdims=True) + 1e-06) for value in values]
        for h in range(heads):
            out_ref[i, :, h * d : (h + 1) * d] = (values[h] * scales[h] * silus[h]).astype(BF16)


def gated_rows(other, ro, states, gate, gain, toks):
    heads, seq, d = gate.shape
    whole = pl.BlockSpec(memory_space=VMEM)
    half = heads * seq * d // 2
    return pl.pallas_call(
        functools.partial(gate_kernel, other),
        in_specs=[whole] * 4,
        out_specs=whole,
        out_shape=jax.ShapeDtypeStruct((seq // (2 * toks), toks, heads * d), BF16),
        cost_estimate=pl.CostEstimate(flops=2 * half * d, bytes_accessed=8 * half, transcendentals=half),
        compiler_params=pltpu.CompilerParams(vmem_limit_bytes=24 * MIB),
        name="gated_other" if other else "gated_own",
    )(ro, states, gate, gain)


def chunk_at(step, mine_ref, got_ref):
    place = lax.rem((lax.axis_index("exp") >> 1) + step, mine_ref.shape[0])
    return jnp.concatenate([mine_ref[place], got_ref[place]], axis=1)


def far_kernel(mine_ref, got_ref, w_ref, v_ref, a_ref, b_ref):
    rows = chunk_at(2, mine_ref, got_ref)
    deep, half = w_ref.shape[0], a_ref.shape[0]
    part = mxu(rows[:, :deep], w_ref[...]) + mxu(rows[:, deep:], v_ref[...])
    a_ref[...] = part[:half].astype(BF16)
    b_ref[...] = part[half:].astype(BF16)


def near_kernel(mine_ref, got_ref, w_ref, v_ref, right_ref, left_ref, held_ref):
    half = right_ref.shape[0]
    deep = w_ref.shape[0]
    rows = jnp.concatenate(
        [chunk_at(1, mine_ref, got_ref), chunk_at(mine_ref.shape[0] - 1, mine_ref, got_ref)], axis=0
    )
    part = mxu(rows[:, :deep], w_ref[...]) + mxu(rows[:, deep:], v_ref[...])
    held_ref[:half] = part[:half]
    right_ref[...] = part[half : 2 * half].astype(BF16)
    left_ref[...] = part[2 * half : 3 * half].astype(BF16)
    held_ref[half:] = part[3 * half :]


def own_kernel(mine_ref, got_ref, w_ref, v_ref, out_ref):
    rows = chunk_at(0, mine_ref, got_ref)
    deep = w_ref.shape[0]
    out_ref[...] = mxu(rows[:, :deep], w_ref[...]) + mxu(rows[:, deep:], v_ref[...])


def project(kernel, chunks, out_shape, name, mine, got, weight, other):
    count, toks, deep = mine.shape
    width = weight.shape[1]
    whole = pl.BlockSpec(memory_space=VMEM)
    return pl.pallas_call(
        kernel,
        in_specs=[whole] * 4,
        out_specs=[whole] * len(out_shape),
        out_shape=out_shape,
        cost_estimate=pl.CostEstimate(
            flops=4 * chunks * toks * deep * width,
            bytes_accessed=4 * weight.size + 4 * chunks * toks * width,
            transcendentals=0,
        ),
        compiler_params=pltpu.CompilerParams(vmem_limit_bytes=24 * MIB),
        name=name,
    )(mine, got, weight, other)


def relay_kernel(held_ref, a_ref, b_ref, right_ref, left_ref):
    half = a_ref.shape[0]
    right_ref[...] = (held_ref[:half] + a_ref[...].astype(F32)).astype(BF16)
    left_ref[...] = (held_ref[half:] + b_ref[...].astype(F32)).astype(BF16)


def relay(held, first, second):
    shape = jax.ShapeDtypeStruct(first.shape, BF16)
    return pl.pallas_call(
        relay_kernel,
        out_shape=[shape, shape],
        compiler_params=pltpu.CompilerParams(vmem_limit_bytes=16 * MIB),
        name="relay",
    )(held, first, second)


def slot_kernel(experts, ids_ref, out_ref):
    top, toks = ids_ref.shape
    expert = lax.broadcasted_iota(jnp.int32, (experts, toks), 0)
    hits = jnp.zeros((experts, toks), F32)
    for k in range(top):
        hits = hits + (expert == ids_ref[k : k + 1, :]).astype(F32)
    before = (
        lax.broadcasted_iota(jnp.int32, (toks, toks), 0) < lax.broadcasted_iota(jnp.int32, (toks, toks), 1)
    ).astype(BF16)
    earlier = mxu(hits.astype(BF16), before)
    for k in range(top):
        ids = ids_ref[k : k + 1, :]
        rank = jnp.sum(jnp.where(expert == ids, earlier, 0.0), axis=0, keepdims=True)
        out_ref[k : k + 1, :] = ids * CAP + rank.astype(jnp.int32)


def slots_of(ids, experts):
    return pl.pallas_call(
        functools.partial(slot_kernel, experts),
        out_shape=jax.ShapeDtypeStruct(ids.shape, jnp.int32),
        compiler_params=pltpu.CompilerParams(vmem_limit_bytes=16 * MIB),
        name="slots",
    )(ids)


def dispatch_kernel(own_ref, a0_ref, a1_ref, b0_ref, b1_ref, res_ref, gain_ref, slot_ref, att_ref, send_ref, flat_ref):
    toks, width = res_ref.shape
    pieces = width // 128
    own = own_ref[...]
    early = own[: toks // 2] + a0_ref[...].astype(F32) + a1_ref[...].astype(F32)
    late = own[toks // 2 :] + b0_ref[...].astype(F32) + b1_ref[...].astype(F32)
    total = jnp.concatenate([early, late], axis=0)
    attended = (res_ref[...].astype(F32) + total).astype(BF16)
    att_ref[...] = attended
    settled = attended.astype(F32)
    root = jnp.sqrt(jnp.mean(settled * settled, axis=1, keepdims=True) + 1e-06)
    normed = settled / root * gain_ref[...]
    for j in range(pieces):
        flat_ref[pl.ds(j, toks, stride=PITCH), :] = normed[:, j * 128 : (j + 1) * 128]

    @pl.loop(0, toks, unroll=4)
    def _(t):
        tile = flat_ref[pl.ds(pl.multiple_of(t * PITCH, 8), pieces), :].astype(BF16)
        for k in range(slot_ref.shape[0]):
            send_ref[slot_ref[k, t]] = tile


def dispatch(own, early, late, residual, gain, slots, count):
    toks, width = residual.shape
    pieces = width // 128
    whole = pl.BlockSpec(memory_space=VMEM)
    return pl.pallas_call(
        dispatch_kernel,
        in_specs=[whole] * 7 + [pl.BlockSpec(memory_space=pltpu.SMEM)],
        out_specs=[whole, whole],
        out_shape=[
            jax.ShapeDtypeStruct((toks, width), BF16),
            jax.ShapeDtypeStruct((count, pieces, 128), BF16),
        ],
        scratch_shapes=[VMEM((toks * PITCH, 128), F32)],
        compiler_params=pltpu.CompilerParams(vmem_limit_bytes=24 * MIB),
        name="dispatch",
    )(own, *early, *late, residual, gain, slots)


def expert_kernel(x_ref, wg_ref, wu_ref, wd_ref, out_ref, flat_ref):
    sources, _, tall, lanes = x_ref.shape
    pieces = wg_ref.shape[1] // lanes
    rows = flat_ref.shape[0] // PITCH
    tiles_ref = flat_ref.reshape(rows, PITCH, lanes)
    tiles_ref[:, :pieces, :] = x_ref[...].reshape(rows, pieces, lanes).astype(F32)
    x = jnp.concatenate(
        [flat_ref[pl.ds(j, rows, stride=PITCH), :].astype(BF16) for j in range(pieces)], axis=1
    )
    e = pl.program_id(0)
    gate = mxu(x, wg_ref[e])
    up = mxu(x, wu_ref[e])
    inner = (gate * lax.logistic(gate) * up).astype(BF16)
    y = mxu(inner, wd_ref[e])
    for j in range(pieces):
        flat_ref[pl.ds(j, rows, stride=PITCH), :] = y[:, j * lanes : (j + 1) * lanes]
    out_ref[...] = tiles_ref[:, :pieces, :].astype(BF16).reshape(sources, 1, tall, lanes)


def run_experts(x, gate_proj, up_proj, down_proj):
    count, local, tall, lanes = x.shape
    sources = 64
    rows = sources * tall * lanes // gate_proj.shape[1]
    tokens = pl.BlockSpec((sources, 1, tall, lanes), lambda e, i: (i, e, 0, 0))
    return pl.pallas_call(
        expert_kernel,
        grid=(local, count // sources),
        in_specs=[
            tokens,
            pl.BlockSpec(memory_space=VMEM),
            pl.BlockSpec(memory_space=VMEM),
            pl.BlockSpec(memory_space=VMEM),
        ],
        out_specs=tokens,
        out_shape=jax.ShapeDtypeStruct(x.shape, BF16),
        scratch_shapes=[VMEM((rows * PITCH, lanes), F32)],
        compiler_params=pltpu.CompilerParams(
            dimension_semantics=("arbitrary", "arbitrary"), vmem_limit_bytes=36 * MIB
        ),
        name="experts",
    )(x, gate_proj, up_proj, down_proj)


def combine_kernel(back_ref, slot_ref, gate_ref, out_ref, flat_ref):
    toks, width = out_ref.shape
    pieces = width // 128

    @pl.loop(0, toks, unroll=4)
    def _(t):
        total = jnp.zeros((pieces, 128), F32)
        for k in range(slot_ref.shape[0]):
            total = total + gate_ref[k, t] * back_ref[slot_ref[k, t]].astype(F32)
        flat_ref[pl.ds(pl.multiple_of(t * PITCH, 8), pieces), :] = total

    for j in range(pieces):
        out_ref[:, j * 128 : (j + 1) * 128] = flat_ref[pl.ds(j, toks, stride=PITCH), :].astype(BF16)


def combine(back, slots, gates):
    count, pieces, lanes = back.shape
    toks = slots.shape[1]
    smem = pl.BlockSpec(memory_space=pltpu.SMEM)
    return pl.pallas_call(
        combine_kernel,
        in_specs=[pl.BlockSpec(memory_space=VMEM), smem, smem],
        out_specs=pl.BlockSpec(memory_space=VMEM),
        out_shape=jax.ShapeDtypeStruct((toks, pieces * lanes), BF16),
        scratch_shapes=[VMEM((toks * PITCH, lanes), F32)],
        compiler_params=pltpu.CompilerParams(vmem_limit_bytes=24 * MIB),
        name="combine",
    )(back, slots, gates)


def shards(
    queries,
    key_vectors,
    values,
    out_gate,
    write_strength,
    decay_logarithm,
    residual,
    out_weight,
    head_gain,
    post_gain,
    gate_proj,
    up_proj,
    down_proj,
    expert_ids,
    route_gates,
):
    seq, heads, dv = values.shape
    dk = queries.shape[2]
    n_ctx = lax.axis_size("ctx")
    n_exp = lax.axis_size("exp")
    n_dev = n_ctx * n_exp
    parts = n_ctx // heads
    wide = dv // parts
    local_experts = gate_proj.shape[0]
    toks, width = residual.shape

    shift = lambda a, by: lax.ppermute(a, "exp", [(i, (i + 2 * by) % n_exp) for i in range(n_exp)])
    swap = lambda a: lax.ppermute(a, "exp", [(i, i ^ 1) for i in range(n_exp)])
    other_weight = swap(out_weight)
    slots = slots_of(expert_ids.T, local_experts * n_dev)
    gates = route_gates.T

    by_head = lambda a: jnp.transpose(a, (1, 0, 2))
    local_out, msg = local_delta(
        decay_logarithm, write_strength, by_head(queries), by_head(key_vectors), by_head(values), parts
    )
    msg = lax.all_to_all(msg.reshape(n_ctx, dk + wide, dk), "ctx", 0, 0, tiled=True)
    states = lax.all_to_all(prefix_states(msg, wide), "ctx", 0, 0, tiled=True).reshape(heads, dv, dk)
    gating = (local_out, states, by_head(out_gate), head_gain.reshape(1, dv), toks)
    got = swap(gated_rows(1, *gating))
    mine = gated_rows(0, *gating)
    half = jax.ShapeDtypeStruct((toks // 2, width), BF16)
    operands = (mine, got, out_weight, other_weight)
    first, second = project(far_kernel, 1, [half, half], "project_far", *operands)
    first, second = shift(first, 1), shift(second, -1)
    total = jax.ShapeDtypeStruct((toks, width), F32)
    ahead, behind, held = project(near_kernel, 2, [half, half, total], "project_near", *operands)
    ahead, behind = shift(ahead, 1), shift(behind, -1)
    right, left = relay(held, first, second)
    [own] = project(own_kernel, 1, [total], "project_own", *operands)
    attended, send = dispatch(
        own,
        (shift(right, 1), behind),
        (ahead, shift(left, -1)),
        residual,
        post_gain.reshape(1, width),
        slots,
        n_dev * local_experts * CAP,
    )
    tall = CAP * width // 128
    held = lax.all_to_all(
        send.reshape(n_dev, local_experts, tall, 128), ("ctx", "exp"), 0, 0, tiled=True
    )
    done = run_experts(held, gate_proj, up_proj, down_proj)
    back = lax.all_to_all(done, ("ctx", "exp"), 0, 0, tiled=True)
    mixture = combine(back.reshape(n_dev * local_experts * CAP, width // 128, 128), slots, gates)
    return (attended, mixture)


def solution(mesh):
    in_specs = (
        P("ctx", "exp", None),
        P("ctx", "exp", None),
        P("ctx", "exp", None),
        P("ctx", "exp", None),
        P("exp", "ctx"),
        P("exp", "ctx"),
        P(("ctx", "exp"), None),
        P("exp", None),
        P(),
        P(),
        P(("ctx", "exp"), None, None),
        P(("ctx", "exp"), None, None),
        P(("ctx", "exp"), None, None),
        P(("ctx", "exp"), None),
        P(("ctx", "exp"), None),
    )
    out_specs = (P(("ctx", "exp"), None), P(("ctx", "exp"), None))
    return jax.shard_map(shards, mesh=mesh, in_specs=in_specs, out_specs=out_specs, check_vma=False)
```

```python
import functools

import jax
import jax.numpy as jnp
from jax import lax
from jax.experimental import pallas as pl
from jax.experimental.pallas import tpu as pltpu
from jax.sharding import PartitionSpec as P

CHUNK = 128
PER_STEP = 4
CAP = 10
PITCH = 24
F32 = jnp.float32
BF16 = jnp.bfloat16
VMEM = pltpu.VMEM
MIB = 1024 * 1024


def mxu(a, b, dims=((1,), (0,))):
    return lax.dot_general(a, b, (dims, ((), ())), preferred_element_type=F32)


def halves(a):
    high = a.astype(BF16)
    return high, (a - high.astype(F32)).astype(BF16)


def product(a, b):
    width = b[0].shape[1]
    left = jnp.concatenate([a[0], a[1]], axis=1)
    right = jnp.concatenate(
        [
            jnp.concatenate([b[0], b[1]], axis=1),
            jnp.concatenate([b[0], jnp.zeros_like(b[0])], axis=1),
        ],
        axis=0,
    )
    both = mxu(left, right)
    return both[:, :width] + both[:, width:]


def unit_lower_inverses(lowers, row, col):
    eye = (row == col).astype(F32)
    near = row // 16 == col // 16
    diags = [jnp.where(near, low, 0.0) for low in lowers]
    inverses = [eye - diag for diag in diags]
    powers = [halves(-diag) for diag in diags]
    for step in range(3):
        powers = [halves(product(power, power)) for power in powers]
        inverses = [inv + product(halves(inv), power) for inv, power in zip(inverses, powers)]
    size = 16
    while size < row.shape[0]:
        pick = (row // (2 * size) == col // (2 * size)) & (row // size != col // size)
        belows = [jnp.where(pick, low, 0.0).astype(BF16) for low in lowers]
        invs = [inv.astype(BF16) for inv in inverses]
        crossed = [mxu(inv, below).astype(BF16) for inv, below in zip(invs, belows)]
        inverses = [full - mxu(cro, inv) for full, cro, inv in zip(inverses, crossed, invs)]
        size = size * 2
    return inverses


def delta_kernel(decay_ref, beta_ref, q_ref, k_ref, v_ref, left_ref, right_ref, msg_ref, state_ref):
    step = pl.program_id(0)
    heads = v_ref.shape[0]
    group = heads // q_ref.shape[0]
    d = q_ref.shape[2]
    c = CHUNK
    per_step = q_ref.shape[1] // c
    row = lax.broadcasted_iota(jnp.int32, (c, c), 0)
    col = lax.broadcasted_iota(jnp.int32, (c, c), 1)
    causal = row >= col
    strict = row > col

    @pl.when(step == 0)
    def _():
        eye = (row == col).astype(F32)
        for h in range(heads):
            state_ref[h] = jnp.concatenate([eye, jnp.zeros_like(eye)], axis=1)

    upto = (row <= col).astype(BF16)
    rows_of, columns_of = [], []
    for n in range(per_step):
        ds = jnp.concatenate([a[:, n * c : (n + 1) * c] for a in (decay_ref, beta_ref)], axis=0)
        d0 = ds.astype(BF16)
        rest = ds - d0.astype(F32)
        d1 = rest.astype(BF16)
        d2 = (rest - d1.astype(F32)).astype(BF16)
        cum = mxu(d0, upto) + mxu(d1, upto) + mxu(d2, upto)
        half = jnp.where(lax.broadcasted_iota(jnp.int32, ds.shape, 0) < heads, cum, ds)
        rows_of.append(half)
        columns_of.append(jnp.transpose(half, (1, 0)))

    keyed = []
    for n in range(per_step):
        span = pl.ds(n * c, c)
        for g in range(q_ref.shape[0]):
            q, k = q_ref[g, span], k_ref[g, span]
            qf, kf = q.astype(F32), k.astype(F32)
            q_col = (d ** -0.5) / jnp.sqrt(jnp.sum(qf * qf, axis=1, keepdims=True) + 1e-06)
            k_col = 1.0 / jnp.sqrt(jnp.sum(kf * kf, axis=1, keepdims=True) + 1e-06)
            gram = mxu(k, k, ((1,), (1,)))
            k_row = 1.0 / jnp.sqrt(jnp.sum(jnp.where(row == col, gram, 0.0), axis=0, keepdims=True) + 1e-06)
            gram = gram * (k_col * k_row)
            cross = mxu(q, k, ((1,), (1,))) * (q_col * k_row)
            keyed.append((qf, k, q_col, k_col, k_row, gram, cross, jnp.transpose(kf, (1, 0)).astype(BF16)))

    lowers, mixings = [], []
    for n in range(per_step):
        for h in range(heads):
            gram, cross = keyed[n * q_ref.shape[0] + h // group][5:7]
            cum_col, beta_col = columns_of[n][:, h : h + 1], columns_of[n][:, heads + h : heads + h + 1]
            cum_row = rows_of[n][h : h + 1, :]
            spread = jnp.where(causal, jnp.exp(jnp.where(causal, cum_col - cum_row, 0.0)), 0.0)
            lowers.append(jnp.where(strict, beta_col * gram * spread, 0.0))
            mixings.append((cross * spread).astype(BF16))
    inverses = unit_lower_inverses(lowers, row, col)
    weights, writes = [], []
    for n in range(per_step):
        for h in range(heads):
            k, k_row = keyed[n * q_ref.shape[0] + h // group][1], keyed[n * q_ref.shape[0] + h // group][4]
            cum_row, beta_row = rows_of[n][h : h + 1, :], rows_of[n][heads + h : heads + h + 1, :]
            inverse = inverses[n * heads + h]
            t_k = halves(inverse * (beta_row * jnp.exp(cum_row) * k_row))
            t_v = halves(inverse * beta_row)
            v = v_ref[h, pl.ds(n * c, c)]
            weights.append(
                mxu(jnp.concatenate(t_k, axis=1), jnp.concatenate([k, k], axis=0)).astype(BF16)
            )
            writes.append(mxu(jnp.concatenate(t_v, axis=1), jnp.concatenate([v, v], axis=0)))

    states = [state_ref[h] for h in range(heads)]
    for n in range(per_step):
        span = pl.ds(n * c, c)
        bases = [state.astype(BF16) for state in states]
        reads = [mxu(weights[n * heads + h], bases[h]) for h in range(heads)]
        freshes, tails = [], []
        for h in range(heads):
            k_col = keyed[n * q_ref.shape[0] + h // group][3]
            cum_col = columns_of[n][:, h : h + 1]
            closing = rows_of[n][h : h + 1, c - 1 : c]
            written = writes[n * heads + h]
            fresh = jnp.concatenate([-reads[h][:, :d], written - reads[h][:, d:]], axis=1)
            freshes.append(fresh.astype(BF16))
            tails.append((fresh * (k_col * jnp.exp(closing - cum_col))).astype(BF16))
        for h in range(heads):
            closing = rows_of[n][h : h + 1, c - 1 : c]
            k_t = keyed[n * q_ref.shape[0] + h // group][7]
            states[h] = jnp.exp(closing) * states[h] + mxu(k_t, tails[h])
        for h in range(heads):
            qf, q_col = keyed[n * q_ref.shape[0] + h // group][0], keyed[n * q_ref.shape[0] + h // group][2]
            cum_col = columns_of[n][:, h : h + 1]
            query = (qf * (q_col * jnp.exp(cum_col))).astype(BF16)
            left_ref[h, span] = jnp.concatenate([query, mixings[n * heads + h]], axis=1)
            right_ref[h, pl.ds(2 * n * c, c)] = bases[h]
            right_ref[h, pl.ds((2 * n + 1) * c, c)] = freshes[h]
    for h in range(heads):
        state_ref[h] = states[h]

    @pl.when(step == pl.num_programs(0) - 1)
    def _():
        parts = msg_ref.shape[1]
        wide = d // parts
        for h in range(heads):
            state = state_ref[h]
            moved = state[:, :d].astype(msg_ref.dtype)
            added = jnp.transpose(state[:, d:], (1, 0)).astype(msg_ref.dtype)
            for p in range(parts):
                msg_ref[h, p, :d, :] = moved
                msg_ref[h, p, d:, :] = added[p * wide : (p + 1) * wide]


def local_delta(decay, beta, q, k, v, parts):
    heads, seq, dv = v.shape
    kh, _, dk = q.shape
    wide = dv // parts
    rows = PER_STEP * CHUNK
    return pl.pallas_call(
        delta_kernel,
        grid=(seq // rows,),
        in_specs=[
            pl.BlockSpec((heads, rows), lambda i: (0, i)),
            pl.BlockSpec((heads, rows), lambda i: (0, i)),
            pl.BlockSpec((kh, rows, dk), lambda i: (0, i, 0)),
            pl.BlockSpec((kh, rows, dk), lambda i: (0, i, 0)),
            pl.BlockSpec((heads, rows, dv), lambda i: (0, i, 0)),
        ],
        out_specs=[
            pl.BlockSpec((heads, rows, dk + CHUNK), lambda i: (0, i, 0)),
            pl.BlockSpec((heads, 2 * rows, dk + dv), lambda i: (0, i, 0)),
            pl.BlockSpec((heads, parts, dk + wide, dk), lambda i: (0, 0, 0, 0)),
        ],
        out_shape=[
            pltpu.HBM((heads, seq, dk + CHUNK), BF16),
            pltpu.HBM((heads, 2 * seq, dk + dv), BF16),
            jax.ShapeDtypeStruct((heads, parts, dk + wide, dk), BF16),
        ],
        scratch_shapes=[VMEM((heads, dk, dk + dv), F32)],
        compiler_params=pltpu.CompilerParams(
            dimension_semantics=("arbitrary",), vmem_limit_bytes=36 * MIB
        ),
        name="delta_local",
    )(decay, beta, q, k, v)


def outputs_kernel(left_ref, right_ref, out_ref):
    c = CHUNK
    for n in range(left_ref.shape[1] // c):
        for h in range(left_ref.shape[0]):
            span = pl.ds(n * c, c)
            out_ref[h, span] = mxu(left_ref[h, span], right_ref[h, pl.ds(2 * n * c, 2 * c)]).astype(BF16)


def local_outputs(left, right):
    heads, seq, _ = left.shape
    width = right.shape[2]
    rows = 2 * CHUNK
    by_rows = lambda many, wide: pl.BlockSpec((heads, many, wide), lambda i: (0, i, 0))
    return pl.pallas_call(
        outputs_kernel,
        grid=(seq // rows,),
        in_specs=[by_rows(rows, left.shape[2]), by_rows(2 * rows, width)],
        out_specs=by_rows(rows, width),
        out_shape=pltpu.HBM((heads, seq, width), BF16),
        cost_estimate=pl.CostEstimate(
            flops=2 * left.size * width, bytes_accessed=2 * (2 * left.size + right.size), transcendentals=0
        ),
        compiler_params=pltpu.CompilerParams(dimension_semantics=("arbitrary",), vmem_limit_bytes=56 * MIB),
        name="local_outputs",
    )(left, right)


def prefix_kernel(msg_ref, out_ref):
    count, tall, dk = msg_ref.shape
    wide = tall - dk
    state = jnp.zeros((wide, dk), F32)
    for i in range(count):
        out_ref[i] = state.astype(out_ref.dtype)
        if i < count - 1:
            both = jnp.concatenate(halves(state), axis=0)
            moved = mxu(both, msg_ref[i, :dk, :], ((1,), (1,)))
            state = moved[:wide] + moved[wide:] + msg_ref[i, dk:, :].astype(F32)


def prefix_states(msg, wide):
    count, tall, dk = msg.shape
    return pl.pallas_call(
        prefix_kernel,
        out_shape=jax.ShapeDtypeStruct((count, wide, dk), BF16),
        compiler_params=pltpu.CompilerParams(vmem_limit_bytes=16 * MIB),
        name="prefix_states",
    )(msg)


def gate_kernel(other, ro_ref, s_ref, g_ref, gain_ref, out_ref):
    heads, d, _ = s_ref.shape
    chunks, rows, _ = out_ref.shape
    part = (lax.axis_index("exp") & 1) ^ other
    for i in range(chunks):
        span = pl.ds(pl.multiple_of((2 * i + part) * rows, rows), rows)
        both = [ro_ref[h, span, :] for h in range(heads)]
        reads = [mxu(both[h][:, :d], s_ref[h], ((1,), (1,))) for h in range(heads)]
        gates = [g_ref[h, span, :].astype(F32) for h in range(heads)]
        silus = [gate * lax.logistic(gate) * gain_ref[...] for gate in gates]
        values = [both[h][:, d:].astype(F32) + reads[h] for h in range(heads)]
        scales = [1.0 / jnp.sqrt(jnp.mean(value * value, axis=1, keepdims=True) + 1e-06) for value in values]
        for h in range(heads):
            out_ref[i, :, h * d : (h + 1) * d] = (values[h] * scales[h] * silus[h]).astype(BF16)


def gated_rows(other, ro, states, gate, gain, toks):
    heads, seq, d = gate.shape
    whole = pl.BlockSpec(memory_space=VMEM)
    half = heads * seq * d // 2
    return pl.pallas_call(
        functools.partial(gate_kernel, other),
        in_specs=[whole] * 4,
        out_specs=whole,
        out_shape=jax.ShapeDtypeStruct((seq // (2 * toks), toks, heads * d), BF16),
        cost_estimate=pl.CostEstimate(flops=2 * half * d, bytes_accessed=8 * half, transcendentals=half),
        compiler_params=pltpu.CompilerParams(vmem_limit_bytes=24 * MIB),
        name="gated_other" if other else "gated_own",
    )(ro, states, gate, gain)


def chunk_at(step, mine_ref, got_ref):
    place = lax.rem((lax.axis_index("exp") >> 1) + step, mine_ref.shape[0])
    return jnp.concatenate([mine_ref[place], got_ref[place]], axis=1)


def far_kernel(mine_ref, got_ref, w_ref, v_ref, a_ref, b_ref):
    rows = chunk_at(2, mine_ref, got_ref)
    deep, half = w_ref.shape[0], a_ref.shape[0]
    part = mxu(rows[:, :deep], w_ref[...]) + mxu(rows[:, deep:], v_ref[...])
    a_ref[...] = part[:half].astype(BF16)
    b_ref[...] = part[half:].astype(BF16)


def near_kernel(mine_ref, got_ref, w_ref, v_ref, right_ref, left_ref, held_ref):
    half = right_ref.shape[0]
    deep = w_ref.shape[0]
    rows = jnp.concatenate(
        [chunk_at(1, mine_ref, got_ref), chunk_at(mine_ref.shape[0] - 1, mine_ref, got_ref)], axis=0
    )
    part = mxu(rows[:, :deep], w_ref[...]) + mxu(rows[:, deep:], v_ref[...])
    held_ref[:half] = part[:half]
    right_ref[...] = part[half : 2 * half].astype(BF16)
    left_ref[...] = part[2 * half : 3 * half].astype(BF16)
    held_ref[half:] = part[3 * half :]


def own_kernel(mine_ref, got_ref, w_ref, v_ref, out_ref):
    rows = chunk_at(0, mine_ref, got_ref)
    deep = w_ref.shape[0]
    out_ref[...] = mxu(rows[:, :deep], w_ref[...]) + mxu(rows[:, deep:], v_ref[...])


def project(kernel, chunks, out_shape, name, mine, got, weight, other):
    count, toks, deep = mine.shape
    width = weight.shape[1]
    whole = pl.BlockSpec(memory_space=VMEM)
    return pl.pallas_call(
        kernel,
        in_specs=[whole] * 4,
        out_specs=[whole] * len(out_shape),
        out_shape=out_shape,
        cost_estimate=pl.CostEstimate(
            flops=4 * chunks * toks * deep * width,
            bytes_accessed=4 * weight.size + 4 * chunks * toks * width,
            transcendentals=0,
        ),
        compiler_params=pltpu.CompilerParams(vmem_limit_bytes=24 * MIB),
        name=name,
    )(mine, got, weight, other)


def relay_kernel(held_ref, a_ref, b_ref, right_ref, left_ref):
    half = a_ref.shape[0]
    right_ref[...] = (held_ref[:half] + a_ref[...].astype(F32)).astype(BF16)
    left_ref[...] = (held_ref[half:] + b_ref[...].astype(F32)).astype(BF16)


def relay(held, first, second):
    shape = jax.ShapeDtypeStruct(first.shape, BF16)
    return pl.pallas_call(
        relay_kernel,
        out_shape=[shape, shape],
        compiler_params=pltpu.CompilerParams(vmem_limit_bytes=16 * MIB),
        name="relay",
    )(held, first, second)


def slot_kernel(experts, ids_ref, out_ref):
    top, toks = ids_ref.shape
    expert = lax.broadcasted_iota(jnp.int32, (experts, toks), 0)
    hits = jnp.zeros((experts, toks), F32)
    for k in range(top):
        hits = hits + (expert == ids_ref[k : k + 1, :]).astype(F32)
    before = (
        lax.broadcasted_iota(jnp.int32, (toks, toks), 0) < lax.broadcasted_iota(jnp.int32, (toks, toks), 1)
    ).astype(BF16)
    earlier = mxu(hits.astype(BF16), before)
    for k in range(top):
        ids = ids_ref[k : k + 1, :]
        rank = jnp.sum(jnp.where(expert == ids, earlier, 0.0), axis=0, keepdims=True)
        out_ref[k : k + 1, :] = ids * CAP + rank.astype(jnp.int32)


def slots_of(ids, experts):
    return pl.pallas_call(
        functools.partial(slot_kernel, experts),
        out_shape=jax.ShapeDtypeStruct(ids.shape, jnp.int32),
        compiler_params=pltpu.CompilerParams(vmem_limit_bytes=16 * MIB),
        name="slots",
    )(ids)


def dispatch_kernel(own_ref, a0_ref, a1_ref, b0_ref, b1_ref, res_ref, gain_ref, slot_ref, att_ref, send_ref, flat_ref):
    toks, width = res_ref.shape
    pieces = width // 128
    own = own_ref[...]
    early = own[: toks // 2] + a0_ref[...].astype(F32) + a1_ref[...].astype(F32)
    late = own[toks // 2 :] + b0_ref[...].astype(F32) + b1_ref[...].astype(F32)
    total = jnp.concatenate([early, late], axis=0)
    attended = (res_ref[...].astype(F32) + total).astype(BF16)
    att_ref[...] = attended
    settled = attended.astype(F32)
    scale = 1.0 / jnp.sqrt(jnp.mean(settled * settled, axis=1, keepdims=True) + 1e-06)
    normed = settled * scale * gain_ref[...]
    for j in range(pieces):
        flat_ref[pl.ds(j, toks, stride=PITCH), :] = normed[:, j * 128 : (j + 1) * 128]

    @pl.loop(0, toks, unroll=4)
    def _(t):
        tile = flat_ref[pl.ds(pl.multiple_of(t * PITCH, 8), pieces), :].astype(BF16)
        for k in range(slot_ref.shape[0]):
            send_ref[slot_ref[k, t]] = tile


def dispatch(own, early, late, residual, gain, slots, count):
    toks, width = residual.shape
    pieces = width // 128
    whole = pl.BlockSpec(memory_space=VMEM)
    return pl.pallas_call(
        dispatch_kernel,
        in_specs=[whole] * 7 + [pl.BlockSpec(memory_space=pltpu.SMEM)],
        out_specs=[whole, whole],
        out_shape=[
            jax.ShapeDtypeStruct((toks, width), BF16),
            jax.ShapeDtypeStruct((count, pieces, 128), BF16),
        ],
        scratch_shapes=[VMEM((toks * PITCH, 128), F32)],
        compiler_params=pltpu.CompilerParams(vmem_limit_bytes=24 * MIB),
        name="dispatch",
    )(own, *early, *late, residual, gain, slots)


def expert_kernel(x_ref, wg_ref, wu_ref, wd_ref, out_ref, flat_ref):
    sources, _, tall, lanes = x_ref.shape
    pieces = wg_ref.shape[1] // lanes
    rows = flat_ref.shape[0] // PITCH
    tiles_ref = flat_ref.reshape(rows, PITCH, lanes)
    tiles_ref[:, :pieces, :] = x_ref[...].reshape(rows, pieces, lanes).astype(F32)
    x = jnp.concatenate(
        [flat_ref[pl.ds(j, rows, stride=PITCH), :].astype(BF16) for j in range(pieces)], axis=1
    )
    e = pl.program_id(0)
    gate = mxu(x, wg_ref[e])
    up = mxu(x, wu_ref[e])
    inner = (gate * lax.logistic(gate) * up).astype(BF16)
    y = mxu(inner, wd_ref[e])
    for j in range(pieces):
        flat_ref[pl.ds(j, rows, stride=PITCH), :] = y[:, j * lanes : (j + 1) * lanes]
    out_ref[...] = tiles_ref[:, :pieces, :].astype(BF16).reshape(sources, 1, tall, lanes)


def run_experts(x, gate_proj, up_proj, down_proj):
    count, local, tall, lanes = x.shape
    sources = 64
    rows = sources * tall * lanes // gate_proj.shape[1]
    tokens = pl.BlockSpec((sources, 1, tall, lanes), lambda e, i: (i, e, 0, 0))
    return pl.pallas_call(
        expert_kernel,
        grid=(local, count // sources),
        in_specs=[
            tokens,
            pl.BlockSpec(memory_space=VMEM),
            pl.BlockSpec(memory_space=VMEM),
            pl.BlockSpec(memory_space=VMEM),
        ],
        out_specs=tokens,
        out_shape=jax.ShapeDtypeStruct(x.shape, BF16),
        scratch_shapes=[VMEM((rows * PITCH, lanes), F32)],
        compiler_params=pltpu.CompilerParams(
            dimension_semantics=("arbitrary", "arbitrary"), vmem_limit_bytes=36 * MIB
        ),
        name="experts",
    )(x, gate_proj, up_proj, down_proj)


def combine_kernel(back_ref, slot_ref, gate_ref, out_ref, flat_ref):
    toks, width = out_ref.shape
    pieces = width // 128

    @pl.loop(0, toks, unroll=4)
    def _(t):
        total = jnp.zeros((pieces, 128), F32)
        for k in range(slot_ref.shape[0]):
            total = total + gate_ref[k, t] * back_ref[slot_ref[k, t]].astype(F32)
        flat_ref[pl.ds(pl.multiple_of(t * PITCH, 8), pieces), :] = total

    for j in range(pieces):
        out_ref[:, j * 128 : (j + 1) * 128] = flat_ref[pl.ds(j, toks, stride=PITCH), :].astype(BF16)


def combine(back, slots, gates):
    count, pieces, lanes = back.shape
    toks = slots.shape[1]
    smem = pl.BlockSpec(memory_space=pltpu.SMEM)
    return pl.pallas_call(
        combine_kernel,
        in_specs=[pl.BlockSpec(memory_space=VMEM), smem, smem],
        out_specs=pl.BlockSpec(memory_space=VMEM),
        out_shape=jax.ShapeDtypeStruct((toks, pieces * lanes), BF16),
        scratch_shapes=[VMEM((toks * PITCH, lanes), F32)],
        compiler_params=pltpu.CompilerParams(vmem_limit_bytes=24 * MIB),
        name="combine",
    )(back, slots, gates)


def shards(
    queries,
    key_vectors,
    values,
    out_gate,
    write_strength,
    decay_logarithm,
    residual,
    out_weight,
    head_gain,
    post_gain,
    gate_proj,
    up_proj,
    down_proj,
    expert_ids,
    route_gates,
):
    seq, heads, dv = values.shape
    dk = queries.shape[2]
    n_ctx = lax.axis_size("ctx")
    n_exp = lax.axis_size("exp")
    n_dev = n_ctx * n_exp
    parts = n_ctx // heads
    wide = dv // parts
    local_experts = gate_proj.shape[0]
    toks, width = residual.shape

    shift = lambda a, by: lax.ppermute(a, "exp", [(i, (i + 2 * by) % n_exp) for i in range(n_exp)])
    swap = lambda a: lax.ppermute(a, "exp", [(i, i ^ 1) for i in range(n_exp)])
    other_weight = swap(out_weight)
    slots = slots_of(expert_ids.T, local_experts * n_dev)
    gates = route_gates.T

    by_head = lambda a: jnp.transpose(a, (1, 0, 2))
    left_side, right_side, msg = local_delta(
        decay_logarithm, write_strength, by_head(queries), by_head(key_vectors), by_head(values), parts
    )
    msg = lax.all_to_all(msg.reshape(n_ctx, dk + wide, dk), "ctx", 0, 0, tiled=True)
    local_out = local_outputs(left_side, right_side)
    states = lax.all_to_all(prefix_states(msg, wide), "ctx", 0, 0, tiled=True).reshape(heads, dv, dk)
    gating = (local_out, states, by_head(out_gate), head_gain.reshape(1, dv), toks)
    got = swap(gated_rows(1, *gating))
    mine = gated_rows(0, *gating)
    half = jax.ShapeDtypeStruct((toks // 2, width), BF16)
    operands = (mine, got, out_weight, other_weight)
    first, second = project(far_kernel, 1, [half, half], "project_far", *operands)
    first, second = shift(first, 1), shift(second, -1)
    total = jax.ShapeDtypeStruct((toks, width), F32)
    ahead, behind, held = project(near_kernel, 2, [half, half, total], "project_near", *operands)
    ahead, behind = shift(ahead, 1), shift(behind, -1)
    right, left = relay(held, first, second)
    [own] = project(own_kernel, 1, [total], "project_own", *operands)
    attended, send = dispatch(
        own,
        (shift(right, 1), behind),
        (ahead, shift(left, -1)),
        residual,
        post_gain.reshape(1, width),
        slots,
        n_dev * local_experts * CAP,
    )
    tall = CAP * width // 128
    held = lax.all_to_all(
        send.reshape(n_dev, local_experts, tall, 128), ("ctx", "exp"), 0, 0, tiled=True
    )
    done = run_experts(held, gate_proj, up_proj, down_proj)
    back = lax.all_to_all(done, ("ctx", "exp"), 0, 0, tiled=True)
    mixture = combine(back.reshape(n_dev * local_experts * CAP, width // 128, 128), slots, gates)
    return (attended, mixture)


def solution(mesh):
    in_specs = (
        P("ctx", "exp", None),
        P("ctx", "exp", None),
        P("ctx", "exp", None),
        P("ctx", "exp", None),
        P("exp", "ctx"),
        P("exp", "ctx"),
        P(("ctx", "exp"), None),
        P("exp", None),
        P(),
        P(),
        P(("ctx", "exp"), None, None),
        P(("ctx", "exp"), None, None),
        P(("ctx", "exp"), None, None),
        P(("ctx", "exp"), None),
        P(("ctx", "exp"), None),
    )
    out_specs = (P(("ctx", "exp"), None), P(("ctx", "exp"), None))
    return jax.shard_map(shards, mesh=mesh, in_specs=in_specs, out_specs=out_specs, check_vma=False)
```

```python
import functools

import jax
import jax.numpy as jnp
from jax import lax
from jax.experimental import pallas as pl
from jax.experimental.pallas import tpu as pltpu
from jax.sharding import PartitionSpec as P

CHUNK = 128
PER_STEP = 4
CAP = 10
PITCH = 24
F32 = jnp.float32
BF16 = jnp.bfloat16
VMEM = pltpu.VMEM
MIB = 1024 * 1024


def mxu(a, b, dims=((1,), (0,))):
    return lax.dot_general(a, b, (dims, ((), ())), preferred_element_type=F32)


def halves(a):
    high = a.astype(BF16)
    return high, (a - high.astype(F32)).astype(BF16)


def product(a, b):
    width = b[0].shape[1]
    left = jnp.concatenate([a[0], a[1]], axis=1)
    right = jnp.concatenate(
        [
            jnp.concatenate([b[0], b[1]], axis=1),
            jnp.concatenate([b[0], jnp.zeros_like(b[0])], axis=1),
        ],
        axis=0,
    )
    both = mxu(left, right)
    return both[:, :width] + both[:, width:]


def unit_lower_inverses(lowers, row, col):
    eye = (row == col).astype(F32)
    near = row // 16 == col // 16
    diags = [jnp.where(near, low, 0.0) for low in lowers]
    inverses = [eye - diag for diag in diags]
    powers = [halves(-diag) for diag in diags]
    for step in range(3):
        powers = [halves(product(power, power)) for power in powers]
        inverses = [inv + product(halves(inv), power) for inv, power in zip(inverses, powers)]
    size = 16
    while size < row.shape[0]:
        pick = (row // (2 * size) == col // (2 * size)) & (row // size != col // size)
        belows = [jnp.where(pick, low, 0.0).astype(BF16) for low in lowers]
        invs = [inv.astype(BF16) for inv in inverses]
        crossed = [mxu(inv, below).astype(BF16) for inv, below in zip(invs, belows)]
        inverses = [full - mxu(cro, inv) for full, cro, inv in zip(inverses, crossed, invs)]
        size = size * 2
    return inverses


def delta_kernel(decay_ref, beta_ref, q_ref, k_ref, v_ref, out_ref, msg_ref, state_ref):
    step = pl.program_id(0)
    heads = v_ref.shape[0]
    group = heads // q_ref.shape[0]
    d = q_ref.shape[2]
    c = CHUNK
    per_step = q_ref.shape[1] // c
    row = lax.broadcasted_iota(jnp.int32, (c, c), 0)
    col = lax.broadcasted_iota(jnp.int32, (c, c), 1)
    causal = row >= col
    strict = row > col

    @pl.when(step == 0)
    def _():
        eye = (row == col).astype(F32)
        for h in range(heads):
            state_ref[h] = jnp.concatenate([eye, jnp.zeros_like(eye)], axis=1)

    upto = (row <= col).astype(BF16)
    rows_of, columns_of = [], []
    for n in range(per_step):
        ds = jnp.concatenate([a[:, n * c : (n + 1) * c] for a in (decay_ref, beta_ref)], axis=0)
        d0 = ds.astype(BF16)
        rest = ds - d0.astype(F32)
        d1 = rest.astype(BF16)
        d2 = (rest - d1.astype(F32)).astype(BF16)
        cum = mxu(d0, upto) + mxu(d1, upto) + mxu(d2, upto)
        half = jnp.where(lax.broadcasted_iota(jnp.int32, ds.shape, 0) < heads, cum, ds)
        rows_of.append(half)
        columns_of.append(jnp.transpose(half, (1, 0)))

    keyed = []
    for n in range(per_step):
        span = pl.ds(n * c, c)
        for g in range(q_ref.shape[0]):
            q, k = q_ref[g, span], k_ref[g, span]
            qf, kf = q.astype(F32), k.astype(F32)
            q_col = (d ** -0.5) / jnp.sqrt(jnp.sum(qf * qf, axis=1, keepdims=True) + 1e-06)
            k_col = 1.0 / jnp.sqrt(jnp.sum(kf * kf, axis=1, keepdims=True) + 1e-06)
            gram = mxu(k, k, ((1,), (1,)))
            k_row = 1.0 / jnp.sqrt(jnp.sum(jnp.where(row == col, gram, 0.0), axis=0, keepdims=True) + 1e-06)
            gram = gram * (k_col * k_row)
            cross = mxu(q, k, ((1,), (1,))) * (q_col * k_row)
            keyed.append((qf, k, q_col, k_col, k_row, gram, cross, jnp.transpose(kf, (1, 0)).astype(BF16)))

    lowers, mixings = [], []
    for n in range(per_step):
        for h in range(heads):
            gram, cross = keyed[n * q_ref.shape[0] + h // group][5:7]
            cum_col, beta_col = columns_of[n][:, h : h + 1], columns_of[n][:, heads + h : heads + h + 1]
            cum_row = rows_of[n][h : h + 1, :]
            spread = jnp.where(causal, jnp.exp(jnp.where(causal, cum_col - cum_row, 0.0)), 0.0)
            lowers.append(jnp.where(strict, beta_col * gram * spread, 0.0))
            mixings.append((cross * spread).astype(BF16))
    inverses = unit_lower_inverses(lowers, row, col)
    weights, writes = [], []
    for n in range(per_step):
        for h in range(heads):
            k, k_row = keyed[n * q_ref.shape[0] + h // group][1], keyed[n * q_ref.shape[0] + h // group][4]
            cum_row, beta_row = rows_of[n][h : h + 1, :], rows_of[n][heads + h : heads + h + 1, :]
            inverse = inverses[n * heads + h]
            t_k = halves(inverse * (beta_row * jnp.exp(cum_row) * k_row))
            t_v = halves(inverse * beta_row)
            v = v_ref[h, pl.ds(n * c, c)]
            weights.append(
                mxu(jnp.concatenate(t_k, axis=1), jnp.concatenate([k, k], axis=0)).astype(BF16)
            )
            writes.append(mxu(jnp.concatenate(t_v, axis=1), jnp.concatenate([v, v], axis=0)))

    states = [state_ref[h] for h in range(heads)]
    for n in range(per_step):
        span = pl.ds(n * c, c)
        bases = [state.astype(BF16) for state in states]
        reads = [mxu(weights[n * heads + h], bases[h]) for h in range(heads)]
        freshes, tails = [], []
        for h in range(heads):
            k_col = keyed[n * q_ref.shape[0] + h // group][3]
            cum_col = columns_of[n][:, h : h + 1]
            closing = rows_of[n][h : h + 1, c - 1 : c]
            written = writes[n * heads + h]
            fresh = jnp.concatenate([-reads[h][:, :d], written - reads[h][:, d:]], axis=1)
            freshes.append(fresh.astype(BF16))
            tails.append((fresh * (k_col * jnp.exp(closing - cum_col))).astype(BF16))
        for h in range(heads):
            closing = rows_of[n][h : h + 1, c - 1 : c]
            k_t = keyed[n * q_ref.shape[0] + h // group][7]
            states[h] = jnp.exp(closing) * states[h] + mxu(k_t, tails[h])
        for h in range(heads):
            qf, q_col = keyed[n * q_ref.shape[0] + h // group][0], keyed[n * q_ref.shape[0] + h // group][2]
            cum_col = columns_of[n][:, h : h + 1]
            query = (qf * (q_col * jnp.exp(cum_col))).astype(BF16)
            out = mxu(
                jnp.concatenate([query, mixings[n * heads + h]], axis=1),
                jnp.concatenate([bases[h], freshes[h]], axis=0),
            )
            out_ref[h, span] = out.astype(BF16)
    for h in range(heads):
        state_ref[h] = states[h]

    @pl.when(step == pl.num_programs(0) - 1)
    def _():
        parts = msg_ref.shape[1]
        wide = d // parts
        for h in range(heads):
            state = state_ref[h]
            moved = state[:, :d].astype(msg_ref.dtype)
            added = jnp.transpose(state[:, d:], (1, 0)).astype(msg_ref.dtype)
            for p in range(parts):
                msg_ref[h, p, :d, :] = moved
                msg_ref[h, p, d:, :] = added[p * wide : (p + 1) * wide]


def local_delta(decay, beta, q, k, v, parts):
    heads, seq, dv = v.shape
    kh, _, dk = q.shape
    wide = dv // parts
    rows = PER_STEP * CHUNK
    return pl.pallas_call(
        delta_kernel,
        grid=(seq // rows,),
        in_specs=[
            pl.BlockSpec((heads, rows), lambda i: (0, i)),
            pl.BlockSpec((heads, rows), lambda i: (0, i)),
            pl.BlockSpec((kh, rows, dk), lambda i: (0, i, 0)),
            pl.BlockSpec((kh, rows, dk), lambda i: (0, i, 0)),
            pl.BlockSpec((heads, rows, dv), lambda i: (0, i, 0)),
        ],
        out_specs=[
            pl.BlockSpec((heads, rows, dk + dv), lambda i: (0, i, 0)),
            pl.BlockSpec((heads, parts, dk + wide, dk), lambda i: (0, 0, 0, 0)),
        ],
        out_shape=[
            pltpu.HBM((heads, seq, dk + dv), BF16),
            jax.ShapeDtypeStruct((heads, parts, dk + wide, dk), BF16),
        ],
        scratch_shapes=[VMEM((heads, dk, dk + dv), F32)],
        compiler_params=pltpu.CompilerParams(
            dimension_semantics=("arbitrary",), vmem_limit_bytes=30 * MIB
        ),
        name="delta_local",
    )(decay, beta, q, k, v)


def prefix_kernel(msg_ref, out_ref):
    count, tall, dk = msg_ref.shape
    wide = tall - dk
    state = jnp.zeros((wide, dk), F32)
    for i in range(count):
        out_ref[i] = state.astype(out_ref.dtype)
        if i < count - 1:
            both = jnp.concatenate(halves(state), axis=0)
            moved = mxu(both, msg_ref[i, :dk, :], ((1,), (1,)))
            state = moved[:wide] + moved[wide:] + msg_ref[i, dk:, :].astype(F32)


def prefix_states(msg, wide):
    count, tall, dk = msg.shape
    return pl.pallas_call(
        prefix_kernel,
        out_shape=jax.ShapeDtypeStruct((count, wide, dk), BF16),
        compiler_params=pltpu.CompilerParams(vmem_limit_bytes=16 * MIB),
        name="prefix_states",
    )(msg)


def gate_kernel(other, ro_ref, s_ref, g_ref, gain_ref, out_ref):
    heads, d, _ = s_ref.shape
    chunks, rows, _ = out_ref.shape
    part = (lax.axis_index("exp") & 1) ^ other
    for i in range(chunks):
        span = pl.ds(pl.multiple_of((2 * i + part) * rows, rows), rows)
        both = [ro_ref[h, span, :] for h in range(heads)]
        reads = [mxu(both[h][:, :d], s_ref[h], ((1,), (1,))) for h in range(heads)]
        gates = [g_ref[h, span, :].astype(F32) for h in range(heads)]
        silus = [gate * lax.logistic(gate) * gain_ref[...] for gate in gates]
        values = [both[h][:, d:].astype(F32) + reads[h] for h in range(heads)]
        scales = [1.0 / jnp.sqrt(jnp.mean(value * value, axis=1, keepdims=True) + 1e-06) for value in values]
        for h in range(heads):
            out_ref[i, :, h * d : (h + 1) * d] = (values[h] * scales[h] * silus[h]).astype(BF16)


def gated_rows(other, ro, states, gate, gain, toks):
    heads, seq, d = gate.shape
    whole = pl.BlockSpec(memory_space=VMEM)
    half = heads * seq * d // 2
    return pl.pallas_call(
        functools.partial(gate_kernel, other),
        in_specs=[whole] * 4,
        out_specs=whole,
        out_shape=jax.ShapeDtypeStruct((seq // (2 * toks), toks, heads * d), BF16),
        cost_estimate=pl.CostEstimate(flops=2 * half * d, bytes_accessed=8 * half, transcendentals=half),
        compiler_params=pltpu.CompilerParams(vmem_limit_bytes=24 * MIB),
        name="gated_other" if other else "gated_own",
    )(ro, states, gate, gain)


def chunk_at(step, mine_ref, got_ref):
    place = lax.rem((lax.axis_index("exp") >> 1) + step, mine_ref.shape[0])
    return jnp.concatenate([mine_ref[place], got_ref[place]], axis=1)


def far_kernel(mine_ref, got_ref, w_ref, v_ref, a_ref, b_ref):
    rows = chunk_at(2, mine_ref, got_ref)
    deep, half = w_ref.shape[0], a_ref.shape[0]
    part = mxu(rows[:, :deep], w_ref[...]) + mxu(rows[:, deep:], v_ref[...])
    a_ref[...] = part[:half].astype(BF16)
    b_ref[...] = part[half:].astype(BF16)


def near_kernel(mine_ref, got_ref, w_ref, v_ref, right_ref, left_ref, held_ref):
    half = right_ref.shape[0]
    deep = w_ref.shape[0]
    rows = jnp.concatenate(
        [chunk_at(1, mine_ref, got_ref), chunk_at(mine_ref.shape[0] - 1, mine_ref, got_ref)], axis=0
    )
    part = mxu(rows[:, :deep], w_ref[...]) + mxu(rows[:, deep:], v_ref[...])
    held_ref[:half] = part[:half]
    right_ref[...] = part[half : 2 * half].astype(BF16)
    left_ref[...] = part[2 * half : 3 * half].astype(BF16)
    held_ref[half:] = part[3 * half :]


def own_kernel(mine_ref, got_ref, w_ref, v_ref, out_ref):
    rows = chunk_at(0, mine_ref, got_ref)
    deep = w_ref.shape[0]
    out_ref[...] = mxu(rows[:, :deep], w_ref[...]) + mxu(rows[:, deep:], v_ref[...])


def project(kernel, chunks, out_shape, name, mine, got, weight, other):
    count, toks, deep = mine.shape
    width = weight.shape[1]
    whole = pl.BlockSpec(memory_space=VMEM)
    return pl.pallas_call(
        kernel,
        in_specs=[whole] * 4,
        out_specs=[whole] * len(out_shape),
        out_shape=out_shape,
        cost_estimate=pl.CostEstimate(
            flops=4 * chunks * toks * deep * width,
            bytes_accessed=4 * weight.size + 4 * chunks * toks * width,
            transcendentals=0,
        ),
        compiler_params=pltpu.CompilerParams(vmem_limit_bytes=24 * MIB),
        name=name,
    )(mine, got, weight, other)


def relay_kernel(held_ref, a_ref, b_ref, right_ref, left_ref):
    half = a_ref.shape[0]
    right_ref[...] = (held_ref[:half] + a_ref[...].astype(F32)).astype(BF16)
    left_ref[...] = (held_ref[half:] + b_ref[...].astype(F32)).astype(BF16)


def relay(held, first, second):
    shape = jax.ShapeDtypeStruct(first.shape, BF16)
    return pl.pallas_call(
        relay_kernel,
        out_shape=[shape, shape],
        compiler_params=pltpu.CompilerParams(vmem_limit_bytes=16 * MIB),
        name="relay",
    )(held, first, second)


def slot_kernel(experts, ids_ref, out_ref):
    top, toks = ids_ref.shape
    expert = lax.broadcasted_iota(jnp.int32, (experts, toks), 0)
    hits = jnp.zeros((experts, toks), F32)
    for k in range(top):
        hits = hits + (expert == ids_ref[k : k + 1, :]).astype(F32)
    before = (
        lax.broadcasted_iota(jnp.int32, (toks, toks), 0) < lax.broadcasted_iota(jnp.int32, (toks, toks), 1)
    ).astype(BF16)
    earlier = mxu(hits.astype(BF16), before)
    for k in range(top):
        ids = ids_ref[k : k + 1, :]
        rank = jnp.sum(jnp.where(expert == ids, earlier, 0.0), axis=0, keepdims=True)
        out_ref[k : k + 1, :] = ids * CAP + rank.astype(jnp.int32)


def slots_of(ids, experts):
    return pl.pallas_call(
        functools.partial(slot_kernel, experts),
        out_shape=jax.ShapeDtypeStruct(ids.shape, jnp.int32),
        compiler_params=pltpu.CompilerParams(vmem_limit_bytes=16 * MIB),
        name="slots",
    )(ids)


def dispatch_kernel(own_ref, a0_ref, a1_ref, b0_ref, b1_ref, res_ref, gain_ref, slot_ref, att_ref, send_ref, flat_ref):
    toks, width = res_ref.shape
    pieces = width // 128
    own = own_ref[...]
    early = own[: toks // 2] + a0_ref[...].astype(F32) + a1_ref[...].astype(F32)
    late = own[toks // 2 :] + b0_ref[...].astype(F32) + b1_ref[...].astype(F32)
    total = jnp.concatenate([early, late], axis=0)
    attended = (res_ref[...].astype(F32) + total).astype(BF16)
    att_ref[...] = attended
    settled = attended.astype(F32)
    scale = 1.0 / jnp.sqrt(jnp.mean(settled * settled, axis=1, keepdims=True) + 1e-06)
    normed = settled * scale * gain_ref[...]
    for j in range(pieces):
        flat_ref[pl.ds(j, toks, stride=PITCH), :] = normed[:, j * 128 : (j + 1) * 128]

    @pl.loop(0, toks, unroll=4)
    def _(t):
        tile = flat_ref[pl.ds(pl.multiple_of(t * PITCH, 8), pieces), :].astype(BF16)
        for k in range(slot_ref.shape[0]):
            send_ref[slot_ref[k, t]] = tile


def dispatch(own, early, late, residual, gain, slots, count):
    toks, width = residual.shape
    pieces = width // 128
    whole = pl.BlockSpec(memory_space=VMEM)
    return pl.pallas_call(
        dispatch_kernel,
        in_specs=[whole] * 7 + [pl.BlockSpec(memory_space=pltpu.SMEM)],
        out_specs=[whole, whole],
        out_shape=[
            jax.ShapeDtypeStruct((toks, width), BF16),
            jax.ShapeDtypeStruct((count, pieces, 128), BF16),
        ],
        scratch_shapes=[VMEM((toks * PITCH, 128), F32)],
        compiler_params=pltpu.CompilerParams(vmem_limit_bytes=24 * MIB),
        name="dispatch",
    )(own, *early, *late, residual, gain, slots)


def expert_kernel(x_ref, wg_ref, wu_ref, wd_ref, out_ref, flat_ref):
    sources, _, tall, lanes = x_ref.shape
    pieces = wg_ref.shape[1] // lanes
    rows = flat_ref.shape[0] // PITCH
    tiles_ref = flat_ref.reshape(rows, PITCH, lanes)
    tiles_ref[:, :pieces, :] = x_ref[...].reshape(rows, pieces, lanes).astype(F32)
    x = jnp.concatenate(
        [flat_ref[pl.ds(j, rows, stride=PITCH), :].astype(BF16) for j in range(pieces)], axis=1
    )
    e = pl.program_id(0)
    gate = mxu(x, wg_ref[e])
    up = mxu(x, wu_ref[e])
    inner = (gate * lax.logistic(gate) * up).astype(BF16)
    y = mxu(inner, wd_ref[e])
    for j in range(pieces):
        flat_ref[pl.ds(j, rows, stride=PITCH), :] = y[:, j * lanes : (j + 1) * lanes]
    out_ref[...] = tiles_ref[:, :pieces, :].astype(BF16).reshape(sources, 1, tall, lanes)


def run_experts(x, gate_proj, up_proj, down_proj):
    count, local, tall, lanes = x.shape
    sources = 64
    rows = sources * tall * lanes // gate_proj.shape[1]
    tokens = pl.BlockSpec((sources, 1, tall, lanes), lambda e, i: (i, e, 0, 0))
    return pl.pallas_call(
        expert_kernel,
        grid=(local, count // sources),
        in_specs=[
            tokens,
            pl.BlockSpec(memory_space=VMEM),
            pl.BlockSpec(memory_space=VMEM),
            pl.BlockSpec(memory_space=VMEM),
        ],
        out_specs=tokens,
        out_shape=jax.ShapeDtypeStruct(x.shape, BF16),
        scratch_shapes=[VMEM((rows * PITCH, lanes), F32)],
        compiler_params=pltpu.CompilerParams(
            dimension_semantics=("arbitrary", "arbitrary"), vmem_limit_bytes=36 * MIB
        ),
        name="experts",
    )(x, gate_proj, up_proj, down_proj)


def combine_kernel(back_ref, slot_ref, gate_ref, out_ref, flat_ref):
    toks, width = out_ref.shape
    pieces = width // 128

    @pl.loop(0, toks, unroll=16)
    def _(t):
        total = jnp.zeros((pieces, 128), F32)
        for k in range(slot_ref.shape[0]):
            total = total + gate_ref[k, t] * back_ref[slot_ref[k, t]].astype(F32)
        flat_ref[pl.ds(pl.multiple_of(t * PITCH, 8), pieces), :] = total

    for j in range(pieces):
        out_ref[:, j * 128 : (j + 1) * 128] = flat_ref[pl.ds(j, toks, stride=PITCH), :].astype(BF16)


def combine(back, slots, gates):
    count, pieces, lanes = back.shape
    toks = slots.shape[1]
    smem = pl.BlockSpec(memory_space=pltpu.SMEM)
    return pl.pallas_call(
        combine_kernel,
        in_specs=[pl.BlockSpec(memory_space=VMEM), smem, smem],
        out_specs=pl.BlockSpec(memory_space=VMEM),
        out_shape=jax.ShapeDtypeStruct((toks, pieces * lanes), BF16),
        scratch_shapes=[VMEM((toks * PITCH, lanes), F32)],
        compiler_params=pltpu.CompilerParams(vmem_limit_bytes=24 * MIB),
        name="combine",
    )(back, slots, gates)


def shards(
    queries,
    key_vectors,
    values,
    out_gate,
    write_strength,
    decay_logarithm,
    residual,
    out_weight,
    head_gain,
    post_gain,
    gate_proj,
    up_proj,
    down_proj,
    expert_ids,
    route_gates,
):
    seq, heads, dv = values.shape
    dk = queries.shape[2]
    n_ctx = lax.axis_size("ctx")
    n_exp = lax.axis_size("exp")
    n_dev = n_ctx * n_exp
    parts = n_ctx // heads
    wide = dv // parts
    local_experts = gate_proj.shape[0]
    toks, width = residual.shape

    shift = lambda a, by: lax.ppermute(a, "exp", [(i, (i + 2 * by) % n_exp) for i in range(n_exp)])
    swap = lambda a: lax.ppermute(a, "exp", [(i, i ^ 1) for i in range(n_exp)])
    other_weight = swap(out_weight)
    slots = slots_of(expert_ids.T, local_experts * n_dev)
    gates = route_gates.T

    by_head = lambda a: jnp.transpose(a, (1, 0, 2))
    local_out, msg = local_delta(
        decay_logarithm, write_strength, by_head(queries), by_head(key_vectors), by_head(values), parts
    )
    msg = lax.all_to_all(msg.reshape(n_ctx, dk + wide, dk), "ctx", 0, 0, tiled=True)
    states = lax.all_to_all(prefix_states(msg, wide), "ctx", 0, 0, tiled=True).reshape(heads, dv, dk)
    gating = (local_out, states, by_head(out_gate), head_gain.reshape(1, dv), toks)
    got = swap(gated_rows(1, *gating))
    mine = gated_rows(0, *gating)
    half = jax.ShapeDtypeStruct((toks // 2, width), BF16)
    operands = (mine, got, out_weight, other_weight)
    first, second = project(far_kernel, 1, [half, half], "project_far", *operands)
    first, second = shift(first, 1), shift(second, -1)
    total = jax.ShapeDtypeStruct((toks, width), F32)
    ahead, behind, held = project(near_kernel, 2, [half, half, total], "project_near", *operands)
    ahead, behind = shift(ahead, 1), shift(behind, -1)
    right, left = relay(held, first, second)
    [own] = project(own_kernel, 1, [total], "project_own", *operands)
    attended, send = dispatch(
        own,
        (shift(right, 1), behind),
        (ahead, shift(left, -1)),
        residual,
        post_gain.reshape(1, width),
        slots,
        n_dev * local_experts * CAP,
    )
    tall = CAP * width // 128
    held = lax.all_to_all(
        send.reshape(n_dev, local_experts, tall, 128), ("ctx", "exp"), 0, 0, tiled=True
    )
    done = run_experts(held, gate_proj, up_proj, down_proj)
    back = lax.all_to_all(done, ("ctx", "exp"), 0, 0, tiled=True)
    mixture = combine(back.reshape(n_dev * local_experts * CAP, width // 128, 128), slots, gates)
    return (attended, mixture)


def solution(mesh):
    in_specs = (
        P("ctx", "exp", None),
        P("ctx", "exp", None),
        P("ctx", "exp", None),
        P("ctx", "exp", None),
        P("exp", "ctx"),
        P("exp", "ctx"),
        P(("ctx", "exp"), None),
        P("exp", None),
        P(),
        P(),
        P(("ctx", "exp"), None, None),
        P(("ctx", "exp"), None, None),
        P(("ctx", "exp"), None, None),
        P(("ctx", "exp"), None),
        P(("ctx", "exp"), None),
    )
    out_specs = (P(("ctx", "exp"), None), P(("ctx", "exp"), None))
    return jax.shard_map(shards, mesh=mesh, in_specs=in_specs, out_specs=out_specs, check_vma=False)
```
